256 devices in a mesh: dp: 32 (over z, y_lo, core), space: 8 (over x, y_hi).
Axes of the slice: x: 4, y: 4 (y_hi: 2, y_lo: 2; y = y_hi * 2 + y_lo), z: 8, core: 2. Of those that a mesh axis runs over, the one named last changes fastest.
Arguments:
- occupancy: int32 [32, 5, 128, 128], P('dp', None, 'space'), may hold values from 0 to 8191
- state_labels: int32 [32, 8, 8], P('dp', 'space'), may hold values 0 or 1
- lift_weight: bfloat16 [13, 32], replicated, may hold values from -1.75 to 1.75
- temporal_weight: bfloat16 [3, 3, 5, 32, 64], replicated, may hold values from -0.21875 to 0.21875
- middle_weight: bfloat16 [3, 3, 64, 128], replicated, may hold values from -0.375 to 0.375
- deeper_weight: bfloat16 [3, 3, 128, 256], replicated, may hold values from -0.25 to 0.25
- deepest_weight: bfloat16 [3, 3, 256, 512], replicated, may hold values from -0.1875 to 0.1875
- head_weight: bfloat16 [512], replicated, may hold values from -0.25 to 0.25
Outputs:
- temporal_grad: float32 [3, 3, 5, 32, 64], replicated
- middle_grad: float32 [3, 3, 64, 128], replicated
- deeper_grad: float32 [3, 3, 128, 256], replicated
- deepest_grad: float32 [3, 3, 256, 512], replicated
- head_grad: float32 [512], replicated
The draws below stay inside these ranges and needn't reach their ends.
All inputs are finite; a program needn't handle non-finite values. No bound on the sum of `state_labels` on one device may be relied on, other than what follows from the above.
Results may differ from the reference program's by a relative error of at most 0.015.
Values may be sent and summed in bfloat16 or wider, within the bound.
A program may use at most 64 MiB of HBM per device.

```python
import jax
import jax.numpy as jnp
from jax import lax

HEIGHTS = 13
CH_LIFT = 32
CH_ONE = 64
CH_TWO = 128
CH_THREE = 256
CH_FOUR = 512
FRAMES = 5
COLS = 128
BATCH = 32
HEIGHT_CELLS = 128


def plant(drawn, rng, least, largest):
    index_at = [jax.random.randint(jax.random.fold_in(rng, axis), (), 0, length) for axis, length in enumerate(drawn.shape)]
    longest = drawn.shape.index(max(drawn.shape))
    neighbour = index_at[:longest] + [(index_at[longest] + 1) % drawn.shape[longest]] + index_at[longest + 1:]
    return drawn.at[tuple(index_at)].set(least).at[tuple(neighbour)].set(largest)


def bell_draw(stream_key, extent, spread, bound, held_as=jnp.bfloat16):
    array = spread * jax.random.normal(stream_key, extent, jnp.float32)
    return jnp.clip(array, min=-bound, max=bound).astype(held_as)


def setup_inputs(seed: int = 0) -> dict:
    key_list = jax.random.split(jax.random.key(seed), 9)
    occupancy = plant(jax.random.randint(key_list[0], (BATCH, FRAMES, HEIGHT_CELLS, COLS), 0, 2 ** HEIGHTS), jax.random.fold_in(key_list[0], 1), 0, (2 ** HEIGHTS) - 1).astype(jnp.int32)
    state_labels = plant((jax.random.randint(key_list[1], (BATCH, HEIGHT_CELLS // 16, COLS // 16), 0, 2) < 1).astype(jnp.int32), jax.random.fold_in(key_list[1], 1), 0, 1)
    lift_weight = bell_draw(key_list[2], (HEIGHTS, CH_LIFT), HEIGHTS ** -0.5, 1.75)
    temporal_weight = bell_draw(key_list[3], (3, 3, FRAMES, CH_LIFT, CH_ONE), (9 * FRAMES * CH_LIFT // 2) ** -0.5, 0.21875)
    middle_weight = bell_draw(key_list[4], (3, 3, CH_ONE, CH_TWO), (9 * CH_ONE // 2) ** -0.5, 0.375)
    deeper_weight = bell_draw(key_list[5], (3, 3, CH_TWO, CH_THREE), (9 * CH_TWO // 2) ** -0.5, 0.25)
    deepest_weight = bell_draw(key_list[6], (3, 3, CH_THREE, CH_FOUR), (9 * CH_THREE // 2) ** -0.5, 0.1875)
    head_weight = bell_draw(key_list[7], (CH_FOUR,), CH_FOUR ** -0.5, 0.25)
    return {"occupancy": occupancy, "state_labels": state_labels, "lift_weight": lift_weight, "temporal_weight": temporal_weight, "middle_weight": middle_weight, "deeper_weight": deeper_weight, "deepest_weight": deepest_weight, "head_weight": head_weight}


def tap_view(padded, row_tap, col_tap, out_rows, out_cols):
    leading = padded.shape[:-2]
    anchor = (0,) * len(leading) + (row_tap, col_tap)
    bounds = tuple(leading) + (row_tap + 2 * out_rows - 1, col_tap + 2 * out_cols - 1)
    strides = (1,) * len(leading) + (2, 2)
    return lax.slice(padded, anchor, bounds, strides)

def pad_field(feature_map):
    return jnp.pad(feature_map, ((0, 0), (1, 0), (1, 0)))

def conv_layer(feature_map, weight):
    padded = pad_field(feature_map)
    out_rows = feature_map.shape[1] // 2
    out_cols = feature_map.shape[2] // 2
    accumulated = jnp.zeros((weight.shape[3], out_rows, out_cols), jnp.float32)
    for row_tap in range(3):
        for col_tap in range(3):
            cells = tap_view(padded, row_tap, col_tap, out_rows, out_cols).astype(jnp.float32)
            accumulated = accumulated + jnp.einsum('crw,co->orw', cells, weight[row_tap, col_tap].astype(jnp.float32))
    gate = jax.nn.sigmoid(accumulated)
    slope = gate * (1.0 + accumulated * (1.0 - gate))
    return ((accumulated * gate).astype(jnp.bfloat16), slope, padded)

def weight_grad(padded, delta):
    out_rows = delta.shape[1]
    out_cols = delta.shape[2]
    rows_list = []
    for row_tap in range(3):
        cols_list = []
        for col_tap in range(3):
            cells = tap_view(padded, row_tap, col_tap, out_rows, out_cols).astype(jnp.float32)
            cols_list.append(jnp.einsum('crw,orw->co', cells, delta.astype(jnp.float32)))
        rows_list.append(jnp.stack(cols_list))
    return jnp.stack(rows_list)

def input_grad(delta, weight):
    out_rows = delta.shape[1]
    out_cols = delta.shape[2]
    accumulated = jnp.zeros((weight.shape[2], 2 * out_rows + 1, 2 * out_cols + 1), jnp.float32)
    for row_tap in range(3):
        for col_tap in range(3):
            contribution = jnp.einsum('orw,co->crw', delta.astype(jnp.float32), weight[row_tap, col_tap].astype(jnp.float32))
            zero_value = jnp.zeros((), contribution.dtype)
            accumulated = accumulated + lax.pad(contribution, zero_value, ((0, 0, 0), (row_tap, 2 - row_tap, 1), (col_tap, 2 - col_tap, 1)))
    return accumulated[:, 1:, 1:]

def sample_grads(occupancy_sample, labels, lift_weight, temporal_weight, middle_weight, deeper_weight, deepest_weight, head_weight):
    shifts = jnp.arange(HEIGHTS, dtype=jnp.int32)
    height_bits = jnp.bitwise_and(jnp.right_shift(occupancy_sample[:, None], shifts[None, :, None, None]), 1).astype(jnp.float32)
    lifted = jnp.einsum('tcrw,ck->tkrw', height_bits, lift_weight.astype(jnp.float32))
    lifted = jnp.maximum(lifted, 0.0).astype(jnp.bfloat16)
    lifted = lifted.reshape(FRAMES * CH_LIFT, lifted.shape[2], lifted.shape[3])
    first_kernel = temporal_weight.reshape(3, 3, FRAMES * CH_LIFT, CH_ONE)
    first_map, first_slope, lifted_padded = conv_layer(lifted, first_kernel)
    second_map, second_slope, first_padded = conv_layer(first_map, middle_weight)
    third_map, third_slope, second_padded = conv_layer(second_map, deeper_weight)
    fourth_map, fourth_slope, third_padded = conv_layer(third_map, deepest_weight)
    head_float = head_weight.astype(jnp.float32)
    fourth_float = fourth_map.astype(jnp.float32)
    logits = jnp.einsum('orw,o->rw', fourth_float, head_float)
    logit_grad = (jax.nn.sigmoid(logits) - labels.astype(jnp.float32)) / BATCH
    head_grad = jnp.einsum('orw,rw->o', fourth_float, logit_grad)
    fourth_delta = (logit_grad[None] * head_float[:, None, None] * fourth_slope).astype(jnp.bfloat16)
    deepest_grad = weight_grad(third_padded, fourth_delta)
    third_delta = (input_grad(fourth_delta, deepest_weight) * third_slope).astype(jnp.bfloat16)
    deeper_grad = weight_grad(second_padded, third_delta)
    second_delta = (input_grad(third_delta, deeper_weight) * second_slope).astype(jnp.bfloat16)
    middle_grad = weight_grad(first_padded, second_delta)
    first_delta = (input_grad(second_delta, middle_weight) * first_slope).astype(jnp.bfloat16)
    temporal_grad = weight_grad(lifted_padded, first_delta).reshape(3, 3, FRAMES, CH_LIFT, CH_ONE)
    return (temporal_grad, middle_grad, deeper_grad, deepest_grad, head_grad)

def reference(occupancy, state_labels, lift_weight, temporal_weight, middle_weight, deeper_weight, deepest_weight, head_weight):
    initial = (jnp.zeros(temporal_weight.shape, jnp.float32), jnp.zeros(middle_weight.shape, jnp.float32), jnp.zeros(deeper_weight.shape, jnp.float32), jnp.zeros(deepest_weight.shape, jnp.float32), jnp.zeros(head_weight.shape, jnp.float32))

    def accumulate(running, sample):
        gradients = sample_grads(sample[0], sample[1], lift_weight, temporal_weight, middle_weight, deeper_weight, deepest_weight, head_weight)
        return (jax.tree.map(lambda left, right: left + right, running, gradients), None)
    summed, _ = lax.scan(accumulate, initial, (occupancy, state_labels))
    return (summed[0], summed[1], summed[2], summed[3], summed[4])
```

```python
import functools

import jax
import jax.numpy as jnp
from jax import lax
from jax.experimental import pallas as pl
from jax.experimental.pallas import tpu as pltpu
from jax.sharding import PartitionSpec as P

BF = jnp.bfloat16
F32 = jnp.float32
MESH = pl.DeviceIdType.MESH

NX, NY, NZ = 4, 4, 8
SIZE = {"x": NX, "y": NY, "z": NZ}
DEEPEST_AT, DEEPER_AT, TEMPORAL_AT, HEAD_AT, MIDDLE_AT = 0, 576, 720, 765, 768
PARTS = ((("x", "y", "z"), 12), (("y", "z", "x"), 4), (("z", "x", "y"), 3))
LENGTHS = tuple(SIZE[order[0]] * SIZE[order[1]] * kept for order, kept in PARTS)
STARTS = tuple(sum(LENGTHS[:i]) for i in range(len(PARTS)))
HALF = sum(LENGTHS)
TILES = 2 * HALF


def vmem():
    return pl.BlockSpec(memory_space=pltpu.VMEM)


def halo_kernel(occ_ref, window_ref, landed, send_sem, recv_sem):
    space = lax.axis_index("space")
    below = lax.rem(space + 1, 8)
    above = lax.rem(space + 7, 8)
    barrier = pltpu.get_barrier_semaphore()
    for peer in (below, above):
        pl.semaphore_signal(barrier, inc=1, device_id={"space": peer}, device_id_type=MESH)
    pl.semaphore_wait(barrier, 2)
    copy = pltpu.make_async_remote_copy(
        src_ref=occ_ref,
        dst_ref=landed,
        send_sem=send_sem,
        recv_sem=recv_sem,
        device_id={"space": below},
        device_id_type=MESH,
    )
    copy.start()
    window_ref[:, 16:32, :] = occ_ref[...]
    copy.wait()
    keep = jnp.where(space == 0, 0, 1)
    window_ref[:, 0:16, :] = landed[...] * keep


def halo(occ):
    return pl.pallas_call(
        halo_kernel,
        out_shape=jax.ShapeDtypeStruct((5, 32, 128), jnp.int32),
        in_specs=[vmem()],
        out_specs=vmem(),
        scratch_shapes=[
            pltpu.VMEM((5, 16, 128), jnp.int32),
            pltpu.SemaphoreType.DMA(()),
            pltpu.SemaphoreType.DMA(()),
        ],
        compiler_params=pltpu.CompilerParams(collective_id=0, has_side_effects=True),
    )(occ)


def dot(a, b):
    return lax.dot_general(a, b, (((1,), (0,)), ((), ())), preferred_element_type=F32)


def dot_nt(a, b):
    return lax.dot_general(a, b, (((1,), (1,)), ((), ())), preferred_element_type=F32)


def dot_tn(a, b):
    return lax.dot_general(a, b, (((0,), (0,)), ((), ())), preferred_element_type=F32)


def activate(pre):
    gate = jax.nn.sigmoid(pre)
    slope = gate * (1.0 + pre * (1.0 - gate))
    return pre * gate, slope


def later(block):
    rolled = pltpu.roll(block, 1, block.ndim - 2)
    index = lax.broadcasted_iota(jnp.int32, block.shape, block.ndim - 2)
    return jnp.where(index == 0, 0.0, rolled)


def sooner(block):
    size = block.shape[-2]
    rolled = pltpu.roll(block, size - 1, block.ndim - 2)
    index = lax.broadcasted_iota(jnp.int32, block.shape, block.ndim - 2)
    return jnp.where(index == size - 1, 0.0, rolled)


def tap_of(ref, p, q, rows, phases):
    a, b = p // 2, p % 2
    c, d = q // 2, q % 2
    block = ref[a : a + rows, b, c : c + phases, d]
    return block.reshape(rows * phases * block.shape[2], block.shape[3])


def store_map(ref, value, rows, phases):
    shifted = later(value[:, phases - 1])
    for r in range(rows):
        ref[r // 2, r % 2, 0, 0] = shifted[r].astype(BF)
        for m in range(phases):
            s = m + 1
            ref[r // 2, r % 2, s // 2, s % 2] = value[r, m].astype(BF)


def map_grad(delta, weight_ref, rows, phases):
    out = {}

    def put(r, m, value):
        out[(r, m)] = value if (r, m) not in out else out[(r, m)] + value

    for p in range(3):
        for q in range(3):
            part = dot_nt(delta, weight_ref[3 * p + q])
            part = part.reshape(rows, phases, 16, part.shape[1])
            for m in range(phases):
                s = 2 * m + q - 1
                for o in range(rows):
                    value = part[o, m]
                    if s < 0:
                        put(2 * o + p, 2 * phases - 1, sooner(value))
                    else:
                        put(2 * o + p, s, value)
    return out


def every_second(ref, r, start):
    halves = [ref[r, h, pl.ds(start, 16, stride=2), :] for h in range(2)]
    return jnp.concatenate(halves, axis=1)


def compute_kernel(
    window_ref,
    labels_ref,
    lift_ref,
    w1_ref,
    w2_ref,
    w3_ref,
    w4_ref,
    head_ref,
    grads_ref,
    lifted,
    first,
    first_slope,
    second,
    second_slope,
    third,
    third_slope,
    third_dx,
    first_delta,
):
    to = lax.broadcasted_iota(jnp.int32, (128, 128), 0)
    come = lax.broadcasted_iota(jnp.int32, (128, 128), 1)
    order = jnp.where(come == lax.rem(to, 16) * 8 + to // 16, 1.0, 0.0).astype(BF)
    shifts = lax.broadcasted_iota(jnp.int32, (16, 128), 0)
    lift = lift_ref[...]
    for r in range(31):
        frames = []
        for t in range(5):
            row = jnp.broadcast_to(window_ref[t, r + 1 : r + 2, :], (16, 128))
            bits = jnp.bitwise_and(jnp.right_shift(row, shifts), 1)
            frames.append(bits.astype(F32).astype(BF))
        turned = dot_nt(order, jnp.concatenate(frames, axis=0)).astype(BF)
        value = jnp.maximum(dot(turned, lift), 0.0).reshape(8, 16, 160)
        lifted[r // 2, r % 2, 0, 0] = later(value[7]).astype(BF)
        for m in range(8):
            s = m + 1
            lifted[r // 2, r % 2, s // 2, s % 2] = value[m].astype(BF)
    zero_row = jnp.zeros((5, 2, 16, 160), BF)
    lifted[15, 1] = zero_row
    lifted[16, 0] = zero_row
    lifted[16, 1] = zero_row

    pre = jnp.zeros((960, 64), F32)
    for p in range(3):
        for q in range(3):
            pre = pre + dot(tap_of(lifted, p, q, 15, 4), w1_ref[3 * p + q])
    value, slope = activate(pre)
    store_map(first, value.reshape(15, 4, 16, 64), 15, 4)
    first_slope[...] = slope.reshape(15, 4, 16, 64)

    pre = jnp.zeros((224, 128), F32)
    for p in range(3):
        for q in range(3):
            pre = pre + dot(tap_of(first, p, q, 7, 2), w2_ref[3 * p + q])
    value, slope = activate(pre)
    store_map(second, value.reshape(7, 2, 16, 128), 7, 2)
    second_slope[...] = slope.reshape(7, 2, 16, 128)

    pre = jnp.zeros((48, 256), F32)
    for p in range(3):
        for q in range(3):
            pre = pre + dot(tap_of(second, p, q, 3, 1), w3_ref[3 * p + q])
    value, slope = activate(pre)
    third[...] = jnp.zeros((3, 2, 32, 128), F32)
    for r in range(3):
        for h in range(2):
            third[r, h, 0:16, :] = value[16 * r : 16 * r + 16, 128 * h : 128 * h + 128]
    third_slope[...] = slope.reshape(3, 16, 256)

    place = lax.broadcasted_iota(jnp.int32, (16, 256), 0)
    cells = []
    pre = jnp.zeros((16, 512), F32)
    for p in range(3):
        even = every_second(third, p, 0)
        odd = every_second(third, p, 1)
        left = jnp.where((place > 0) & (place < 8), pltpu.roll(odd, 1, 0), 0.0)
        for q, block in enumerate((left, even, odd)):
            block = block.astype(BF)
            cells.append(block)
            pre = pre + dot(block, w4_ref[3 * p + q])
    value, slope = activate(pre)
    fourth = value.astype(BF).astype(F32)
    head = head_ref[...].astype(F32)
    logits = jnp.sum(fourth * head, axis=1, keepdims=True)
    logit_grad = (jax.nn.sigmoid(logits) - labels_ref[...].astype(F32)) / 32.0
    logit_grad = jnp.where(lax.broadcasted_iota(jnp.int32, (16, 1), 0) < 8, logit_grad, 0.0)
    head_grad = jnp.sum(fourth * logit_grad, axis=0, keepdims=True)
    grads_ref[HEAD_AT : HEAD_AT + 3] = jnp.zeros((3, 16, 128), BF)
    for lane in range(4):
        part = head_grad[:, 128 * lane : 128 * lane + 128]
        grads_ref[HEAD_AT, :, :] = jnp.where(
            lax.broadcasted_iota(jnp.int32, (16, 128), 0) == lane,
            jnp.broadcast_to(part, (16, 128)),
            grads_ref[HEAD_AT].astype(F32),
        ).astype(BF)
    grads_ref[804:TILES] = jnp.zeros((TILES - 804, 16, 128), BF)
    delta = (logit_grad * head * slope).astype(BF)

    for p in range(3):
        parts = []
        for q in range(3):
            t = 3 * p + q
            grad = dot_tn(cells[t], delta).astype(BF)
            for lane in range(4):
                grads_ref[64 * t + 16 * lane : 64 * t + 16 * lane + 16] = grad[
                    :, 128 * lane : 128 * lane + 128
                ].reshape(16, 16, 128)
            parts.append(dot_nt(delta, w4_ref[t]))
        odd = parts[2] + pltpu.roll(parts[0], 15, 0)
        for h in range(2):
            lanes = slice(128 * h, 128 * h + 128)
            third_dx[p, h, pl.ds(0, 16, stride=2), :] = parts[1][:, lanes]
            third_dx[p, h, pl.ds(1, 16, stride=2), :] = odd[:, lanes]
    delta = jnp.concatenate(
        [
            jnp.concatenate([third_dx[r, h, 0:16, :] for h in range(2)], axis=1) * third_slope[r]
            for r in range(3)
        ],
        axis=0,
    ).astype(BF)

    for t in range(9):
        grad = dot_tn(tap_of(second, t // 3, t % 3, 3, 1), delta).astype(BF)
        for lane in range(2):
            at = DEEPER_AT + 16 * t + 8 * lane
            grads_ref[at : at + 8] = grad[:, 128 * lane : 128 * lane + 128].reshape(8, 16, 128)
    dx = map_grad(delta, w3_ref, 3, 1)
    delta = jnp.concatenate(
        [dx[(r, m)] * second_slope[r, m] for r in range(7) for m in range(2)], axis=0
    ).astype(BF)

    for t in range(9):
        grad = dot_tn(tap_of(first, t // 3, t % 3, 7, 2), delta).astype(BF)
        at = MIDDLE_AT + 4 * t
        grads_ref[at : at + 4] = grad.reshape(4, 16, 128)
    dx = map_grad(delta, w2_ref, 7, 2)
    for r in range(15):
        for m in range(4):
            at = 64 * r + 16 * m
            first_delta[at : at + 16, :] = dx[(r, m)] * first_slope[r, m]
    first_delta[960:1024, :] = jnp.zeros((64, 64), F32)

    turned = jnp.transpose(first_delta[...]).astype(BF)
    for t in range(9):
        grad = dot(turned, tap_of(lifted, t // 3, t % 3, 16, 4))
        grad = jnp.transpose(grad)
        grad = jnp.concatenate([grad[0:80], grad[80:160]], axis=1).astype(BF)
        at = TEMPORAL_AT + 5 * t
        grads_ref[at : at + 5] = grad.reshape(5, 16, 128)


def compute(window, labels, lift, w1, w2, w3, w4, head):
    return pl.pallas_call(
        compute_kernel,
        out_shape=jax.ShapeDtypeStruct((TILES, 16, 128), BF),
        in_specs=[vmem()] * 8,
        out_specs=vmem(),
        scratch_shapes=[
            pltpu.VMEM((17, 2, 5, 2, 16, 160), BF),
            pltpu.VMEM((8, 2, 3, 2, 16, 64), BF),
            pltpu.VMEM((15, 4, 16, 64), F32),
            pltpu.VMEM((4, 2, 2, 2, 16, 128), BF),
            pltpu.VMEM((7, 2, 16, 128), F32),
            pltpu.VMEM((3, 2, 32, 128), F32),
            pltpu.VMEM((3, 16, 256), F32),
            pltpu.VMEM((3, 2, 32, 128), F32),
            pltpu.VMEM((1024, 64), F32),
        ],
        compiler_params=pltpu.CompilerParams(vmem_limit_bytes=48 * 1024 * 1024),
    )(window, labels, lift, w1, w2, w3, w4, head)


def position():
    dp = lax.axis_index("dp")
    space = lax.axis_index("space")
    return {
        "x": space // 2,
        "y": lax.rem(space, 2) * 2 + lax.rem(dp // 2, 2),
        "z": dp // 4,
        "core": lax.rem(dp, 2),
    }


def device_at(place):
    dp = place["z"] * 4 + lax.rem(place["y"], 2) * 2 + place["core"]
    space = place["x"] * 2 + place["y"] // 2
    return (dp, space)


def along(here, axis, distance):
    there = dict(here)
    there[axis] = lax.rem(here[axis] + distance, SIZE[axis])
    return there


def reduce_kernel(grads_ref, total_ref, *scratch):
    paired, *rest = scratch
    shared = rest[0:3]
    landed1, sum1 = rest[3:6], rest[6:9]
    landed2, sum2 = rest[9:12], rest[12:15]
    landed3 = rest[15:18]
    send_sem, recv_sem = rest[18], rest[19]

    here = position()
    core = here["core"]
    partner = dict(here)
    partner["core"] = 1 - core

    barrier = pltpu.get_barrier_semaphore()
    peers = [device_at(partner)]
    for axis, size in SIZE.items():
        peers += [device_at(along(here, axis, d)) for d in range(1, size)]
    for peer in peers:
        pl.semaphore_signal(barrier, inc=1, device_id=peer, device_id_type=MESH)
    pl.semaphore_wait(barrier, len(peers))

    used = [0]

    def send(src, dst, place):
        index = used[0]
        used[0] += 1
        copy = pltpu.make_async_remote_copy(
            src_ref=src,
            dst_ref=dst,
            send_sem=send_sem.at[index],
            recv_sem=recv_sem.at[index],
            device_id=device_at(place),
            device_id_type=MESH,
        )
        copy.start()
        return copy

    pending = []

    def arrive(copies):
        for copy in copies:
            copy.wait_recv()
        pending.extend(copies)

    flights = []
    for i in range(3):
        at = pl.ds((1 - core) * HALF + STARTS[i], LENGTHS[i])
        flights.append(
            [send(grads_ref.at[at], paired.at[pl.ds(STARTS[i], LENGTHS[i])], partner)]
        )

    for i, (order, kept) in enumerate(PARTS):
        first, second = SIZE[order[0]], SIZE[order[1]]
        arrive(flights[i])
        at = pl.ds(core * HALF + STARTS[i], LENGTHS[i])
        both = grads_ref[at].astype(F32) + paired[STARTS[i] : STARTS[i] + LENGTHS[i]].astype(F32)
        shared[i][...] = both.astype(BF).reshape(first, second * kept, 16, 128)
        flights[i] = []
        for d in range(1, first):
            there = along(here, order[0], d)
            flights[i].append(
                send(shared[i].at[there[order[0]]], landed1[i].at[d - 1], there)
            )

    for i, (order, kept) in enumerate(PARTS):
        first, second = SIZE[order[0]], SIZE[order[1]]
        arrive(flights[i])
        total = shared[i][here[order[0]]].astype(F32)
        for d in range(1, first):
            total = total + landed1[i][d - 1].astype(F32)
        sum1[i][...] = total.astype(BF).reshape(second, kept, 16, 128)
        flights[i] = []
        for d in range(1, second):
            there = along(here, order[1], d)
            flights[i].append(send(sum1[i].at[there[order[1]]], landed2[i].at[d - 1], there))

    for i, (order, kept) in enumerate(PARTS):
        second, third = SIZE[order[1]], SIZE[order[2]]
        arrive(flights[i])
        total = sum1[i][here[order[1]]].astype(F32)
        for d in range(1, second):
            total = total + landed2[i][d - 1].astype(F32)
        sum2[i][...] = total.astype(BF)
        flights[i] = []
        for d in range(1, third):
            there = along(here, order[2], d)
            flights[i].append(send(sum2[i], landed3[i].at[d - 1], there))

    for i, (order, kept) in enumerate(PARTS):
        second, third = SIZE[order[1]], SIZE[order[2]]
        mine = here[order[2]]
        arrive(flights[i])
        total = jnp.zeros((kept, 16, 128), F32)
        own = sum2[i][...].astype(F32)
        for k in range(third):
            back = lax.rem(mine - k + third, third)
            other = landed3[i][lax.rem(back + third - 1, third)].astype(F32)
            total = total + jnp.where(back == 0, own, other)
        at = core * HALF + STARTS[i] + here[order[0]] * (second * kept) + here[order[1]] * kept
        total_ref[pl.ds(at, kept)] = total.astype(BF)
        flights[i] = []
        for d in range(1, second):
            there = along(here, order[1], d)
            flights[i].append(
                send(total_ref.at[pl.ds(at, kept)], total_ref.at[pl.ds(at, kept)], there)
            )

    for i, (order, kept) in enumerate(PARTS):
        first, second = SIZE[order[0]], SIZE[order[1]]
        arrive(flights[i])
        at = core * HALF + STARTS[i] + here[order[0]] * (second * kept)
        flights[i] = []
        for d in range(1, first):
            there = along(here, order[0], d)
            flights[i].append(
                send(
                    total_ref.at[pl.ds(at, second * kept)],
                    total_ref.at[pl.ds(at, second * kept)],
                    there,
                )
            )

    for i in range(3):
        arrive(flights[i])
        at = pl.ds(core * HALF + STARTS[i], LENGTHS[i])
        flights[i] = [send(total_ref.at[at], total_ref.at[at], partner)]
    for i in range(3):
        arrive(flights[i])
    for copy in pending:
        copy.wait_send()


def all_reduce(grads):
    scratch = [pltpu.VMEM((HALF, 16, 128), BF)]
    dims = []
    for order, kept in PARTS:
        dims.append((SIZE[order[0]], SIZE[order[1]], SIZE[order[2]], kept))
    scratch += [pltpu.VMEM((a, b * k, 16, 128), BF) for a, b, c, k in dims]
    scratch += [pltpu.VMEM((a - 1, b * k, 16, 128), BF) for a, b, c, k in dims]
    scratch += [pltpu.VMEM((b, k, 16, 128), BF) for a, b, c, k in dims]
    scratch += [pltpu.VMEM((b - 1, k, 16, 128), BF) for a, b, c, k in dims]
    scratch += [pltpu.VMEM((k, 16, 128), BF) for a, b, c, k in dims]
    scratch += [pltpu.VMEM((c, k, 16, 128), BF) for a, b, c, k in dims]
    copies = 6 + sum(2 * (a - 1) + 2 * (b - 1) + (c - 1) for a, b, c, k in dims)
    scratch += [pltpu.SemaphoreType.DMA((copies,)), pltpu.SemaphoreType.DMA((copies,))]
    return pl.pallas_call(
        reduce_kernel,
        out_shape=jax.ShapeDtypeStruct((TILES, 16, 128), BF),
        in_specs=[vmem()],
        out_specs=vmem(),
        scratch_shapes=scratch,
        compiler_params=pltpu.CompilerParams(
            collective_id=1, has_side_effects=True, vmem_limit_bytes=48 * 1024 * 1024
        ),
    )(grads)


def unpack_kernel(d4, d3, d1, dh, d2, g1, g2, g3, g4, gh):
    for lane in range(4):
        g4[0, :, 128 * lane : 128 * lane + 128] = (
            d4[16 * lane : 16 * lane + 16].reshape(256, 128).astype(F32)
        )
    for lane in range(2):
        g3[0, :, 128 * lane : 128 * lane + 128] = (
            d3[8 * lane : 8 * lane + 8].reshape(128, 128).astype(F32)
        )
    g2[0] = d2[...].reshape(64, 128).astype(F32)
    block = d1[...].reshape(80, 128).astype(F32)
    g1[0, 0:80, :] = block[:, 0:64]
    g1[0, 80:160, :] = block[:, 64:128]
    gh[...] = dh[0, 0:8, :].astype(F32)


def unpack(total):
    return pl.pallas_call(
        unpack_kernel,
        grid=(9,),
        out_shape=[
            jax.ShapeDtypeStruct((9, 160, 64), F32),
            jax.ShapeDtypeStruct((9, 64, 128), F32),
            jax.ShapeDtypeStruct((9, 128, 256), F32),
            jax.ShapeDtypeStruct((9, 256, 512), F32),
            jax.ShapeDtypeStruct((8, 128), F32),
        ],
        in_specs=[
            pl.BlockSpec((64, 16, 128), lambda t: (t, 0, 0)),
            pl.BlockSpec((16, 16, 128), lambda t: (DEEPER_AT // 16 + t, 0, 0)),
            pl.BlockSpec((5, 16, 128), lambda t: (TEMPORAL_AT // 5 + t, 0, 0)),
            pl.BlockSpec((1, 16, 128), lambda t: (HEAD_AT, 0, 0)),
            pl.BlockSpec((4, 16, 128), lambda t: (MIDDLE_AT // 4 + t, 0, 0)),
        ],
        out_specs=[
            pl.BlockSpec((1, 160, 64), lambda t: (t, 0, 0)),
            pl.BlockSpec((1, 64, 128), lambda t: (t, 0, 0)),
            pl.BlockSpec((1, 128, 256), lambda t: (t, 0, 0)),
            pl.BlockSpec((1, 256, 512), lambda t: (t, 0, 0)),
            pl.BlockSpec((8, 128), lambda t: (0, 0)),
        ],
    )(total, total, total, total, total)


def local(
    occupancy,
    state_labels,
    lift_weight,
    temporal_weight,
    middle_weight,
    deeper_weight,
    deepest_weight,
    head_weight,
):
    window = halo(occupancy[0])
    labels = jnp.pad(state_labels.reshape(8, 1), ((0, 8), (0, 0)))
    padded = jnp.pad(lift_weight, ((0, 3), (0, 0)))
    spread = jnp.eye(5, dtype=BF)[:, None, :, None] * padded[None, :, None, :]
    grads = compute(
        window,
        labels,
        spread.reshape(80, 160),
        temporal_weight.reshape(9, 160, 64),
        middle_weight.reshape(9, 64, 128),
        deeper_weight.reshape(9, 128, 256),
        deepest_weight.reshape(9, 256, 512),
        head_weight.reshape(1, 512),
    )
    g1, g2, g3, g4, gh = unpack(all_reduce(grads))
    return (
        g1.reshape(3, 3, 5, 32, 64),
        g2.reshape(3, 3, 64, 128),
        g3.reshape(3, 3, 128, 256),
        g4.reshape(3, 3, 256, 512),
        gh[0:4].reshape(512),
    )


def solution(mesh):
    return jax.shard_map(
        local,
        mesh=mesh,
        in_specs=(
            P("dp", None, "space", None),
            P("dp", "space", None),
            P(),
            P(),
            P(),
            P(),
            P(),
            P(),
        ),
        out_specs=(P(), P(), P(), P(), P()),
        check_vma=False,
    )
```

```python
import math

import jax
import jax.numpy as jnp
from jax import lax
from jax.experimental import pallas as pl
from jax.experimental.pallas import tpu as pltpu
from jax.sharding import PartitionSpec as P

BF = jnp.bfloat16
F32 = jnp.float32
MESH = pl.DeviceIdType.MESH

NX, NY, NZ = 4, 4, 8
SIZE = {"x": NX, "y": NY, "z": NZ}
DEEPEST_AT, DEEPER_AT, TEMPORAL_AT, HEAD_AT, MIDDLE_AT = 0, 576, 720, 765, 768
PARTS = (
    (("z", "x", "y"), False, 5),
    (("x", "y", "z"), True, 1),
    (("y", "x", "z"), True, 1),
)


def shares(order, split):
    return SIZE[order[0]], SIZE[order[1]], SIZE[order[2]] if split else 1


LENGTHS = tuple(math.prod(shares(order, split)) * kept for order, split, kept in PARTS)
STARTS = tuple(sum(LENGTHS[:i]) for i in range(len(PARTS)))
HALF = sum(LENGTHS)
TILES = 2 * HALF


def vmem():
    return pl.BlockSpec(memory_space=pltpu.VMEM)


def halo_kernel(occ_ref, window_ref, landed, send_sem, recv_sem):
    space = lax.axis_index("space")
    below = lax.rem(space + 1, 8)
    above = lax.rem(space + 7, 8)
    barrier = pltpu.get_barrier_semaphore()
    for peer in (below, above):
        pl.semaphore_signal(barrier, inc=1, device_id={"space": peer}, device_id_type=MESH)
    pl.semaphore_wait(barrier, 2)
    copy = pltpu.make_async_remote_copy(
        src_ref=occ_ref,
        dst_ref=landed,
        send_sem=send_sem,
        recv_sem=recv_sem,
        device_id={"space": below},
        device_id_type=MESH,
    )
    copy.start()
    window_ref[:, 16:32, :] = occ_ref[...]
    copy.wait()
    keep = jnp.where(space == 0, 0, 1)
    window_ref[:, 0:16, :] = landed[...] * keep


def halo(occ):
    return pl.pallas_call(
        halo_kernel,
        out_shape=jax.ShapeDtypeStruct((5, 32, 128), jnp.int32),
        in_specs=[vmem()],
        out_specs=vmem(),
        scratch_shapes=[
            pltpu.VMEM((5, 16, 128), jnp.int32),
            pltpu.SemaphoreType.DMA(()),
            pltpu.SemaphoreType.DMA(()),
        ],
        compiler_params=pltpu.CompilerParams(collective_id=0, has_side_effects=True),
    )(occ)


def dot(a, b):
    return lax.dot_general(a, b, (((1,), (0,)), ((), ())), preferred_element_type=F32)


def dot_nt(a, b):
    return lax.dot_general(a, b, (((1,), (1,)), ((), ())), preferred_element_type=F32)


def dot_tn(a, b):
    return lax.dot_general(a, b, (((0,), (0,)), ((), ())), preferred_element_type=F32)


def activate(pre):
    gate = jax.nn.sigmoid(pre)
    slope = gate * (1.0 + pre * (1.0 - gate))
    return pre * gate, slope


def later(block):
    rolled = pltpu.roll(block, 1, block.ndim - 2)
    index = lax.broadcasted_iota(jnp.int32, block.shape, block.ndim - 2)
    return jnp.where(index == 0, 0.0, rolled)


def sooner(block):
    size = block.shape[-2]
    rolled = pltpu.roll(block, size - 1, block.ndim - 2)
    index = lax.broadcasted_iota(jnp.int32, block.shape, block.ndim - 2)
    return jnp.where(index == size - 1, 0.0, rolled)


def tap_of(ref, p, q, rows, phases):
    a, b = p // 2, p % 2
    c, d = q // 2, q % 2
    block = ref[a : a + rows, b, c : c + phases, d]
    return block.reshape(rows * phases * block.shape[2], block.shape[3])


def store_map(ref, value, rows, phases):
    shifted = later(value[:, phases - 1])
    for r in range(rows):
        ref[r // 2, r % 2, 0, 0] = shifted[r].astype(BF)
        for m in range(phases):
            s = m + 1
            ref[r // 2, r % 2, s // 2, s % 2] = value[r, m].astype(BF)


def map_grad(delta, weight_ref, rows, phases):
    out = {}

    def put(r, m, value):
        out[(r, m)] = value if (r, m) not in out else out[(r, m)] + value

    for p in range(3):
        for q in range(3):
            part = dot_nt(delta, weight_ref[3 * p + q])
            part = part.reshape(rows, phases, 16, part.shape[1])
            for m in range(phases):
                s = 2 * m + q - 1
                for o in range(rows):
                    value = part[o, m]
                    if s < 0:
                        put(2 * o + p, 2 * phases - 1, sooner(value))
                    else:
                        put(2 * o + p, s, value)
    return out


def every_second(ref, r, start):
    halves = [ref[r, h, pl.ds(start, 16, stride=2), :] for h in range(2)]
    return jnp.concatenate(halves, axis=1)


def compute_kernel(
    window_ref,
    labels_ref,
    lift_ref,
    w1_ref,
    w2_ref,
    w3_ref,
    w4_ref,
    head_ref,
    grads_ref,
    lifted,
    first,
    first_slope,
    second,
    second_slope,
    third,
    third_slope,
    third_dx,
    first_delta,
):
    to = lax.broadcasted_iota(jnp.int32, (128, 128), 0)
    come = lax.broadcasted_iota(jnp.int32, (128, 128), 1)
    order = jnp.where(come == lax.rem(to, 16) * 8 + to // 16, 1.0, 0.0).astype(BF)
    shifts = lax.broadcasted_iota(jnp.int32, (16, 128), 0)
    lift = lift_ref[...]
    for r in range(31):
        frames = []
        for t in range(5):
            row = jnp.broadcast_to(window_ref[t, r + 1 : r + 2, :], (16, 128))
            bits = jnp.bitwise_and(jnp.right_shift(row, shifts), 1)
            frames.append(bits.astype(F32).astype(BF))
        turned = dot_nt(order, jnp.concatenate(frames, axis=0)).astype(BF)
        value = jnp.maximum(dot(turned, lift), 0.0).reshape(8, 16, 160)
        lifted[r // 2, r % 2, 0, 0] = later(value[7]).astype(BF)
        for m in range(8):
            s = m + 1
            lifted[r // 2, r % 2, s // 2, s % 2] = value[m].astype(BF)
    zero_row = jnp.zeros((5, 2, 16, 160), BF)
    lifted[15, 1] = zero_row
    lifted[16, 0] = zero_row
    lifted[16, 1] = zero_row

    pre = jnp.zeros((960, 64), F32)
    for p in range(3):
        for q in range(3):
            pre = pre + dot(tap_of(lifted, p, q, 15, 4), w1_ref[3 * p + q])
    value, slope = activate(pre)
    store_map(first, value.reshape(15, 4, 16, 64), 15, 4)
    first_slope[...] = slope.reshape(15, 4, 16, 64)

    pre = jnp.zeros((224, 128), F32)
    for p in range(3):
        for q in range(3):
            pre = pre + dot(tap_of(first, p, q, 7, 2), w2_ref[3 * p + q])
    value, slope = activate(pre)
    store_map(second, value.reshape(7, 2, 16, 128), 7, 2)
    second_slope[...] = slope.reshape(7, 2, 16, 128)

    pre = jnp.zeros((48, 256), F32)
    for p in range(3):
        for q in range(3):
            pre = pre + dot(tap_of(second, p, q, 3, 1), w3_ref[3 * p + q])
    value, slope = activate(pre)
    third[...] = jnp.zeros((3, 2, 32, 128), F32)
    for r in range(3):
        for h in range(2):
            third[r, h, 0:16, :] = value[16 * r : 16 * r + 16, 128 * h : 128 * h + 128]
    third_slope[...] = slope.reshape(3, 16, 256)

    place = lax.broadcasted_iota(jnp.int32, (16, 256), 0)
    cells = []
    pre = jnp.zeros((16, 512), F32)
    for p in range(3):
        even = every_second(third, p, 0)
        odd = every_second(third, p, 1)
        left = jnp.where((place > 0) & (place < 8), pltpu.roll(odd, 1, 0), 0.0)
        for q, block in enumerate((left, even, odd)):
            block = block.astype(BF)
            cells.append(block)
            pre = pre + dot(block, w4_ref[3 * p + q])
    value, slope = activate(pre)
    fourth = value.astype(BF).astype(F32)
    head = head_ref[...].astype(F32)
    logits = jnp.sum(fourth * head, axis=1, keepdims=True)
    logit_grad = (jax.nn.sigmoid(logits) - labels_ref[...].astype(F32)) / 32.0
    logit_grad = jnp.where(lax.broadcasted_iota(jnp.int32, (16, 1), 0) < 8, logit_grad, 0.0)
    head_grad = jnp.sum(fourth * logit_grad, axis=0, keepdims=True)
    grads_ref[HEAD_AT : HEAD_AT + 3] = jnp.zeros((3, 16, 128), BF)
    for lane in range(4):
        part = head_grad[:, 128 * lane : 128 * lane + 128]
        grads_ref[HEAD_AT, :, :] = jnp.where(
            lax.broadcasted_iota(jnp.int32, (16, 128), 0) == lane,
            jnp.broadcast_to(part, (16, 128)),
            grads_ref[HEAD_AT].astype(F32),
        ).astype(BF)
    grads_ref[804:TILES] = jnp.zeros((TILES - 804, 16, 128), BF)
    delta = (logit_grad * head * slope).astype(BF)

    for p in range(3):
        parts = []
        for q in range(3):
            t = 3 * p + q
            grad = dot_tn(cells[t], delta).astype(BF)
            for lane in range(4):
                grads_ref[64 * t + 16 * lane : 64 * t + 16 * lane + 16] = grad[
                    :, 128 * lane : 128 * lane + 128
                ].reshape(16, 16, 128)
            parts.append(dot_nt(delta, w4_ref[t]))
        odd = parts[2] + pltpu.roll(parts[0], 15, 0)
        for h in range(2):
            lanes = slice(128 * h, 128 * h + 128)
            third_dx[p, h, pl.ds(0, 16, stride=2), :] = parts[1][:, lanes]
            third_dx[p, h, pl.ds(1, 16, stride=2), :] = odd[:, lanes]
    delta = jnp.concatenate(
        [
            jnp.concatenate([third_dx[r, h, 0:16, :] for h in range(2)], axis=1) * third_slope[r]
            for r in range(3)
        ],
        axis=0,
    ).astype(BF)

    for t in range(9):
        grad = dot_tn(tap_of(second, t // 3, t % 3, 3, 1), delta).astype(BF)
        for lane in range(2):
            at = DEEPER_AT + 16 * t + 8 * lane
            grads_ref[at : at + 8] = grad[:, 128 * lane : 128 * lane + 128].reshape(8, 16, 128)
    dx = map_grad(delta, w3_ref, 3, 1)
    delta = jnp.concatenate(
        [dx[(r, m)] * second_slope[r, m] for r in range(7) for m in range(2)], axis=0
    ).astype(BF)

    for t in range(9):
        grad = dot_tn(tap_of(first, t // 3, t % 3, 7, 2), delta).astype(BF)
        at = MIDDLE_AT + 4 * t
        grads_ref[at : at + 4] = grad.reshape(4, 16, 128)
    dx = map_grad(delta, w2_ref, 7, 2)
    for r in range(15):
        for m in range(4):
            at = 64 * r + 16 * m
            first_delta[at : at + 16, :] = dx[(r, m)] * first_slope[r, m]
    first_delta[960:1024, :] = jnp.zeros((64, 64), F32)

    turned = jnp.transpose(first_delta[...]).astype(BF)
    for t in range(9):
        grad = dot(turned, tap_of(lifted, t // 3, t % 3, 16, 4))
        grad = jnp.transpose(grad)
        grad = jnp.concatenate([grad[0:80], grad[80:160]], axis=1).astype(BF)
        at = TEMPORAL_AT + 5 * t
        grads_ref[at : at + 5] = grad.reshape(5, 16, 128)


def compute(window, labels, lift, w1, w2, w3, w4, head):
    return pl.pallas_call(
        compute_kernel,
        out_shape=jax.ShapeDtypeStruct((TILES, 16, 128), BF),
        in_specs=[vmem()] * 8,
        out_specs=vmem(),
        scratch_shapes=[
            pltpu.VMEM((17, 2, 5, 2, 16, 160), BF),
            pltpu.VMEM((8, 2, 3, 2, 16, 64), BF),
            pltpu.VMEM((15, 4, 16, 64), F32),
            pltpu.VMEM((4, 2, 2, 2, 16, 128), BF),
            pltpu.VMEM((7, 2, 16, 128), F32),
            pltpu.VMEM((3, 2, 32, 128), F32),
            pltpu.VMEM((3, 16, 256), F32),
            pltpu.VMEM((3, 2, 32, 128), F32),
            pltpu.VMEM((1024, 64), F32),
        ],
        compiler_params=pltpu.CompilerParams(vmem_limit_bytes=48 * 1024 * 1024),
    )(window, labels, lift, w1, w2, w3, w4, head)


def position():
    dp = lax.axis_index("dp")
    space = lax.axis_index("space")
    return {
        "x": space // 2,
        "y": lax.rem(space, 2) * 2 + lax.rem(dp // 2, 2),
        "z": dp // 4,
        "core": lax.rem(dp, 2),
    }


def device_at(place):
    dp = place["z"] * 4 + lax.rem(place["y"], 2) * 2 + place["core"]
    space = place["x"] * 2 + place["y"] // 2
    return (dp, space)


def along(here, axis, distance):
    there = dict(here)
    size = SIZE[axis]
    there[axis] = lax.rem(here[axis] + distance + size, size)
    return there


class Wires:
    def __init__(self, send_sem, recv_sem):
        self.send_sem, self.recv_sem = send_sem, recv_sem
        self.used = 0
        self.sent = []

    def send(self, src, dst, place):
        copy = pltpu.make_async_remote_copy(
            src_ref=src,
            dst_ref=dst,
            send_sem=self.send_sem.at[self.used],
            recv_sem=self.recv_sem.at[self.used],
            device_id=device_at(place),
            device_id_type=MESH,
        )
        self.used += 1
        copy.start()
        self.sent.append(copy)
        return copy

    def finish(self):
        for copy in self.sent:
            copy.wait_send()


def greet(here):
    partner = dict(here)
    partner["core"] = 1 - here["core"]
    barrier = pltpu.get_barrier_semaphore()
    peers = [device_at(partner)]
    for axis, size in SIZE.items():
        peers += [device_at(along(here, axis, d)) for d in range(1, size)]
    for peer in peers:
        pl.semaphore_signal(barrier, inc=1, device_id=peer, device_id_type=MESH)
    pl.semaphore_wait(barrier, len(peers))


def f32(block):
    return block.astype(F32)


def relayed_scatter(wires, here, axis, parts, right_in, left_in, right_out, left_out, m):
    n = SIZE[axis]
    half, h = n // 2, m // 2
    me = here[axis]
    right, left = along(here, axis, 1), along(here, axis, -1)

    def chunk(distance):
        return lax.rem(me + distance + n, n)

    lo, hi = pl.ds(0, h), pl.ds(h, m - h)
    far = chunk(half)
    from_left = [wires.send(parts.at[far, lo], right_in.at[0, lo], right)]
    from_right = [wires.send(parts.at[far, hi], left_in.at[0, hi], left)]
    early_left = wires.send(parts.at[chunk(half - 1), hi], right_in.at[1, hi], right)
    early_right = wires.send(parts.at[chunk(1 - half), lo], left_in.at[1, lo], left)
    for s in range(1, half):
        yield
        to_right, to_left = chunk(half - s), chunk(s - half)
        if s == 1:
            from_left[-1].wait_recv()
            right_out[0, 0:h] = (f32(parts[to_right, 0:h]) + f32(right_in[0, 0:h])).astype(BF)
            from_left.append(wires.send(right_out.at[0, lo], right_in.at[1, lo], right))
            from_right[-1].wait_recv()
            left_out[0, h:m] = (f32(parts[to_left, h:m]) + f32(left_in[0, h:m])).astype(BF)
            from_right.append(wires.send(left_out.at[0, hi], left_in.at[1, hi], left))
        else:
            if s == 2:
                early_left.wait_recv()
                early_right.wait_recv()
            from_left[-1].wait_recv()
            right_out[s - 1] = (f32(parts[to_right]) + f32(right_in[s - 1])).astype(BF)
            from_left.append(wires.send(right_out.at[s - 1], right_in.at[s], right))
            from_right[-1].wait_recv()
            left_out[s - 1] = (f32(parts[to_left]) + f32(left_in[s - 1])).astype(BF)
            from_right.append(wires.send(left_out.at[s - 1], left_in.at[s], left))
    yield
    if half == 2:
        early_left.wait_recv()
        early_right.wait_recv()
    from_left[-1].wait_recv()
    from_right[-1].wait_recv()
    return f32(parts[me]) + f32(right_in[half - 1]) + f32(left_in[half - 1])


def relayed_gather(wires, here, axis, total_ref, base, m, partner):
    n = SIZE[axis]
    half, h = n // 2, m // 2
    me = here[axis]
    right, left = along(here, axis, 1), along(here, axis, -1)
    swapped = []

    def piece(distance, at, size):
        k = lax.rem(me + distance + n, n)
        return total_ref.at[pl.ds(base + k * m + at, size)]

    def swap(where):
        swapped.append(wires.send(where, where, partner))

    own = piece(0, 0, m)
    from_left = wires.send(own, own, right)
    from_right = wires.send(own, own, left)
    swap(own)
    for s in range(1, half):
        yield
        from_left.wait_recv()
        at, size = (0, h) if s == half - 1 else (0, m)
        here_now = piece(-s, at, size)
        from_left = wires.send(here_now, here_now, right)
        swap(piece(-s, 0, m))
        from_right.wait_recv()
        at, size = (h, m - h) if s == half - 1 else (0, m)
        here_now = piece(s, at, size)
        from_right = wires.send(here_now, here_now, left)
        swap(piece(s, 0, m))
    yield
    from_left.wait_recv()
    swap(piece(-half, 0, h))
    from_right.wait_recv()
    swap(piece(half, h, m - h))
    yield
    for copy in swapped:
        copy.wait_recv()


def direct_scatter(wires, here, axis, parts, landed):
    n = SIZE[axis]
    flights = []
    for d in range(1, n):
        there = along(here, axis, d)
        flights.append(wires.send(parts.at[there[axis]], landed.at[d - 1], there))
    yield
    for copy in flights:
        copy.wait_recv()
    total = f32(parts[here[axis]])
    for d in range(1, n):
        total = total + f32(landed[d - 1])
    return total


def direct_gather(wires, here, axis, total_ref, base, m):
    n = SIZE[axis]
    own = total_ref.at[pl.ds(base + here[axis] * m, m)]
    flights = [wires.send(own, own, along(here, axis, d)) for d in range(1, n)]
    yield
    for copy in flights:
        copy.wait_recv()


def direct_exchange(wires, here, axis, own, landed):
    n = SIZE[axis]
    me = here[axis]
    flights = []
    for d in range(1, n):
        flights.append(wires.send(own, landed.at[d - 1], along(here, axis, d)))
    yield
    for copy in flights:
        copy.wait_recv()
    total = jnp.zeros(own.shape, F32)
    for k in range(n):
        back = lax.rem(me - k + n, n)
        other = f32(landed[lax.rem(back + n - 1, n)])
        total = total + jnp.where(back == 0, f32(own[...]), other)
    return total


def part_scratch(order, split, kept):
    a, b, c = shares(order, split)
    m = b * c * kept
    return [
        pltpu.VMEM((a, m, 16, 128), BF),
        pltpu.VMEM((a // 2, m, 16, 128), BF),
        pltpu.VMEM((a // 2, m, 16, 128), BF),
        pltpu.VMEM((a // 2, m, 16, 128), BF),
        pltpu.VMEM((a // 2, m, 16, 128), BF),
        pltpu.VMEM((b, c * kept, 16, 128), BF),
        pltpu.VMEM((b - 1, c * kept, 16, 128), BF),
        pltpu.VMEM((c, kept, 16, 128), BF),
        pltpu.VMEM((SIZE[order[2]], kept, 16, 128), BF),
    ]


def reduce_part(wires, here, partner, grads_ref, total_ref, paired, scratch, start, part):
    shared, right_in, left_in, right_out, left_out, sum1, landed2, sum2, landed3 = scratch
    order, split, kept = part
    a, b, c = shares(order, split)
    m = b * c * kept
    core = here["core"]
    there = pl.ds((1 - core) * HALF + start, a * m)
    flight = wires.send(grads_ref.at[there], paired.at[pl.ds(start, a * m)], partner)
    yield
    flight.wait_recv()
    both = f32(grads_ref[pl.ds(core * HALF + start, a * m)]) + f32(paired[start : start + a * m])
    shared[...] = both.astype(BF).reshape(a, m, 16, 128)
    total = yield from relayed_scatter(
        wires, here, order[0], shared, right_in, left_in, right_out, left_out, m
    )
    sum1[...] = total.astype(BF).reshape(b, c * kept, 16, 128)
    total = yield from direct_scatter(wires, here, order[1], sum1, landed2)
    sum2[...] = total.astype(BF).reshape(c, kept, 16, 128)
    if split:
        total = yield from direct_scatter(wires, here, order[2], sum2, landed3)
    else:
        total = yield from direct_exchange(wires, here, order[2], sum2.at[0], landed3)
    base0 = core * HALF + start
    base1 = base0 + here[order[0]] * m
    base2 = base1 + here[order[1]] * (c * kept)
    if split:
        total_ref[pl.ds(base2 + here[order[2]] * kept, kept)] = total.astype(BF)
        yield from direct_gather(wires, here, order[2], total_ref, base2, kept)
    else:
        total_ref[pl.ds(base2, kept)] = total.astype(BF)
    yield from direct_gather(wires, here, order[1], total_ref, base1, c * kept)
    yield from relayed_gather(wires, here, order[0], total_ref, base0, m, partner)


def interleave(programs):
    programs = list(programs)
    while programs:
        still = []
        for program in programs:
            try:
                next(program)
                still.append(program)
            except StopIteration:
                pass
        programs = still


def reduce_all(here, grads_ref, total_ref, scratch):
    paired, send_sem, recv_sem, *rest = scratch
    partner = dict(here)
    partner["core"] = 1 - here["core"]
    wires = Wires(send_sem, recv_sem)
    programs = []
    for i, part in enumerate(PARTS):
        scratch = rest[9 * i : 9 * i + 9]
        programs.append(
            reduce_part(
                wires, here, partner, grads_ref, total_ref, paired, scratch, STARTS[i], part
            )
        )
    interleave(programs)
    wires.finish()


def reduce_scratch():
    scratch = [
        pltpu.VMEM((HALF, 16, 128), BF),
        pltpu.SemaphoreType.DMA((128,)),
        pltpu.SemaphoreType.DMA((128,)),
    ]
    for order, split, kept in PARTS:
        scratch += part_scratch(order, split, kept)
    return scratch


def reduce_kernel(grads_ref, total_ref, *scratch):
    here = position()
    greet(here)
    reduce_all(here, grads_ref, total_ref, scratch)


def all_reduce(grads):
    return pl.pallas_call(
        reduce_kernel,
        out_shape=jax.ShapeDtypeStruct((TILES, 16, 128), BF),
        in_specs=[vmem()],
        out_specs=vmem(),
        scratch_shapes=reduce_scratch(),
        compiler_params=pltpu.CompilerParams(
            collective_id=1, has_side_effects=True, vmem_limit_bytes=48 * 1024 * 1024
        ),
    )(grads)


def unpack_kernel(d4, d3, d1, dh, d2, g1, g2, g3, g4, gh):
    for lane in range(4):
        g4[0, :, 128 * lane : 128 * lane + 128] = (
            d4[16 * lane : 16 * lane + 16].reshape(256, 128).astype(F32)
        )
    for lane in range(2):
        g3[0, :, 128 * lane : 128 * lane + 128] = (
            d3[8 * lane : 8 * lane + 8].reshape(128, 128).astype(F32)
        )
    g2[0] = d2[...].reshape(64, 128).astype(F32)
    block = d1[...].reshape(80, 128).astype(F32)
    g1[0, 0:80, :] = block[:, 0:64]
    g1[0, 80:160, :] = block[:, 64:128]
    gh[...] = dh[0, 0:8, :].astype(F32)


def unpack(total):
    return pl.pallas_call(
        unpack_kernel,
        grid=(9,),
        out_shape=[
            jax.ShapeDtypeStruct((9, 160, 64), F32),
            jax.ShapeDtypeStruct((9, 64, 128), F32),
            jax.ShapeDtypeStruct((9, 128, 256), F32),
            jax.ShapeDtypeStruct((9, 256, 512), F32),
            jax.ShapeDtypeStruct((8, 128), F32),
        ],
        in_specs=[
            pl.BlockSpec((64, 16, 128), lambda t: (t, 0, 0)),
            pl.BlockSpec((16, 16, 128), lambda t: (DEEPER_AT // 16 + t, 0, 0)),
            pl.BlockSpec((5, 16, 128), lambda t: (TEMPORAL_AT // 5 + t, 0, 0)),
            pl.BlockSpec((1, 16, 128), lambda t: (HEAD_AT, 0, 0)),
            pl.BlockSpec((4, 16, 128), lambda t: (MIDDLE_AT // 4 + t, 0, 0)),
        ],
        out_specs=[
            pl.BlockSpec((1, 160, 64), lambda t: (t, 0, 0)),
            pl.BlockSpec((1, 64, 128), lambda t: (t, 0, 0)),
            pl.BlockSpec((1, 128, 256), lambda t: (t, 0, 0)),
            pl.BlockSpec((1, 256, 512), lambda t: (t, 0, 0)),
            pl.BlockSpec((8, 128), lambda t: (0, 0)),
        ],
    )(total, total, total, total, total)


def local(
    occupancy,
    state_labels,
    lift_weight,
    temporal_weight,
    middle_weight,
    deeper_weight,
    deepest_weight,
    head_weight,
):
    window = halo(occupancy[0])
    labels = jnp.pad(state_labels.reshape(8, 1), ((0, 8), (0, 0)))
    padded = jnp.pad(lift_weight, ((0, 3), (0, 0)))
    spread = jnp.eye(5, dtype=BF)[:, None, :, None] * padded[None, :, None, :]
    grads = compute(
        window,
        labels,
        spread.reshape(80, 160),
        temporal_weight.reshape(9, 160, 64),
        middle_weight.reshape(9, 64, 128),
        deeper_weight.reshape(9, 128, 256),
        deepest_weight.reshape(9, 256, 512),
        head_weight.reshape(1, 512),
    )
    g1, g2, g3, g4, gh = unpack(all_reduce(grads))
    return (
        g1.reshape(3, 3, 5, 32, 64),
        g2.reshape(3, 3, 64, 128),
        g3.reshape(3, 3, 128, 256),
        g4.reshape(3, 3, 256, 512),
        gh[0:4].reshape(512),
    )


def solution(mesh):
    return jax.shard_map(
        local,
        mesh=mesh,
        in_specs=(
            P("dp", None, "space", None),
            P("dp", "space", None),
            P(),
            P(),
            P(),
            P(),
            P(),
            P(),
        ),
        out_specs=(P(), P(), P(), P(), P()),
        check_vma=False,
    )
```

```python
import math

import jax
import jax.numpy as jnp
from jax import lax
from jax.experimental import pallas as pl
from jax.experimental.pallas import tpu as pltpu
from jax.sharding import PartitionSpec as P

BF = jnp.bfloat16
F32 = jnp.float32
MESH = pl.DeviceIdType.MESH

NX, NY, NZ = 4, 4, 8
SIZE = {"x": NX, "y": NY, "z": NZ}
DEEPEST_AT, DEEPER_AT, MIDDLE_AT, TEMPORAL_AT = 0, 288, 360, 378
HEAD_AT, HALF_ENDS = 398, (403, 399)
PARTS = (
    (("z", "x", "y"), False, 5),
    (("x", "y", "z"), True, 1),
    (("y", "x", "z"), True, 1),
)


def shares(order, split):
    return SIZE[order[0]], SIZE[order[1]], SIZE[order[2]] if split else 1


LENGTHS = tuple(math.prod(shares(order, split)) * kept for order, split, kept in PARTS)
STARTS = tuple(sum(LENGTHS[:i]) for i in range(len(PARTS)))
HALF = sum(LENGTHS)
TILES = 2 * HALF


def vmem():
    return pl.BlockSpec(memory_space=pltpu.VMEM)


def dot(a, b):
    return lax.dot_general(a, b, (((1,), (0,)), ((), ())), preferred_element_type=F32)


def dot_nt(a, b):
    return lax.dot_general(a, b, (((1,), (1,)), ((), ())), preferred_element_type=F32)


def dot_tn(a, b):
    return lax.dot_general(a, b, (((0,), (0,)), ((), ())), preferred_element_type=F32)


def activate(pre):
    gate = jax.nn.sigmoid(pre)
    slope = gate * (1.0 + pre * (1.0 - gate))
    return pre * gate, slope


def later(block):
    rolled = pltpu.roll(block, 1, block.ndim - 2)
    index = lax.broadcasted_iota(jnp.int32, block.shape, block.ndim - 2)
    return jnp.where(index == 0, 0.0, rolled)


def sooner(block):
    size = block.shape[-2]
    rolled = pltpu.roll(block, size - 1, block.ndim - 2)
    index = lax.broadcasted_iota(jnp.int32, block.shape, block.ndim - 2)
    return jnp.where(index == size - 1, 0.0, rolled)


def tap_of(ref, p, q, rows, phases):
    a, b = p // 2, p % 2
    c, d = q // 2, q % 2
    block = ref[a : a + rows, b, c : c + phases, d]
    return block.reshape(rows * phases * block.shape[2], block.shape[3])


def store_map(ref, value, rows, phases):
    shifted = later(value[:, phases - 1])
    for r in range(rows):
        ref[r // 2, r % 2, 0, 0] = shifted[r].astype(BF)
        for m in range(phases):
            s = m + 1
            ref[r // 2, r % 2, s // 2, s % 2] = value[r, m].astype(BF)


def map_grad(delta, weight_ref, rows, phases):
    out = {}

    def put(r, m, value):
        out[(r, m)] = value if (r, m) not in out else out[(r, m)] + value

    for p in range(3):
        for q in range(3):
            part = dot_nt(delta, weight_ref[3 * p + q])
            part = part.reshape(rows, phases, 16, part.shape[1])
            for m in range(phases):
                s = 2 * m + q - 1
                for o in range(rows):
                    value = part[o, m]
                    if s < 0:
                        put(2 * o + p, 2 * phases - 1, sooner(value))
                    else:
                        put(2 * o + p, s, value)
    return out


def every_second(ref, r, start):
    halves = [ref[r, h, pl.ds(start, 16, stride=2), :] for h in range(2)]
    return jnp.concatenate(halves, axis=1)


def lift_row(order, shifts, lift, source, row, keep, lifted, r):
    frames = []
    for t in range(5):
        line = source[t, row : row + 1, :]
        if keep is not None:
            line = line * keep
        bits = jnp.bitwise_and(jnp.right_shift(jnp.broadcast_to(line, (16, 128)), shifts), 1)
        frames.append(bits.astype(F32).astype(BF))
    turned = dot_nt(order, jnp.concatenate(frames, axis=0)).astype(BF)
    value = jnp.maximum(dot(turned, lift), 0.0).reshape(8, 16, 160)
    lifted[r // 2, r % 2, 0, 0] = later(value[7]).astype(BF)
    for m in range(8):
        s = m + 1
        lifted[r // 2, r % 2, s // 2, s % 2] = value[m].astype(BF)


def step_kernel(
    occ_ref,
    labels_ref,
    lift_ref,
    w1_hbm,
    w2_hbm,
    w3_hbm,
    w4_hbm,
    head_ref,
    total_ref,
    w1_ref,
    w2_ref,
    w3_ref,
    w4_ref,
    weight_sem,
    landed,
    halo_sem,
    grads_ref,
    lift_pad,
    lifted,
    first,
    first_slope,
    second,
    second_slope,
    third,
    third_slope,
    third_dx,
    first_delta,
    *reduce_scratch,
):
    loads = [
        pltpu.make_async_copy(source, target, weight_sem.at[i])
        for i, (source, target) in enumerate(
            ((w1_hbm, w1_ref), (w2_hbm, w2_ref), (w3_hbm, w3_ref), (w4_hbm, w4_ref))
        )
    ]
    for load in loads:
        load.start()
    here = position()
    space = lax.axis_index("space")
    below = lax.rem(space + 1, 8)
    above = lax.rem(space + 7, 8)
    dp = lax.axis_index("dp")
    greet(here, [(dp, below), (dp, above)])
    halo = pltpu.make_async_remote_copy(
        src_ref=occ_ref,
        dst_ref=landed,
        send_sem=halo_sem.at[0],
        recv_sem=halo_sem.at[1],
        device_id=(dp, below),
        device_id_type=MESH,
    )
    halo.start()
    reducing = Reduction(here, grads_ref, total_ref, reduce_scratch)

    to = lax.broadcasted_iota(jnp.int32, (128, 128), 0)
    come = lax.broadcasted_iota(jnp.int32, (128, 128), 1)
    order = jnp.where(come == lax.rem(to, 16) * 8 + to // 16, 1.0, 0.0).astype(BF)
    shifts = lax.broadcasted_iota(jnp.int32, (16, 128), 0)
    lift_pad[...] = jnp.zeros((16, 32), F32)
    lift_pad[0:13, :] = lift_ref[...].astype(F32)
    wide = jnp.concatenate([lift_pad[...]] * 5, axis=1)
    frame_of = lax.broadcasted_iota(jnp.int32, (16, 160), 1) // 32
    lift = jnp.concatenate([jnp.where(frame_of == t, wide, 0.0) for t in range(5)], axis=0)
    lift = lift.astype(BF)
    zero_row = jnp.zeros((5, 2, 16, 160), BF)
    lifted[15, 1] = zero_row
    lifted[16, 0] = zero_row
    lifted[16, 1] = zero_row
    for half in range(2):
        grads_ref[half * HALF + HALF_ENDS[half] : half * HALF + HALF] = jnp.zeros(
            (HALF - HALF_ENDS[half], 16, 128), BF
        )
    for row in range(16):
        lift_row(order, shifts, lift, occ_ref, row, None, lifted, row + 15)
    halo.wait_recv()
    keep = jnp.where(space == 0, 0, 1)
    for row in range(1, 16):
        lift_row(order, shifts, lift, landed, row, keep, lifted, row - 1)

    loads[0].wait()
    pre = jnp.zeros((960, 64), F32)
    for p in range(3):
        for q in range(3):
            pre = pre + dot(tap_of(lifted, p, q, 15, 4), w1_ref[3 * p + q])
    value, slope = activate(pre)
    store_map(first, value.reshape(15, 4, 16, 64), 15, 4)
    first_slope[...] = slope.reshape(15, 4, 16, 64)

    loads[1].wait()
    pre = jnp.zeros((224, 128), F32)
    for p in range(3):
        for q in range(3):
            pre = pre + dot(tap_of(first, p, q, 7, 2), w2_ref[3 * p + q])
    value, slope = activate(pre)
    store_map(second, value.reshape(7, 2, 16, 128), 7, 2)
    second_slope[...] = slope.reshape(7, 2, 16, 128)

    loads[2].wait()
    pre = jnp.zeros((48, 256), F32)
    for p in range(3):
        for q in range(3):
            pre = pre + dot(tap_of(second, p, q, 3, 1), w3_ref[3 * p + q])
    value, slope = activate(pre)
    third[...] = jnp.zeros((3, 2, 32, 128), F32)
    for r in range(3):
        for h in range(2):
            third[r, h, 0:16, :] = value[16 * r : 16 * r + 16, 128 * h : 128 * h + 128]
    third_slope[...] = slope.reshape(3, 16, 256)

    loads[3].wait()
    place = lax.broadcasted_iota(jnp.int32, (16, 256), 0)
    cells = []
    pre = jnp.zeros((16, 512), F32)
    for p in range(3):
        even = every_second(third, p, 0)
        odd = every_second(third, p, 1)
        left = jnp.where((place > 0) & (place < 8), pltpu.roll(odd, 1, 0), 0.0)
        for q, block in enumerate((left, even, odd)):
            block = block.astype(BF)
            cells.append(block)
            pre = pre + dot(block, w4_ref[3 * p + q])
    value, slope = activate(pre)
    fourth = value.astype(BF).astype(F32)
    head = head_ref[...].astype(F32).reshape(1, 512)
    logits = jnp.sum(fourth * head, axis=1, keepdims=True)
    cell = lax.broadcasted_iota(jnp.int32, (16, 8), 0)
    lane = lax.broadcasted_iota(jnp.int32, (16, 8), 1)
    labels = jnp.broadcast_to(labels_ref[...].astype(F32), (16, 8))
    labels = jnp.sum(jnp.where(cell == lane, labels, 0.0), axis=1, keepdims=True)
    logit_grad = (jax.nn.sigmoid(logits) - labels) / 32.0
    logit_grad = jnp.where(lax.broadcasted_iota(jnp.int32, (16, 1), 0) < 8, logit_grad, 0.0)
    delta = (logit_grad * head * slope).astype(BF)

    for t in range(9):
        grad = dot_tn(cells[t], delta).astype(BF)
        for lane in range(4):
            at = (lane // 2) * HALF + DEEPEST_AT + 32 * t + 16 * (lane % 2)
            grads_ref[at : at + 16] = grad[:, 128 * lane : 128 * lane + 128].reshape(16, 16, 128)
        if t == 4:
            reducing.begin(0)
    reducing.begin(1)
    head_grad = jnp.sum(fourth * logit_grad, axis=0, keepdims=True)
    row = lax.broadcasted_iota(jnp.int32, (16, 128), 0)
    head_tile = jnp.zeros((16, 128), F32)
    for lane in range(4):
        part = jnp.broadcast_to(head_grad[:, 128 * lane : 128 * lane + 128], (16, 128))
        head_tile = jnp.where(row == lane, part, head_tile)
    grads_ref[HALF + HEAD_AT] = head_tile.astype(BF)
    for p in range(3):
        parts = [dot_nt(delta, w4_ref[3 * p + q]) for q in range(3)]
        odd = parts[2] + pltpu.roll(parts[0], 15, 0)
        for h in range(2):
            lanes = slice(128 * h, 128 * h + 128)
            third_dx[p, h, pl.ds(0, 16, stride=2), :] = parts[1][:, lanes]
            third_dx[p, h, pl.ds(1, 16, stride=2), :] = odd[:, lanes]
    delta = jnp.concatenate(
        [
            jnp.concatenate([third_dx[r, h, 0:16, :] for h in range(2)], axis=1) * third_slope[r]
            for r in range(3)
        ],
        axis=0,
    ).astype(BF)

    for t in range(9):
        grad = dot_tn(tap_of(second, t // 3, t % 3, 3, 1), delta).astype(BF)
        for half in range(2):
            at = half * HALF + DEEPER_AT + 8 * t
            grads_ref[at : at + 8] = grad[:, 128 * half : 128 * half + 128].reshape(8, 16, 128)
    dx = map_grad(delta, w3_ref, 3, 1)
    delta = jnp.concatenate(
        [dx[(r, m)] * second_slope[r, m] for r in range(7) for m in range(2)], axis=0
    ).astype(BF)
    reducing.advance(0)

    for t in range(9):
        grad = dot_tn(tap_of(first, t // 3, t % 3, 7, 2), delta).astype(BF).reshape(4, 16, 128)
        for half in range(2):
            at = half * HALF + MIDDLE_AT + 2 * t
            grads_ref[at : at + 2] = grad[2 * half : 2 * half + 2]
    reducing.advance(1)
    dx = map_grad(delta, w2_ref, 7, 2)
    for r in range(15):
        for m in range(4):
            at = 64 * r + 16 * m
            first_delta[at : at + 16, :] = dx[(r, m)] * first_slope[r, m]
    first_delta[960:1024, :] = jnp.zeros((64, 64), F32)
    reducing.advance(0)

    turned = jnp.transpose(first_delta[...]).astype(BF)
    for t in range(9):
        grad = dot(turned, tap_of(lifted, t // 3, t % 3, 16, 4))
        grad = jnp.transpose(grad)
        grad = jnp.concatenate([grad[0:80], grad[80:160]], axis=1).astype(BF)
        at = TEMPORAL_AT + 5 * t if t < 5 else HALF + TEMPORAL_AT + 5 * (t - 5)
        grads_ref[at : at + 5] = grad.reshape(5, 16, 128)
    reducing.begin(2)
    reducing.finish()
    halo.wait_send()


def step(occ, labels, lift, w1, w2, w3, w4, head):
    hbm = pl.BlockSpec(memory_space=pl.ANY)
    return pl.pallas_call(
        step_kernel,
        out_shape=jax.ShapeDtypeStruct((TILES, 16, 128), BF),
        in_specs=[vmem()] * 3 + [hbm] * 4 + [vmem()],
        out_specs=vmem(),
        scratch_shapes=[
            pltpu.VMEM(w1.shape, BF),
            pltpu.VMEM(w2.shape, BF),
            pltpu.VMEM(w3.shape, BF),
            pltpu.VMEM(w4.shape, BF),
            pltpu.SemaphoreType.DMA((4,)),
            pltpu.VMEM((5, 16, 128), jnp.int32),
            pltpu.SemaphoreType.DMA((2,)),
            pltpu.VMEM((TILES, 16, 128), BF),
            pltpu.VMEM((16, 32), F32),
            pltpu.VMEM((17, 2, 5, 2, 16, 160), BF),
            pltpu.VMEM((8, 2, 3, 2, 16, 64), BF),
            pltpu.VMEM((15, 4, 16, 64), F32),
            pltpu.VMEM((4, 2, 2, 2, 16, 128), BF),
            pltpu.VMEM((7, 2, 16, 128), F32),
            pltpu.VMEM((3, 2, 32, 128), F32),
            pltpu.VMEM((3, 16, 256), F32),
            pltpu.VMEM((3, 2, 32, 128), F32),
            pltpu.VMEM((1024, 64), F32),
        ]
        + reduce_scratch(),
        compiler_params=pltpu.CompilerParams(
            collective_id=0, has_side_effects=True, vmem_limit_bytes=50 * 1024 * 1024
        ),
    )(occ, labels, lift, w1, w2, w3, w4, head)


def position():
    dp = lax.axis_index("dp")
    space = lax.axis_index("space")
    return {
        "x": space // 2,
        "y": lax.rem(space, 2) * 2 + lax.rem(dp // 2, 2),
        "z": dp // 4,
        "core": lax.rem(dp, 2),
    }


def device_at(place):
    dp = place["z"] * 4 + lax.rem(place["y"], 2) * 2 + place["core"]
    space = place["x"] * 2 + place["y"] // 2
    return (dp, space)


def along(here, axis, distance):
    there = dict(here)
    size = SIZE[axis]
    there[axis] = lax.rem(here[axis] + distance + size, size)
    return there


class Wires:
    def __init__(self, send_sem, recv_sem):
        self.send_sem, self.recv_sem = send_sem, recv_sem
        self.used = 0
        self.sent = []

    def send(self, src, dst, place):
        copy = pltpu.make_async_remote_copy(
            src_ref=src,
            dst_ref=dst,
            send_sem=self.send_sem.at[self.used],
            recv_sem=self.recv_sem.at[self.used],
            device_id=device_at(place),
            device_id_type=MESH,
        )
        self.used += 1
        copy.start()
        self.sent.append(copy)
        return copy

    def finish(self):
        for copy in self.sent:
            copy.wait_send()


def greet(here, others):
    partner = dict(here)
    partner["core"] = 1 - here["core"]
    barrier = pltpu.get_barrier_semaphore()
    peers = [device_at(partner)] + others
    for axis, size in SIZE.items():
        peers += [device_at(along(here, axis, d)) for d in range(1, size)]
    for peer in peers:
        pl.semaphore_signal(barrier, inc=1, device_id=peer, device_id_type=MESH)
    pl.semaphore_wait(barrier, len(peers))


def f32(block):
    return block.astype(F32)


def relayed_scatter(wires, here, axis, parts, right_in, left_in, right_out, left_out, m):
    n = SIZE[axis]
    half, h = n // 2, m // 2
    me = here[axis]
    right, left = along(here, axis, 1), along(here, axis, -1)

    def chunk(distance):
        return lax.rem(me + distance + n, n)

    lo, hi = pl.ds(0, h), pl.ds(h, m - h)
    far = chunk(half)
    from_left = [wires.send(parts.at[far, lo], right_in.at[0, lo], right)]
    from_right = [wires.send(parts.at[far, hi], left_in.at[0, hi], left)]
    early_left = wires.send(parts.at[chunk(half - 1), hi], right_in.at[1, hi], right)
    early_right = wires.send(parts.at[chunk(1 - half), lo], left_in.at[1, lo], left)
    for s in range(1, half):
        yield
        to_right, to_left = chunk(half - s), chunk(s - half)
        if s == 1:
            from_left[-1].wait_recv()
            right_out[0, 0:h] = (f32(parts[to_right, 0:h]) + f32(right_in[0, 0:h])).astype(BF)
            from_left.append(wires.send(right_out.at[0, lo], right_in.at[1, lo], right))
            from_right[-1].wait_recv()
            left_out[0, h:m] = (f32(parts[to_left, h:m]) + f32(left_in[0, h:m])).astype(BF)
            from_right.append(wires.send(left_out.at[0, hi], left_in.at[1, hi], left))
        else:
            if s == 2:
                early_left.wait_recv()
                early_right.wait_recv()
            from_left[-1].wait_recv()
            right_out[s - 1] = (f32(parts[to_right]) + f32(right_in[s - 1])).astype(BF)
            from_left.append(wires.send(right_out.at[s - 1], right_in.at[s], right))
            from_right[-1].wait_recv()
            left_out[s - 1] = (f32(parts[to_left]) + f32(left_in[s - 1])).astype(BF)
            from_right.append(wires.send(left_out.at[s - 1], left_in.at[s], left))
    yield
    if half == 2:
        early_left.wait_recv()
        early_right.wait_recv()
    from_left[-1].wait_recv()
    from_right[-1].wait_recv()
    return f32(parts[me]) + f32(right_in[half - 1]) + f32(left_in[half - 1])


def relayed_gather(wires, here, axis, total_ref, base, m, partner):
    n = SIZE[axis]
    half, h = n // 2, m // 2
    me = here[axis]
    right, left = along(here, axis, 1), along(here, axis, -1)
    swapped = []

    def piece(distance, at, size):
        k = lax.rem(me + distance + n, n)
        return total_ref.at[pl.ds(base + k * m + at, size)]

    def swap(where):
        swapped.append(wires.send(where, where, partner))

    own = piece(0, 0, m)
    from_left = wires.send(own, own, right)
    from_right = wires.send(own, own, left)
    swap(own)
    for s in range(1, half):
        yield
        from_left.wait_recv()
        at, size = (0, h) if s == half - 1 else (0, m)
        here_now = piece(-s, at, size)
        from_left = wires.send(here_now, here_now, right)
        swap(piece(-s, 0, m))
        from_right.wait_recv()
        at, size = (h, m - h) if s == half - 1 else (0, m)
        here_now = piece(s, at, size)
        from_right = wires.send(here_now, here_now, left)
        swap(piece(s, 0, m))
    yield
    from_left.wait_recv()
    swap(piece(-half, 0, h))
    from_right.wait_recv()
    swap(piece(half, h, m - h))
    yield
    for copy in swapped:
        copy.wait_recv()


def direct_scatter(wires, here, axis, parts, landed):
    n = SIZE[axis]
    flights = []
    for d in range(1, n):
        there = along(here, axis, d)
        flights.append(wires.send(parts.at[there[axis]], landed.at[d - 1], there))
    yield
    for copy in flights:
        copy.wait_recv()
    total = f32(parts[here[axis]])
    for d in range(1, n):
        total = total + f32(landed[d - 1])
    return total


def direct_gather(wires, here, axis, total_ref, base, m):
    n = SIZE[axis]
    own = total_ref.at[pl.ds(base + here[axis] * m, m)]
    flights = [wires.send(own, own, along(here, axis, d)) for d in range(1, n)]
    yield
    for copy in flights:
        copy.wait_recv()


def direct_exchange(wires, here, axis, own, landed):
    n = SIZE[axis]
    me = here[axis]
    flights = []
    for d in range(1, n):
        flights.append(wires.send(own, landed.at[d - 1], along(here, axis, d)))
    yield
    for copy in flights:
        copy.wait_recv()
    total = jnp.zeros(own.shape, F32)
    for k in range(n):
        back = lax.rem(me - k + n, n)
        other = f32(landed[lax.rem(back + n - 1, n)])
        total = total + jnp.where(back == 0, f32(own[...]), other)
    return total


def part_scratch(order, split, kept):
    a, b, c = shares(order, split)
    m = b * c * kept
    return [
        pltpu.VMEM((a, m, 16, 128), BF),
        pltpu.VMEM((a // 2, m, 16, 128), BF),
        pltpu.VMEM((a // 2, m, 16, 128), BF),
        pltpu.VMEM((a // 2, m, 16, 128), BF),
        pltpu.VMEM((a // 2, m, 16, 128), BF),
        pltpu.VMEM((b, c * kept, 16, 128), BF),
        pltpu.VMEM((b - 1, c * kept, 16, 128), BF),
        pltpu.VMEM((c, kept, 16, 128), BF),
        pltpu.VMEM((SIZE[order[2]], kept, 16, 128), BF),
    ]


def reduce_part(wires, here, partner, grads_ref, total_ref, paired, scratch, start, part):
    shared, right_in, left_in, right_out, left_out, sum1, landed2, sum2, landed3 = scratch
    order, split, kept = part
    a, b, c = shares(order, split)
    m = b * c * kept
    core = here["core"]
    there = pl.ds((1 - core) * HALF + start, a * m)
    flight = wires.send(grads_ref.at[there], paired.at[pl.ds(start, a * m)], partner)
    yield
    flight.wait_recv()
    both = f32(grads_ref[pl.ds(core * HALF + start, a * m)]) + f32(paired[start : start + a * m])
    shared[...] = both.astype(BF).reshape(a, m, 16, 128)
    total = yield from relayed_scatter(
        wires, here, order[0], shared, right_in, left_in, right_out, left_out, m
    )
    sum1[...] = total.astype(BF).reshape(b, c * kept, 16, 128)
    total = yield from direct_scatter(wires, here, order[1], sum1, landed2)
    sum2[...] = total.astype(BF).reshape(c, kept, 16, 128)
    if split:
        total = yield from direct_scatter(wires, here, order[2], sum2, landed3)
    else:
        total = yield from direct_exchange(wires, here, order[2], sum2.at[0], landed3)
    base0 = core * HALF + start
    base1 = base0 + here[order[0]] * m
    base2 = base1 + here[order[1]] * (c * kept)
    if split:
        total_ref[pl.ds(base2 + here[order[2]] * kept, kept)] = total.astype(BF)
        yield from direct_gather(wires, here, order[2], total_ref, base2, kept)
    else:
        total_ref[pl.ds(base2, kept)] = total.astype(BF)
    yield from direct_gather(wires, here, order[1], total_ref, base1, c * kept)
    yield from relayed_gather(wires, here, order[0], total_ref, base0, m, partner)


def interleave(programs):
    programs = list(programs)
    while programs:
        still = []
        for program in programs:
            try:
                next(program)
                still.append(program)
            except StopIteration:
                pass
        programs = still


class Reduction:
    def __init__(self, here, grads_ref, total_ref, scratch):
        paired, send_sem, recv_sem, *rest = scratch
        partner = dict(here)
        partner["core"] = 1 - here["core"]
        self.wires = Wires(send_sem, recv_sem)
        self.programs = []
        for i, part in enumerate(PARTS):
            own = rest[9 * i : 9 * i + 9]
            self.programs.append(
                reduce_part(
                    self.wires, here, partner, grads_ref, total_ref, paired, own, STARTS[i], part
                )
            )

    def begin(self, i):
        next(self.programs[i])

    advance = begin

    def finish(self):
        interleave(self.programs)
        self.wires.finish()


def reduce_scratch():
    scratch = [
        pltpu.VMEM((HALF, 16, 128), BF),
        pltpu.SemaphoreType.DMA((128,)),
        pltpu.SemaphoreType.DMA((128,)),
    ]
    for order, split, kept in PARTS:
        scratch += part_scratch(order, split, kept)
    return scratch


def unpack_kernel(total_ref, g1, g2, g3, g4, gh, s1, s2, s3, s4, sem):
    copies = []

    def out(source, target):
        copy = pltpu.make_async_copy(source, target, sem.at[len(copies)])
        copy.start()
        copies.append(copy)

    for t in range(9):
        for lane in range(4):
            at = (lane // 2) * HALF + DEEPEST_AT + 32 * t + 16 * (lane % 2)
            s4[t, :, 128 * lane : 128 * lane + 128] = f32(
                total_ref[at : at + 16].reshape(256, 128)
            )
        out(s4.at[t], g4.at[t])
    for t in range(9):
        for half in range(2):
            at = half * HALF + DEEPER_AT + 8 * t
            s3[t, :, 128 * half : 128 * half + 128] = f32(
                total_ref[at : at + 8].reshape(128, 128)
            )
    out(s3, g3)
    for t in range(9):
        for half in range(2):
            at = half * HALF + MIDDLE_AT + 2 * t
            s2[t, 32 * half : 32 * half + 32, :] = f32(total_ref[at : at + 2].reshape(32, 128))
        at = TEMPORAL_AT + 5 * t if t < 5 else HALF + TEMPORAL_AT + 5 * (t - 5)
        block = f32(total_ref[at : at + 5].reshape(80, 128))
        s1[t, 0:80, :] = block[:, 0:64]
        s1[t, 80:160, :] = block[:, 64:128]
    out(s2, g2)
    out(s1, g1)
    tile = f32(total_ref[HALF + HEAD_AT])
    for lane in range(4):
        gh[pl.ds(128 * lane, 128)] = tile[lane]
    for copy in copies:
        copy.wait()


def unpack(total):
    shapes = ((9, 160, 64), (9, 64, 128), (9, 128, 256), (9, 256, 512))
    hbm = pl.BlockSpec(memory_space=pl.ANY)
    return pl.pallas_call(
        unpack_kernel,
        out_shape=[jax.ShapeDtypeStruct(shape, F32) for shape in shapes + ((512,),)],
        in_specs=[vmem()],
        out_specs=[hbm] * 4 + [vmem()],
        scratch_shapes=[pltpu.VMEM(shape, F32) for shape in shapes]
        + [pltpu.SemaphoreType.DMA((12,))],
        compiler_params=pltpu.CompilerParams(vmem_limit_bytes=40 * 1024 * 1024),
    )(total)


def local(
    occupancy,
    state_labels,
    lift_weight,
    temporal_weight,
    middle_weight,
    deeper_weight,
    deepest_weight,
    head_weight,
):
    total = step(
        occupancy[0],
        state_labels[0],
        lift_weight,
        temporal_weight.reshape(9, 160, 64),
        middle_weight.reshape(9, 64, 128),
        deeper_weight.reshape(9, 128, 256),
        deepest_weight.reshape(9, 256, 512),
        head_weight,
    )
    g1, g2, g3, g4, gh = unpack(total)
    return (
        g1.reshape(3, 3, 5, 32, 64),
        g2.reshape(3, 3, 64, 128),
        g3.reshape(3, 3, 128, 256),
        g4.reshape(3, 3, 256, 512),
        gh,
    )


def solution(mesh):
    return jax.shard_map(
        local,
        mesh=mesh,
        in_specs=(
            P("dp", None, "space", None),
            P("dp", "space", None),
            P(),
            P(),
            P(),
            P(),
            P(),
            P(),
        ),
        out_specs=(P(), P(), P(), P(), P()),
        check_vma=False,
    )
```

```python
import math

import jax
import jax.numpy as jnp
from jax import lax
from jax.experimental import pallas as pl
from jax.experimental.pallas import tpu as pltpu
from jax.sharding import PartitionSpec as P

BF = jnp.bfloat16
F32 = jnp.float32
MESH = pl.DeviceIdType.MESH

NX, NY, NZ = 4, 4, 8
SIZE = {"x": NX, "y": NY, "z": NZ}
DEEPEST_AT, DEEPER_AT, MIDDLE_AT, TEMPORAL_AT = 0, 288, 360, 378
HEAD_AT, HALF_ENDS = 398, (403, 399)
PARTS = (
    (("z", "x", "y"), False, 3),
    (("x", "y", "z"), True, 1),
    (("y", "x", "z"), True, 1),
    (("x", "y", "z"), False, 2),
    (("y", "x", "z"), False, 2),
)


def shares(order, split):
    return SIZE[order[0]], SIZE[order[1]], SIZE[order[2]] if split else 1


LENGTHS = tuple(math.prod(shares(order, split)) * kept for order, split, kept in PARTS)
STARTS = tuple(sum(LENGTHS[:i]) for i in range(len(PARTS)))
HALF = sum(LENGTHS)
TILES = 2 * HALF


def vmem():
    return pl.BlockSpec(memory_space=pltpu.VMEM)


def dot(a, b):
    return lax.dot_general(a, b, (((1,), (0,)), ((), ())), preferred_element_type=F32)


def dot_nt(a, b):
    return lax.dot_general(a, b, (((1,), (1,)), ((), ())), preferred_element_type=F32)


def dot_tn(a, b):
    return lax.dot_general(a, b, (((0,), (0,)), ((), ())), preferred_element_type=F32)


def activate(pre):
    gate = jax.nn.sigmoid(pre)
    slope = gate * (1.0 + pre * (1.0 - gate))
    return pre * gate, slope


def later(block):
    rolled = pltpu.roll(block, 1, block.ndim - 2)
    index = lax.broadcasted_iota(jnp.int32, block.shape, block.ndim - 2)
    return jnp.where(index == 0, 0.0, rolled)


def sooner(block):
    size = block.shape[-2]
    rolled = pltpu.roll(block, size - 1, block.ndim - 2)
    index = lax.broadcasted_iota(jnp.int32, block.shape, block.ndim - 2)
    return jnp.where(index == size - 1, 0.0, rolled)


def tap_of(ref, p, q, rows, phases):
    a, b = p // 2, p % 2
    c, d = q // 2, q % 2
    block = ref[a : a + rows, b, c : c + phases, d]
    return block.reshape(rows * phases * block.shape[2], block.shape[3])


def store_map(ref, value, rows, phases):
    shifted = later(value[:, phases - 1])
    for r in range(rows):
        ref[r // 2, r % 2, 0, 0] = shifted[r].astype(BF)
        for m in range(phases):
            s = m + 1
            ref[r // 2, r % 2, s // 2, s % 2] = value[r, m].astype(BF)


def map_grad(delta, weight_ref, rows, phases):
    out = {}

    def put(r, m, value):
        out[(r, m)] = value if (r, m) not in out else out[(r, m)] + value

    for p in range(3):
        for q in range(3):
            part = dot_nt(delta, weight_ref[3 * p + q])
            part = part.reshape(rows, phases, 16, part.shape[1])
            for m in range(phases):
                s = 2 * m + q - 1
                for o in range(rows):
                    value = part[o, m]
                    if s < 0:
                        put(2 * o + p, 2 * phases - 1, sooner(value))
                    else:
                        put(2 * o + p, s, value)
    return out


def every_second(ref, r, start):
    halves = [ref[r, h, pl.ds(start, 16, stride=2), :] for h in range(2)]
    return jnp.concatenate(halves, axis=1)


def lift_row(order, shifts, lift, source, row, keep, lifted, r):
    frames = []
    for t in range(5):
        line = source[t, row : row + 1, :]
        if keep is not None:
            line = line * keep
        bits = jnp.bitwise_and(jnp.right_shift(jnp.broadcast_to(line, (16, 128)), shifts), 1)
        frames.append(bits.astype(F32).astype(BF))
    turned = dot_nt(order, jnp.concatenate(frames, axis=0)).astype(BF)
    value = jnp.maximum(dot(turned, lift), 0.0).reshape(8, 16, 160)
    lifted[r // 2, r % 2, 0, 0] = later(value[7]).astype(BF)
    for m in range(8):
        s = m + 1
        lifted[r // 2, r % 2, s // 2, s % 2] = value[m].astype(BF)


def step_kernel(
    occ_ref,
    labels_ref,
    lift_ref,
    w1_hbm,
    w2_hbm,
    w3_hbm,
    w4_hbm,
    head_ref,
    total_ref,
    w1_ref,
    w2_ref,
    w3_ref,
    w4_ref,
    weight_sem,
    landed,
    halo_sem,
    grads_ref,
    lift_pad,
    lifted,
    first,
    first_slope,
    second,
    second_slope,
    third,
    third_slope,
    third_dx,
    first_delta,
    *reduce_scratch,
):
    loads = [
        pltpu.make_async_copy(source, target, weight_sem.at[i])
        for i, (source, target) in enumerate(
            ((w1_hbm, w1_ref), (w2_hbm, w2_ref), (w3_hbm, w3_ref), (w4_hbm, w4_ref))
        )
    ]
    for load in loads:
        load.start()
    here = position()
    space = lax.axis_index("space")
    below = lax.rem(space + 1, 8)
    above = lax.rem(space + 7, 8)
    dp = lax.axis_index("dp")
    greet(here, [(dp, below), (dp, above)])
    halo = pltpu.make_async_remote_copy(
        src_ref=occ_ref,
        dst_ref=landed,
        send_sem=halo_sem.at[0],
        recv_sem=halo_sem.at[1],
        device_id=(dp, below),
        device_id_type=MESH,
    )
    halo.start()
    reducing = Reduction(here, grads_ref, total_ref, reduce_scratch)

    to = lax.broadcasted_iota(jnp.int32, (128, 128), 0)
    come = lax.broadcasted_iota(jnp.int32, (128, 128), 1)
    order = jnp.where(come == lax.rem(to, 16) * 8 + to // 16, 1.0, 0.0).astype(BF)
    shifts = lax.broadcasted_iota(jnp.int32, (16, 128), 0)
    lift_pad[...] = jnp.zeros((16, 32), F32)
    lift_pad[0:13, :] = lift_ref[...].astype(F32)
    wide = jnp.concatenate([lift_pad[...]] * 5, axis=1)
    frame_of = lax.broadcasted_iota(jnp.int32, (16, 160), 1) // 32
    lift = jnp.concatenate([jnp.where(frame_of == t, wide, 0.0) for t in range(5)], axis=0)
    lift = lift.astype(BF)
    zero_row = jnp.zeros((5, 2, 16, 160), BF)
    lifted[15, 1] = zero_row
    lifted[16, 0] = zero_row
    lifted[16, 1] = zero_row
    for half in range(2):
        grads_ref[half * HALF + HALF_ENDS[half] : half * HALF + HALF] = jnp.zeros(
            (HALF - HALF_ENDS[half], 16, 128), BF
        )
    for row in range(16):
        lift_row(order, shifts, lift, occ_ref, row, None, lifted, row + 15)
    halo.wait_recv()
    keep = jnp.where(space == 0, 0, 1)
    for row in range(1, 16):
        lift_row(order, shifts, lift, landed, row, keep, lifted, row - 1)

    loads[0].wait()
    pre = jnp.zeros((960, 64), F32)
    for p in range(3):
        for q in range(3):
            pre = pre + dot(tap_of(lifted, p, q, 15, 4), w1_ref[3 * p + q])
    value, slope = activate(pre)
    store_map(first, value.reshape(15, 4, 16, 64), 15, 4)
    first_slope[...] = slope.reshape(15, 4, 16, 64)

    loads[1].wait()
    pre = jnp.zeros((224, 128), F32)
    for p in range(3):
        for q in range(3):
            pre = pre + dot(tap_of(first, p, q, 7, 2), w2_ref[3 * p + q])
    value, slope = activate(pre)
    store_map(second, value.reshape(7, 2, 16, 128), 7, 2)
    second_slope[...] = slope.reshape(7, 2, 16, 128)

    loads[2].wait()
    pre = jnp.zeros((48, 256), F32)
    for p in range(3):
        for q in range(3):
            pre = pre + dot(tap_of(second, p, q, 3, 1), w3_ref[3 * p + q])
    value, slope = activate(pre)
    third[...] = jnp.zeros((3, 2, 32, 128), F32)
    for r in range(3):
        for h in range(2):
            third[r, h, 0:16, :] = value[16 * r : 16 * r + 16, 128 * h : 128 * h + 128]
    third_slope[...] = slope.reshape(3, 16, 256)

    loads[3].wait()
    place = lax.broadcasted_iota(jnp.int32, (16, 256), 0)
    cells = []
    pre = jnp.zeros((16, 512), F32)
    for p in range(3):
        even = every_second(third, p, 0)
        odd = every_second(third, p, 1)
        left = jnp.where((place > 0) & (place < 8), pltpu.roll(odd, 1, 0), 0.0)
        for q, block in enumerate((left, even, odd)):
            block = block.astype(BF)
            cells.append(block)
            pre = pre + dot(block, w4_ref[3 * p + q])
    value, slope = activate(pre)
    fourth = value.astype(BF).astype(F32)
    head = head_ref[...].astype(F32).reshape(1, 512)
    logits = jnp.sum(fourth * head, axis=1, keepdims=True)
    cell = lax.broadcasted_iota(jnp.int32, (16, 8), 0)
    lane = lax.broadcasted_iota(jnp.int32, (16, 8), 1)
    labels = jnp.broadcast_to(labels_ref[...].astype(F32), (16, 8))
    labels = jnp.sum(jnp.where(cell == lane, labels, 0.0), axis=1, keepdims=True)
    logit_grad = (jax.nn.sigmoid(logits) - labels) / 32.0
    logit_grad = jnp.where(lax.broadcasted_iota(jnp.int32, (16, 1), 0) < 8, logit_grad, 0.0)
    delta = (logit_grad * head * slope).astype(BF)

    for t in range(9):
        grad = dot_tn(cells[t], delta).astype(BF)
        for lane in range(4):
            at = (lane // 2) * HALF + DEEPEST_AT + 32 * t + 16 * (lane % 2)
            grads_ref[at : at + 16] = grad[:, 128 * lane : 128 * lane + 128].reshape(16, 16, 128)
        if t == 2:
            reducing.begin(0)
        if t == 6:
            reducing.begin(1)
    head_grad = jnp.sum(fourth * logit_grad, axis=0, keepdims=True)
    row = lax.broadcasted_iota(jnp.int32, (16, 128), 0)
    head_tile = jnp.zeros((16, 128), F32)
    for lane in range(4):
        part = jnp.broadcast_to(head_grad[:, 128 * lane : 128 * lane + 128], (16, 128))
        head_tile = jnp.where(row == lane, part, head_tile)
    grads_ref[HALF + HEAD_AT] = head_tile.astype(BF)
    for p in range(3):
        parts = [dot_nt(delta, w4_ref[3 * p + q]) for q in range(3)]
        odd = parts[2] + pltpu.roll(parts[0], 15, 0)
        for h in range(2):
            lanes = slice(128 * h, 128 * h + 128)
            third_dx[p, h, pl.ds(0, 16, stride=2), :] = parts[1][:, lanes]
            third_dx[p, h, pl.ds(1, 16, stride=2), :] = odd[:, lanes]
    delta = jnp.concatenate(
        [
            jnp.concatenate([third_dx[r, h, 0:16, :] for h in range(2)], axis=1) * third_slope[r]
            for r in range(3)
        ],
        axis=0,
    ).astype(BF)

    reducing.advance(0)

    for t in range(9):
        grad = dot_tn(tap_of(second, t // 3, t % 3, 3, 1), delta).astype(BF)
        for half in range(2):
            at = half * HALF + DEEPER_AT + 8 * t
            grads_ref[at : at + 8] = grad[:, 128 * half : 128 * half + 128].reshape(8, 16, 128)
    reducing.begin(2)
    reducing.advance(1)
    dx = map_grad(delta, w3_ref, 3, 1)
    delta = jnp.concatenate(
        [dx[(r, m)] * second_slope[r, m] for r in range(7) for m in range(2)], axis=0
    ).astype(BF)
    reducing.advance(0)

    for t in range(9):
        grad = dot_tn(tap_of(first, t // 3, t % 3, 7, 2), delta).astype(BF).reshape(4, 16, 128)
        for half in range(2):
            at = half * HALF + MIDDLE_AT + 2 * t
            grads_ref[at : at + 2] = grad[2 * half : 2 * half + 2]
    reducing.advance(2)
    dx = map_grad(delta, w2_ref, 7, 2)
    for r in range(15):
        for m in range(4):
            at = 64 * r + 16 * m
            first_delta[at : at + 16, :] = dx[(r, m)] * first_slope[r, m]
    first_delta[960:1024, :] = jnp.zeros((64, 64), F32)
    reducing.advance(0)
    reducing.advance(1)

    turned = jnp.transpose(first_delta[...]).astype(BF)
    for t in range(9):
        grad = dot(turned, tap_of(lifted, t // 3, t % 3, 16, 4))
        grad = jnp.transpose(grad)
        grad = jnp.concatenate([grad[0:80], grad[80:160]], axis=1).astype(BF)
        at = TEMPORAL_AT + 5 * t if t < 5 else HALF + TEMPORAL_AT + 5 * (t - 5)
        grads_ref[at : at + 5] = grad.reshape(5, 16, 128)
        if t == 4:
            reducing.advance(0)
            reducing.advance(2)
    reducing.begin(3)
    reducing.begin(4)
    reducing.finish()
    halo.wait_send()


def step(occ, labels, lift, w1, w2, w3, w4, head):
    hbm = pl.BlockSpec(memory_space=pl.ANY)
    return pl.pallas_call(
        step_kernel,
        out_shape=jax.ShapeDtypeStruct((TILES, 16, 128), BF),
        in_specs=[vmem()] * 3 + [hbm] * 4 + [vmem()],
        out_specs=vmem(),
        scratch_shapes=[
            pltpu.VMEM(w1.shape, BF),
            pltpu.VMEM(w2.shape, BF),
            pltpu.VMEM(w3.shape, BF),
            pltpu.VMEM(w4.shape, BF),
            pltpu.SemaphoreType.DMA((4,)),
            pltpu.VMEM((5, 16, 128), jnp.int32),
            pltpu.SemaphoreType.DMA((2,)),
            pltpu.VMEM((TILES, 16, 128), BF),
            pltpu.VMEM((16, 32), F32),
            pltpu.VMEM((17, 2, 5, 2, 16, 160), BF),
            pltpu.VMEM((8, 2, 3, 2, 16, 64), BF),
            pltpu.VMEM((15, 4, 16, 64), F32),
            pltpu.VMEM((4, 2, 2, 2, 16, 128), BF),
            pltpu.VMEM((7, 2, 16, 128), F32),
            pltpu.VMEM((3, 2, 32, 128), F32),
            pltpu.VMEM((3, 16, 256), F32),
            pltpu.VMEM((3, 2, 32, 128), F32),
            pltpu.VMEM((1024, 64), F32),
        ]
        + reduce_scratch(),
        compiler_params=pltpu.CompilerParams(
            collective_id=0, has_side_effects=True, vmem_limit_bytes=67043328
        ),
    )(occ, labels, lift, w1, w2, w3, w4, head)


def position():
    dp = lax.axis_index("dp")
    space = lax.axis_index("space")
    return {
        "x": space // 2,
        "y": lax.rem(space, 2) * 2 + lax.rem(dp // 2, 2),
        "z": dp // 4,
        "core": lax.rem(dp, 2),
    }


def device_at(place):
    dp = place["z"] * 4 + lax.rem(place["y"], 2) * 2 + place["core"]
    space = place["x"] * 2 + place["y"] // 2
    return (dp, space)


def along(here, axis, distance):
    there = dict(here)
    size = SIZE[axis]
    there[axis] = lax.rem(here[axis] + distance + size, size)
    return there


class Wires:
    def __init__(self, send_sem, recv_sem):
        self.send_sem, self.recv_sem = send_sem, recv_sem
        self.used = 0
        self.sent = []

    def send(self, src, dst, place):
        copy = pltpu.make_async_remote_copy(
            src_ref=src,
            dst_ref=dst,
            send_sem=self.send_sem.at[self.used],
            recv_sem=self.recv_sem.at[self.used],
            device_id=device_at(place),
            device_id_type=MESH,
        )
        self.used += 1
        copy.start()
        self.sent.append(copy)
        return copy

    def finish(self):
        for copy in self.sent:
            copy.wait_send()


def greet(here, others):
    partner = dict(here)
    partner["core"] = 1 - here["core"]
    barrier = pltpu.get_barrier_semaphore()
    peers = [device_at(partner)] + others
    for axis, size in SIZE.items():
        peers += [device_at(along(here, axis, d)) for d in range(1, size)]
    for peer in peers:
        pl.semaphore_signal(barrier, inc=1, device_id=peer, device_id_type=MESH)
    pl.semaphore_wait(barrier, len(peers))


def f32(block):
    return block.astype(F32)


def relayed_scatter(wires, here, axis, parts, right_in, left_in, right_out, left_out, m):
    n = SIZE[axis]
    half, h = n // 2, m // 2
    me = here[axis]
    right, left = along(here, axis, 1), along(here, axis, -1)

    def chunk(distance):
        return lax.rem(me + distance + n, n)

    lo, hi = pl.ds(0, h), pl.ds(h, m - h)
    far = chunk(half)
    from_left = [wires.send(parts.at[far, lo], right_in.at[0, lo], right)]
    from_right = [wires.send(parts.at[far, hi], left_in.at[0, hi], left)]
    early_left = wires.send(parts.at[chunk(half - 1), hi], right_in.at[1, hi], right)
    early_right = wires.send(parts.at[chunk(1 - half), lo], left_in.at[1, lo], left)
    for s in range(1, half):
        yield
        to_right, to_left = chunk(half - s), chunk(s - half)
        if s == 1:
            from_left[-1].wait_recv()
            right_out[0, 0:h] = (f32(parts[to_right, 0:h]) + f32(right_in[0, 0:h])).astype(BF)
            from_left.append(wires.send(right_out.at[0, lo], right_in.at[1, lo], right))
            from_right[-1].wait_recv()
            left_out[0, h:m] = (f32(parts[to_left, h:m]) + f32(left_in[0, h:m])).astype(BF)
            from_right.append(wires.send(left_out.at[0, hi], left_in.at[1, hi], left))
        else:
            if s == 2:
                early_left.wait_recv()
                early_right.wait_recv()
            from_left[-1].wait_recv()
            right_out[s - 1] = (f32(parts[to_right]) + f32(right_in[s - 1])).astype(BF)
            from_left.append(wires.send(right_out.at[s - 1], right_in.at[s], right))
            from_right[-1].wait_recv()
            left_out[s - 1] = (f32(parts[to_left]) + f32(left_in[s - 1])).astype(BF)
            from_right.append(wires.send(left_out.at[s - 1], left_in.at[s], left))
    yield
    if half == 2:
        early_left.wait_recv()
        early_right.wait_recv()
    from_left[-1].wait_recv()
    from_right[-1].wait_recv()
    return f32(parts[me]) + f32(right_in[half - 1]) + f32(left_in[half - 1])


def relayed_gather(wires, here, axis, total_ref, base, m, partner):
    n = SIZE[axis]
    half, h = n // 2, m // 2
    me = here[axis]
    right, left = along(here, axis, 1), along(here, axis, -1)
    swapped = []

    def piece(distance, at, size):
        k = lax.rem(me + distance + n, n)
        return total_ref.at[pl.ds(base + k * m + at, size)]

    def swap(where):
        swapped.append(wires.send(where, where, partner))

    own = piece(0, 0, m)
    from_left = wires.send(own, own, right)
    from_right = wires.send(own, own, left)
    swap(own)
    for s in range(1, half):
        yield
        from_left.wait_recv()
        at, size = (0, h) if s == half - 1 else (0, m)
        here_now = piece(-s, at, size)
        from_left = wires.send(here_now, here_now, right)
        swap(piece(-s, 0, m))
        from_right.wait_recv()
        at, size = (h, m - h) if s == half - 1 else (0, m)
        here_now = piece(s, at, size)
        from_right = wires.send(here_now, here_now, left)
        swap(piece(s, 0, m))
    yield
    from_left.wait_recv()
    swap(piece(-half, 0, h))
    from_right.wait_recv()
    swap(piece(half, h, m - h))
    yield
    for copy in swapped:
        copy.wait_recv()


def direct_scatter(wires, here, axis, parts, landed):
    n = SIZE[axis]
    flights = []
    for d in range(1, n):
        there = along(here, axis, d)
        flights.append(wires.send(parts.at[there[axis]], landed.at[d - 1], there))
    yield
    for copy in flights:
        copy.wait_recv()
    total = f32(parts[here[axis]])
    for d in range(1, n):
        total = total + f32(landed[d - 1])
    return total


def direct_gather(wires, here, axis, total_ref, base, m):
    n = SIZE[axis]
    own = total_ref.at[pl.ds(base + here[axis] * m, m)]
    flights = [wires.send(own, own, along(here, axis, d)) for d in range(1, n)]
    yield
    for copy in flights:
        copy.wait_recv()


def direct_exchange(wires, here, axis, own, landed):
    n = SIZE[axis]
    me = here[axis]
    flights = []
    for d in range(1, n):
        flights.append(wires.send(own, landed.at[d - 1], along(here, axis, d)))
    yield
    for copy in flights:
        copy.wait_recv()
    total = jnp.zeros(own.shape, F32)
    for k in range(n):
        back = lax.rem(me - k + n, n)
        other = f32(landed[lax.rem(back + n - 1, n)])
        total = total + jnp.where(back == 0, f32(own[...]), other)
    return total


def part_scratch(order, split, kept):
    a, b, c = shares(order, split)
    m = b * c * kept
    return [
        pltpu.VMEM((a, m, 16, 128), BF),
        pltpu.VMEM((a // 2, m, 16, 128), BF),
        pltpu.VMEM((a // 2, m, 16, 128), BF),
        pltpu.VMEM((a // 2, m, 16, 128), BF),
        pltpu.VMEM((a // 2, m, 16, 128), BF),
        pltpu.VMEM((b, c * kept, 16, 128), BF),
        pltpu.VMEM((b - 1, c * kept, 16, 128), BF),
        pltpu.VMEM((c, kept, 16, 128), BF),
        pltpu.VMEM((SIZE[order[2]], kept, 16, 128), BF),
    ]


def reduce_part(wires, here, partner, grads_ref, total_ref, paired, scratch, start, part):
    shared, right_in, left_in, right_out, left_out, sum1, landed2, sum2, landed3 = scratch
    order, split, kept = part
    a, b, c = shares(order, split)
    m = b * c * kept
    core = here["core"]
    there = pl.ds((1 - core) * HALF + start, a * m)
    flight = wires.send(grads_ref.at[there], paired.at[pl.ds(start, a * m)], partner)
    yield
    flight.wait_recv()
    both = f32(grads_ref[pl.ds(core * HALF + start, a * m)]) + f32(paired[start : start + a * m])
    shared[...] = both.astype(BF).reshape(a, m, 16, 128)
    total = yield from relayed_scatter(
        wires, here, order[0], shared, right_in, left_in, right_out, left_out, m
    )
    sum1[...] = total.astype(BF).reshape(b, c * kept, 16, 128)
    total = yield from direct_scatter(wires, here, order[1], sum1, landed2)
    sum2[...] = total.astype(BF).reshape(c, kept, 16, 128)
    if split:
        total = yield from direct_scatter(wires, here, order[2], sum2, landed3)
    else:
        total = yield from direct_exchange(wires, here, order[2], sum2.at[0], landed3)
    base0 = core * HALF + start
    base1 = base0 + here[order[0]] * m
    base2 = base1 + here[order[1]] * (c * kept)
    if split:
        total_ref[pl.ds(base2 + here[order[2]] * kept, kept)] = total.astype(BF)
        yield from direct_gather(wires, here, order[2], total_ref, base2, kept)
    else:
        total_ref[pl.ds(base2, kept)] = total.astype(BF)
    yield from direct_gather(wires, here, order[1], total_ref, base1, c * kept)
    yield from relayed_gather(wires, here, order[0], total_ref, base0, m, partner)


def interleave(programs):
    programs = list(programs)
    while programs:
        still = []
        for program in programs:
            try:
                next(program)
                still.append(program)
            except StopIteration:
                pass
        programs = still


class Reduction:
    def __init__(self, here, grads_ref, total_ref, scratch):
        paired, send_sem, recv_sem, *rest = scratch
        partner = dict(here)
        partner["core"] = 1 - here["core"]
        self.wires = Wires(send_sem, recv_sem)
        self.programs = []
        for i, part in enumerate(PARTS):
            own = rest[9 * i : 9 * i + 9]
            self.programs.append(
                reduce_part(
                    self.wires, here, partner, grads_ref, total_ref, paired, own, STARTS[i], part
                )
            )

    def begin(self, i):
        next(self.programs[i])

    advance = begin

    def finish(self):
        interleave(self.programs)
        self.wires.finish()


def reduce_scratch():
    scratch = [
        pltpu.VMEM((HALF, 16, 128), BF),
        pltpu.SemaphoreType.DMA((192,)),
        pltpu.SemaphoreType.DMA((192,)),
    ]
    for order, split, kept in PARTS:
        scratch += part_scratch(order, split, kept)
    return scratch


def unpack_kernel(total_hbm, g1, g2, g3, g4, gh, total_ref, s1, s2, s3, s4, load_sem, sem):
    spans = [(32 * t, 32) for t in range(9)] + [(DEEPER_AT, HALF - DEEPER_AT)]
    loads = []
    for i, (at, size) in enumerate(spans):
        for half in range(2):
            where = pl.ds(half * HALF + at, size)
            load = pltpu.make_async_copy(
                total_hbm.at[where], total_ref.at[where], load_sem.at[2 * i + half]
            )
            load.start()
            loads.append(load)
    copies = []

    def out(source, target):
        copy = pltpu.make_async_copy(source, target, sem.at[len(copies)])
        copy.start()
        copies.append(copy)

    for t in range(9):
        loads[2 * t].wait()
        loads[2 * t + 1].wait()
        for lane in range(4):
            at = (lane // 2) * HALF + DEEPEST_AT + 32 * t + 16 * (lane % 2)
            s4[t, :, 128 * lane : 128 * lane + 128] = f32(
                total_ref[at : at + 16].reshape(256, 128)
            )
        out(s4.at[t], g4.at[t])
    loads[18].wait()
    loads[19].wait()
    for t in range(9):
        for half in range(2):
            at = half * HALF + DEEPER_AT + 8 * t
            s3[t, :, 128 * half : 128 * half + 128] = f32(
                total_ref[at : at + 8].reshape(128, 128)
            )
    out(s3, g3)
    for t in range(9):
        for half in range(2):
            at = half * HALF + MIDDLE_AT + 2 * t
            s2[t, 32 * half : 32 * half + 32, :] = f32(total_ref[at : at + 2].reshape(32, 128))
        at = TEMPORAL_AT + 5 * t if t < 5 else HALF + TEMPORAL_AT + 5 * (t - 5)
        block = f32(total_ref[at : at + 5].reshape(80, 128))
        s1[t, 0:80, :] = block[:, 0:64]
        s1[t, 80:160, :] = block[:, 64:128]
    out(s2, g2)
    out(s1, g1)
    tile = f32(total_ref[HALF + HEAD_AT])
    for lane in range(4):
        gh[pl.ds(128 * lane, 128)] = tile[lane]
    for copy in copies:
        copy.wait()


def unpack(total):
    shapes = ((9, 160, 64), (9, 64, 128), (9, 128, 256), (9, 256, 512))
    hbm = pl.BlockSpec(memory_space=pl.ANY)
    return pl.pallas_call(
        unpack_kernel,
        out_shape=[jax.ShapeDtypeStruct(shape, F32) for shape in shapes + ((512,),)],
        in_specs=[hbm],
        out_specs=[hbm] * 4 + [vmem()],
        scratch_shapes=[pltpu.VMEM((TILES, 16, 128), BF)]
        + [pltpu.VMEM(shape, F32) for shape in shapes]
        + [pltpu.SemaphoreType.DMA((20,)), pltpu.SemaphoreType.DMA((12,))],
        compiler_params=pltpu.CompilerParams(vmem_limit_bytes=67043328),
    )(total)


def local(
    occupancy,
    state_labels,
    lift_weight,
    temporal_weight,
    middle_weight,
    deeper_weight,
    deepest_weight,
    head_weight,
):
    total = step(
        occupancy[0],
        state_labels[0],
        lift_weight,
        temporal_weight.reshape(9, 160, 64),
        middle_weight.reshape(9, 64, 128),
        deeper_weight.reshape(9, 128, 256),
        deepest_weight.reshape(9, 256, 512),
        head_weight,
    )
    g1, g2, g3, g4, gh = unpack(total)
    return (
        g1.reshape(3, 3, 5, 32, 64),
        g2.reshape(3, 3, 64, 128),
        g3.reshape(3, 3, 128, 256),
        g4.reshape(3, 3, 256, 512),
        gh,
    )


def solution(mesh):
    return jax.shard_map(
        local,
        mesh=mesh,
        in_specs=(
            P("dp", None, "space", None),
            P("dp", "space", None),
            P(),
            P(),
            P(),
            P(),
            P(),
            P(),
        ),
        out_specs=(P(), P(), P(), P(), P()),
        check_vma=False,
    )
```

```python
import math

import jax
import jax.numpy as jnp
from jax import lax
from jax.experimental import pallas as pl
from jax.experimental.pallas import tpu as pltpu
from jax.sharding import PartitionSpec as P

BF = jnp.bfloat16
F32 = jnp.float32
MESH = pl.DeviceIdType.MESH

NX, NY, NZ = 4, 4, 8
SIZE = {"x": NX, "y": NY, "z": NZ}
DEEPEST_AT, DEEPER_AT, MIDDLE_AT, TEMPORAL_AT = 0, 288, 360, 378
HEAD_AT, HALF_ENDS = 398, (403, 399)
PARTS = (
    (("z", "x", "y"), False, 2),
    (("x", "y", "z"), True, 1),
    (("y", "x", "z"), True, 1),
    (("x", "y", "z"), False, 3),
    (("y", "x", "z"), False, 3),
)


def shares(order, split):
    return SIZE[order[0]], SIZE[order[1]], SIZE[order[2]] if split else 1


LENGTHS = tuple(math.prod(shares(order, split)) * kept for order, split, kept in PARTS)
STARTS = tuple(sum(LENGTHS[:i]) for i in range(len(PARTS)))
HALF = sum(LENGTHS)
TILES = 2 * HALF


def vmem():
    return pl.BlockSpec(memory_space=pltpu.VMEM)


def dot(a, b):
    return lax.dot_general(a, b, (((1,), (0,)), ((), ())), preferred_element_type=F32)


def dot_nt(a, b):
    return lax.dot_general(a, b, (((1,), (1,)), ((), ())), preferred_element_type=F32)


def dot_tn(a, b):
    return lax.dot_general(a, b, (((0,), (0,)), ((), ())), preferred_element_type=F32)


def activate(pre):
    gate = jax.nn.sigmoid(pre)
    slope = gate * (1.0 + pre * (1.0 - gate))
    return pre * gate, slope


def later(block):
    rolled = pltpu.roll(block, 1, block.ndim - 2)
    index = lax.broadcasted_iota(jnp.int32, block.shape, block.ndim - 2)
    return jnp.where(index == 0, 0.0, rolled)


def sooner(block):
    size = block.shape[-2]
    rolled = pltpu.roll(block, size - 1, block.ndim - 2)
    index = lax.broadcasted_iota(jnp.int32, block.shape, block.ndim - 2)
    return jnp.where(index == size - 1, 0.0, rolled)


def tap_of(ref, p, q, rows, phases, start=0):
    a, b = start + p // 2, p % 2
    c, d = q // 2, q % 2
    block = ref[a : a + rows, b, c : c + phases, d]
    return block.reshape(rows * phases * block.shape[2], block.shape[3])


def store_map(ref, value, rows, phases, start=0):
    shifted = later(value[:, phases - 1])
    value = {start + r: value[r] for r in range(rows)}
    shifted = {start + r: shifted[r] for r in range(rows)}
    for r in range(start, start + rows):
        ref[r // 2, r % 2, 0, 0] = shifted[r].astype(BF)
        for m in range(phases):
            s = m + 1
            ref[r // 2, r % 2, s // 2, s % 2] = value[r][m].astype(BF)


def map_grad(delta, weight_ref, rows, phases):
    out = {}

    def put(r, m, value):
        out[(r, m)] = value if (r, m) not in out else out[(r, m)] + value

    for p in range(3):
        for q in range(3):
            part = dot_nt(delta, weight_ref[3 * p + q])
            part = part.reshape(rows, phases, 16, part.shape[1])
            for m in range(phases):
                s = 2 * m + q - 1
                for o in range(rows):
                    value = part[o, m]
                    if s < 0:
                        put(2 * o + p, 2 * phases - 1, sooner(value))
                    else:
                        put(2 * o + p, s, value)
    return out


def every_second(ref, r, start):
    halves = [ref[r, h, pl.ds(start, 16, stride=2), :] for h in range(2)]
    return jnp.concatenate(halves, axis=1)


def lift_row(order, shifts, lift, source, row, keep, lifted, r):
    frames = []
    for t in range(5):
        line = source[t, row : row + 1, :]
        if keep is not None:
            line = line * keep
        bits = jnp.bitwise_and(jnp.right_shift(jnp.broadcast_to(line, (16, 128)), shifts), 1)
        frames.append(bits.astype(F32).astype(BF))
    turned = dot_nt(order, jnp.concatenate(frames, axis=0)).astype(BF)
    value = jnp.maximum(dot(turned, lift), 0.0).reshape(8, 16, 160)
    lifted[r // 2, r % 2, 0, 0] = later(value[7]).astype(BF)
    for m in range(8):
        s = m + 1
        lifted[r // 2, r % 2, s // 2, s % 2] = value[m].astype(BF)


def step_kernel(
    occ_ref,
    labels_ref,
    lift_ref,
    w1_hbm,
    w2_hbm,
    w3_hbm,
    w4_hbm,
    head_ref,
    total_ref,
    w1_ref,
    w2_ref,
    w3_ref,
    w4_ref,
    weight_sem,
    landed,
    halo_sem,
    grads_ref,
    lift_pad,
    lifted,
    first,
    first_slope,
    second,
    second_slope,
    third,
    third_slope,
    third_dx,
    first_delta,
    *reduce_scratch,
):
    loads = [
        pltpu.make_async_copy(source, target, weight_sem.at[i])
        for i, (source, target) in enumerate(
            ((w1_hbm, w1_ref), (w2_hbm, w2_ref), (w3_hbm, w3_ref), (w4_hbm, w4_ref))
        )
    ]
    for load in loads:
        load.start()
    here = position()
    space = lax.axis_index("space")
    below = lax.rem(space + 1, 8)
    above = lax.rem(space + 7, 8)
    dp = lax.axis_index("dp")
    greet(here, [(dp, below), (dp, above)])
    halo = pltpu.make_async_remote_copy(
        src_ref=occ_ref,
        dst_ref=landed,
        send_sem=halo_sem.at[0],
        recv_sem=halo_sem.at[1],
        device_id=(dp, below),
        device_id_type=MESH,
    )
    halo.start()
    reducing = Reduction(here, grads_ref, total_ref, reduce_scratch)

    to = lax.broadcasted_iota(jnp.int32, (128, 128), 0)
    come = lax.broadcasted_iota(jnp.int32, (128, 128), 1)
    order = jnp.where(come == lax.rem(to, 16) * 8 + to // 16, 1.0, 0.0).astype(BF)
    shifts = lax.broadcasted_iota(jnp.int32, (16, 128), 0)
    lift_pad[...] = jnp.zeros((16, 32), F32)
    lift_pad[0:13, :] = lift_ref[...].astype(F32)
    wide = jnp.concatenate([lift_pad[...]] * 5, axis=1)
    frame_of = lax.broadcasted_iota(jnp.int32, (16, 160), 1) // 32
    lift = jnp.concatenate([jnp.where(frame_of == t, wide, 0.0) for t in range(5)], axis=0)
    lift = lift.astype(BF)
    zero_row = jnp.zeros((5, 2, 16, 160), BF)
    lifted[15, 1] = zero_row
    lifted[16, 0] = zero_row
    lifted[16, 1] = zero_row
    for half in range(2):
        grads_ref[half * HALF + HALF_ENDS[half] : half * HALF + HALF] = jnp.zeros(
            (HALF - HALF_ENDS[half], 16, 128), BF
        )
    for row in range(16):
        lift_row(order, shifts, lift, occ_ref, row, None, lifted, row + 15)
    loads[0].wait()

    def first_rows(start, rows):
        pre = jnp.zeros((64 * rows, 64), F32)
        for p in range(3):
            for q in range(3):
                pre = pre + dot(tap_of(lifted, p, q, rows, 4, start), w1_ref[3 * p + q])
        value, slope = activate(pre)
        store_map(first, value.reshape(rows, 4, 16, 64), rows, 4, start)
        first_slope[start : start + rows] = slope.reshape(rows, 4, 16, 64)

    first_rows(8, 7)
    halo.wait_recv()
    keep = jnp.where(space == 0, 0, 1)
    for row in range(1, 16):
        lift_row(order, shifts, lift, landed, row, keep, lifted, row - 1)
    first_rows(0, 8)

    loads[1].wait()
    pre = jnp.zeros((224, 128), F32)
    for p in range(3):
        for q in range(3):
            pre = pre + dot(tap_of(first, p, q, 7, 2), w2_ref[3 * p + q])
    value, slope = activate(pre)
    store_map(second, value.reshape(7, 2, 16, 128), 7, 2)
    second_slope[...] = slope.reshape(7, 2, 16, 128)

    loads[2].wait()
    pre = jnp.zeros((48, 256), F32)
    for p in range(3):
        for q in range(3):
            pre = pre + dot(tap_of(second, p, q, 3, 1), w3_ref[3 * p + q])
    value, slope = activate(pre)
    third[...] = jnp.zeros((3, 2, 32, 128), F32)
    for r in range(3):
        for h in range(2):
            third[r, h, 0:16, :] = value[16 * r : 16 * r + 16, 128 * h : 128 * h + 128]
    third_slope[...] = slope.reshape(3, 16, 256)

    loads[3].wait()
    place = lax.broadcasted_iota(jnp.int32, (16, 256), 0)
    cells = []
    pre = jnp.zeros((16, 512), F32)
    for p in range(3):
        even = every_second(third, p, 0)
        odd = every_second(third, p, 1)
        left = jnp.where((place > 0) & (place < 8), pltpu.roll(odd, 1, 0), 0.0)
        for q, block in enumerate((left, even, odd)):
            block = block.astype(BF)
            cells.append(block)
            pre = pre + dot(block, w4_ref[3 * p + q])
    value, slope = activate(pre)
    fourth = value.astype(BF).astype(F32)
    head = head_ref[...].astype(F32).reshape(1, 512)
    logits = jnp.sum(fourth * head, axis=1, keepdims=True)
    cell = lax.broadcasted_iota(jnp.int32, (16, 8), 0)
    lane = lax.broadcasted_iota(jnp.int32, (16, 8), 1)
    labels = jnp.broadcast_to(labels_ref[...].astype(F32), (16, 8))
    labels = jnp.sum(jnp.where(cell == lane, labels, 0.0), axis=1, keepdims=True)
    logit_grad = (jax.nn.sigmoid(logits) - labels) / 32.0
    logit_grad = jnp.where(lax.broadcasted_iota(jnp.int32, (16, 1), 0) < 8, logit_grad, 0.0)
    delta = (logit_grad * head * slope).astype(BF)

    for t in range(9):
        grad = dot_tn(cells[t], delta).astype(BF)
        for lane in range(4):
            at = (lane // 2) * HALF + DEEPEST_AT + 32 * t + 16 * (lane % 2)
            grads_ref[at : at + 16] = grad[:, 128 * lane : 128 * lane + 128].reshape(16, 16, 128)
        if t == 1:
            reducing.begin(0)
        if t == 5:
            reducing.begin(1)
    head_grad = jnp.sum(fourth * logit_grad, axis=0, keepdims=True)
    row = lax.broadcasted_iota(jnp.int32, (16, 128), 0)
    head_tile = jnp.zeros((16, 128), F32)
    for lane in range(4):
        part = jnp.broadcast_to(head_grad[:, 128 * lane : 128 * lane + 128], (16, 128))
        head_tile = jnp.where(row == lane, part, head_tile)
    grads_ref[HALF + HEAD_AT] = head_tile.astype(BF)
    for p in range(3):
        parts = [dot_nt(delta, w4_ref[3 * p + q]) for q in range(3)]
        odd = parts[2] + pltpu.roll(parts[0], 15, 0)
        for h in range(2):
            lanes = slice(128 * h, 128 * h + 128)
            third_dx[p, h, pl.ds(0, 16, stride=2), :] = parts[1][:, lanes]
            third_dx[p, h, pl.ds(1, 16, stride=2), :] = odd[:, lanes]
    delta = jnp.concatenate(
        [
            jnp.concatenate([third_dx[r, h, 0:16, :] for h in range(2)], axis=1) * third_slope[r]
            for r in range(3)
        ],
        axis=0,
    ).astype(BF)

    reducing.advance(0)

    for t in range(9):
        grad = dot_tn(tap_of(second, t // 3, t % 3, 3, 1), delta).astype(BF)
        for half in range(2):
            at = half * HALF + DEEPER_AT + 8 * t
            grads_ref[at : at + 8] = grad[:, 128 * half : 128 * half + 128].reshape(8, 16, 128)
    reducing.begin(2)
    reducing.advance(1)
    dx = map_grad(delta, w3_ref, 3, 1)
    delta = jnp.concatenate(
        [dx[(r, m)] * second_slope[r, m] for r in range(7) for m in range(2)], axis=0
    ).astype(BF)

    for t in range(9):
        grad = dot_tn(tap_of(first, t // 3, t % 3, 7, 2), delta).astype(BF).reshape(4, 16, 128)
        for half in range(2):
            at = half * HALF + MIDDLE_AT + 2 * t
            grads_ref[at : at + 2] = grad[2 * half : 2 * half + 2]
    reducing.advance(2)
    dx = map_grad(delta, w2_ref, 7, 2)
    for r in range(15):
        for m in range(4):
            at = 64 * r + 16 * m
            first_delta[at : at + 16, :] = dx[(r, m)] * first_slope[r, m]
    first_delta[960:1024, :] = jnp.zeros((64, 64), F32)

    turned = jnp.transpose(first_delta[...]).astype(BF)
    for t in range(9):
        grad = dot(turned, tap_of(lifted, t // 3, t % 3, 16, 4))
        grad = jnp.transpose(grad)
        grad = jnp.concatenate([grad[0:80], grad[80:160]], axis=1).astype(BF)
        at = TEMPORAL_AT + 5 * t if t < 5 else HALF + TEMPORAL_AT + 5 * (t - 5)
        grads_ref[at : at + 5] = grad.reshape(5, 16, 128)
    reducing.begin(3)
    reducing.begin(4)
    reducing.finish()
    halo.wait_send()


def step(occ, labels, lift, w1, w2, w3, w4, head):
    hbm = pl.BlockSpec(memory_space=pl.ANY)
    return pl.pallas_call(
        step_kernel,
        out_shape=jax.ShapeDtypeStruct((TILES, 16, 128), BF),
        in_specs=[vmem()] * 3 + [hbm] * 4 + [vmem()],
        out_specs=vmem(),
        scratch_shapes=[
            pltpu.VMEM(w1.shape, BF),
            pltpu.VMEM(w2.shape, BF),
            pltpu.VMEM(w3.shape, BF),
            pltpu.VMEM(w4.shape, BF),
            pltpu.SemaphoreType.DMA((4,)),
            pltpu.VMEM((5, 16, 128), jnp.int32),
            pltpu.SemaphoreType.DMA((2,)),
            pltpu.VMEM((TILES, 16, 128), BF),
            pltpu.VMEM((16, 32), F32),
            pltpu.VMEM((17, 2, 5, 2, 16, 160), BF),
            pltpu.VMEM((8, 2, 3, 2, 16, 64), BF),
            pltpu.VMEM((15, 4, 16, 64), F32),
            pltpu.VMEM((4, 2, 2, 2, 16, 128), BF),
            pltpu.VMEM((7, 2, 16, 128), F32),
            pltpu.VMEM((3, 2, 32, 128), F32),
            pltpu.VMEM((3, 16, 256), F32),
            pltpu.VMEM((3, 2, 32, 128), F32),
            pltpu.VMEM((1024, 64), F32),
        ]
        + reduce_scratch(),
        compiler_params=pltpu.CompilerParams(
            collective_id=0, has_side_effects=True, vmem_limit_bytes=67043328
        ),
    )(occ, labels, lift, w1, w2, w3, w4, head)


def position():
    dp = lax.axis_index("dp")
    space = lax.axis_index("space")
    return {
        "x": space // 2,
        "y": lax.rem(space, 2) * 2 + lax.rem(dp // 2, 2),
        "z": dp // 4,
        "core": lax.rem(dp, 2),
    }


def device_at(place):
    dp = place["z"] * 4 + lax.rem(place["y"], 2) * 2 + place["core"]
    space = place["x"] * 2 + place["y"] // 2
    return (dp, space)


def along(here, axis, distance):
    there = dict(here)
    size = SIZE[axis]
    there[axis] = lax.rem(here[axis] + distance + size, size)
    return there


class Wires:
    def __init__(self, send_sem, recv_sem):
        self.send_sem, self.recv_sem = send_sem, recv_sem
        self.used = 0
        self.sent = []

    def send(self, src, dst, place):
        copy = pltpu.make_async_remote_copy(
            src_ref=src,
            dst_ref=dst,
            send_sem=self.send_sem.at[self.used],
            recv_sem=self.recv_sem.at[self.used],
            device_id=device_at(place),
            device_id_type=MESH,
        )
        self.used += 1
        copy.start()
        self.sent.append(copy)
        return copy

    def finish(self):
        for copy in self.sent:
            copy.wait_send()


def greet(here, others):
    partner = dict(here)
    partner["core"] = 1 - here["core"]
    barrier = pltpu.get_barrier_semaphore()
    peers = [device_at(partner)] + others
    for axis, size in SIZE.items():
        peers += [device_at(along(here, axis, d)) for d in range(1, size)]
    for peer in peers:
        pl.semaphore_signal(barrier, inc=1, device_id=peer, device_id_type=MESH)
    pl.semaphore_wait(barrier, len(peers))


def f32(block):
    return block.astype(F32)


def direct_scatter(wires, here, axis, parts, landed):
    n = SIZE[axis]
    flights = []
    for d in range(1, n):
        there = along(here, axis, d)
        flights.append(wires.send(parts.at[there[axis]], landed.at[d - 1], there))
    yield
    for copy in flights:
        copy.wait_recv()
    total = f32(parts[here[axis]])
    for d in range(1, n):
        total = total + f32(landed[d - 1])
    return total


def direct_gather(wires, here, axis, total_ref, base, m):
    n = SIZE[axis]
    own = total_ref.at[pl.ds(base + here[axis] * m, m)]
    flights = [wires.send(own, own, along(here, axis, d)) for d in range(1, n)]
    yield
    for copy in flights:
        copy.wait_recv()


def direct_gather_swap(wires, here, axis, total_ref, base, m, partner):
    n = SIZE[axis]

    def chunk(distance):
        k = lax.rem(here[axis] + distance + n, n)
        return total_ref.at[pl.ds(base + k * m, m)]

    own = chunk(0)
    near_first = sorted(range(1, n), key=lambda d: min(d, n - d))
    flights = [(d, wires.send(own, own, along(here, axis, d))) for d in near_first]
    swapped = [wires.send(own, own, partner)]
    yield
    for d, copy in flights:
        copy.wait_recv()
        swapped.append(wires.send(chunk(-d), chunk(-d), partner))
    yield
    for copy in swapped:
        copy.wait_recv()


def direct_exchange(wires, here, axis, own, landed):
    n = SIZE[axis]
    me = here[axis]
    flights = []
    for d in range(1, n):
        flights.append(wires.send(own, landed.at[d - 1], along(here, axis, d)))
    yield
    for copy in flights:
        copy.wait_recv()
    total = jnp.zeros(own.shape, F32)
    for k in range(n):
        back = lax.rem(me - k + n, n)
        other = f32(landed[lax.rem(back + n - 1, n)])
        total = total + jnp.where(back == 0, f32(own[...]), other)
    return total


def part_scratch(order, split, kept):
    a, b, c = shares(order, split)
    m = b * c * kept
    return [
        pltpu.VMEM((a, m, 16, 128), BF),
        pltpu.VMEM((a - 1, m, 16, 128), BF),
        pltpu.VMEM((b, c * kept, 16, 128), BF),
        pltpu.VMEM((b - 1, c * kept, 16, 128), BF),
        pltpu.VMEM((c, kept, 16, 128), BF),
        pltpu.VMEM((SIZE[order[2]], kept, 16, 128), BF),
    ]


def reduce_part(wires, here, partner, grads_ref, total_ref, paired, scratch, start, part):
    shared, landed1, sum1, landed2, sum2, landed3 = scratch
    order, split, kept = part
    a, b, c = shares(order, split)
    m = b * c * kept
    core = here["core"]
    there = pl.ds((1 - core) * HALF + start, a * m)
    flight = wires.send(grads_ref.at[there], paired.at[pl.ds(start, a * m)], partner)
    yield
    flight.wait_recv()
    both = f32(grads_ref[pl.ds(core * HALF + start, a * m)]) + f32(paired[start : start + a * m])
    shared[...] = both.astype(BF).reshape(a, m, 16, 128)
    total = yield from direct_scatter(wires, here, order[0], shared, landed1)
    sum1[...] = total.astype(BF).reshape(b, c * kept, 16, 128)
    total = yield from direct_scatter(wires, here, order[1], sum1, landed2)
    sum2[...] = total.astype(BF).reshape(c, kept, 16, 128)
    if split:
        total = yield from direct_scatter(wires, here, order[2], sum2, landed3)
    else:
        total = yield from direct_exchange(wires, here, order[2], sum2.at[0], landed3)
    base0 = core * HALF + start
    base1 = base0 + here[order[0]] * m
    base2 = base1 + here[order[1]] * (c * kept)
    if split:
        total_ref[pl.ds(base2 + here[order[2]] * kept, kept)] = total.astype(BF)
        yield from direct_gather(wires, here, order[2], total_ref, base2, kept)
    else:
        total_ref[pl.ds(base2, kept)] = total.astype(BF)
    yield from direct_gather(wires, here, order[1], total_ref, base1, c * kept)
    yield from direct_gather_swap(wires, here, order[0], total_ref, base0, m, partner)


def interleave(programs):
    programs = list(programs)
    while programs:
        still = []
        for program in programs:
            try:
                next(program)
                still.append(program)
            except StopIteration:
                pass
        programs = still


class Reduction:
    def __init__(self, here, grads_ref, total_ref, scratch):
        paired, send_sem, recv_sem, *rest = scratch
        partner = dict(here)
        partner["core"] = 1 - here["core"]
        self.wires = Wires(send_sem, recv_sem)
        self.programs = []
        for i, part in enumerate(PARTS):
            own = rest[6 * i : 6 * i + 6]
            self.programs.append(
                reduce_part(
                    self.wires, here, partner, grads_ref, total_ref, paired, own, STARTS[i], part
                )
            )

    def begin(self, i):
        next(self.programs[i])

    advance = begin

    def finish(self):
        interleave(self.programs)
        self.wires.finish()


def reduce_scratch():
    scratch = [
        pltpu.VMEM((HALF, 16, 128), BF),
        pltpu.SemaphoreType.DMA((192,)),
        pltpu.SemaphoreType.DMA((192,)),
    ]
    for order, split, kept in PARTS:
        scratch += part_scratch(order, split, kept)
    return scratch


def unpack_kernel(total_hbm, g1, g2, g3, g4, gh, total_ref, s1, s2, s3, s4, load_sem, sem):
    spans = [(32 * t, 32) for t in range(9)] + [(DEEPER_AT, HALF - DEEPER_AT)]
    loads = []
    for i, (at, size) in enumerate(spans):
        for half in range(2):
            where = pl.ds(half * HALF + at, size)
            load = pltpu.make_async_copy(
                total_hbm.at[where], total_ref.at[where], load_sem.at[2 * i + half]
            )
            load.start()
            loads.append(load)
    copies = []

    def out(source, target):
        copy = pltpu.make_async_copy(source, target, sem.at[len(copies)])
        copy.start()
        copies.append(copy)

    for t in range(9):
        loads[2 * t].wait()
        loads[2 * t + 1].wait()
        for lane in range(4):
            at = (lane // 2) * HALF + DEEPEST_AT + 32 * t + 16 * (lane % 2)
            s4[t, :, 128 * lane : 128 * lane + 128] = f32(
                total_ref[at : at + 16].reshape(256, 128)
            )
        out(s4.at[t], g4.at[t])
    loads[18].wait()
    loads[19].wait()
    for t in range(9):
        for half in range(2):
            at = half * HALF + DEEPER_AT + 8 * t
            s3[t, :, 128 * half : 128 * half + 128] = f32(
                total_ref[at : at + 8].reshape(128, 128)
            )
    out(s3, g3)
    for t in range(9):
        for half in range(2):
            at = half * HALF + MIDDLE_AT + 2 * t
            s2[t, 32 * half : 32 * half + 32, :] = f32(total_ref[at : at + 2].reshape(32, 128))
        at = TEMPORAL_AT + 5 * t if t < 5 else HALF + TEMPORAL_AT + 5 * (t - 5)
        block = f32(total_ref[at : at + 5].reshape(80, 128))
        s1[t, 0:80, :] = block[:, 0:64]
        s1[t, 80:160, :] = block[:, 64:128]
    out(s2, g2)
    out(s1, g1)
    tile = f32(total_ref[HALF + HEAD_AT])
    for lane in range(4):
        gh[pl.ds(128 * lane, 128)] = tile[lane]
    for copy in copies:
        copy.wait()


def unpack(total):
    shapes = ((9, 160, 64), (9, 64, 128), (9, 128, 256), (9, 256, 512))
    hbm = pl.BlockSpec(memory_space=pl.ANY)
    return pl.pallas_call(
        unpack_kernel,
        out_shape=[jax.ShapeDtypeStruct(shape, F32) for shape in shapes + ((512,),)],
        in_specs=[hbm],
        out_specs=[hbm] * 4 + [vmem()],
        scratch_shapes=[pltpu.VMEM((TILES, 16, 128), BF)]
        + [pltpu.VMEM(shape, F32) for shape in shapes]
        + [pltpu.SemaphoreType.DMA((20,)), pltpu.SemaphoreType.DMA((12,))],
        compiler_params=pltpu.CompilerParams(vmem_limit_bytes=67043328),
    )(total)


def local(
    occupancy,
    state_labels,
    lift_weight,
    temporal_weight,
    middle_weight,
    deeper_weight,
    deepest_weight,
    head_weight,
):
    total = step(
        occupancy[0],
        state_labels[0],
        lift_weight,
        temporal_weight.reshape(9, 160, 64),
        middle_weight.reshape(9, 64, 128),
        deeper_weight.reshape(9, 128, 256),
        deepest_weight.reshape(9, 256, 512),
        head_weight,
    )
    g1, g2, g3, g4, gh = unpack(total)
    return (
        g1.reshape(3, 3, 5, 32, 64),
        g2.reshape(3, 3, 64, 128),
        g3.reshape(3, 3, 128, 256),
        g4.reshape(3, 3, 256, 512),
        gh,
    )


def solution(mesh):
    return jax.shard_map(
        local,
        mesh=mesh,
        in_specs=(
            P("dp", None, "space", None),
            P("dp", "space", None),
            P(),
            P(),
            P(),
            P(),
            P(),
            P(),
        ),
        out_specs=(P(), P(), P(), P(), P()),
        check_vma=False,
    )
```

```python
import math

import jax
import jax.numpy as jnp
from jax import lax
from jax.experimental import pallas as pl
from jax.experimental.pallas import tpu as pltpu
from jax.sharding import PartitionSpec as P

BF = jnp.bfloat16
F32 = jnp.float32
MESH = pl.DeviceIdType.MESH

NX, NY, NZ = 4, 4, 8
SIZE = {"x": NX, "y": NY, "z": NZ}
DEEPEST_AT, DEEPER_AT, MIDDLE_AT, TEMPORAL_AT = 0, 288, 360, 378
HEAD_AT, HALF_ENDS = 398, (403, 399)
PARTS = (
    (("z", "x", "y"), False, 2),
    (("x", "y", "z"), True, 1),
    (("y", "x", "z"), True, 1),
    (("x", "y", "z"), False, 3),
    (("y", "x", "z"), False, 3),
)


def shares(order, split):
    return SIZE[order[0]], SIZE[order[1]], SIZE[order[2]] if split else 1


LENGTHS = tuple(math.prod(shares(order, split)) * kept for order, split, kept in PARTS)
STARTS = tuple(sum(LENGTHS[:i]) for i in range(len(PARTS)))
HALF = sum(LENGTHS)
TILES = 2 * HALF


def vmem():
    return pl.BlockSpec(memory_space=pltpu.VMEM)


def dot(a, b):
    return lax.dot_general(a, b, (((1,), (0,)), ((), ())), preferred_element_type=F32)


def dot_nt(a, b):
    return lax.dot_general(a, b, (((1,), (1,)), ((), ())), preferred_element_type=F32)


def dot_tn(a, b):
    return lax.dot_general(a, b, (((0,), (0,)), ((), ())), preferred_element_type=F32)


def activate(pre):
    gate = jax.nn.sigmoid(pre)
    slope = gate * (1.0 + pre * (1.0 - gate))
    return pre * gate, slope


def later(block):
    rolled = pltpu.roll(block, 1, block.ndim - 2)
    index = lax.broadcasted_iota(jnp.int32, block.shape, block.ndim - 2)
    return jnp.where(index == 0, 0.0, rolled)


def sooner(block):
    size = block.shape[-2]
    rolled = pltpu.roll(block, size - 1, block.ndim - 2)
    index = lax.broadcasted_iota(jnp.int32, block.shape, block.ndim - 2)
    return jnp.where(index == size - 1, 0.0, rolled)


def tap_of(ref, p, q, rows, phases, start=0):
    a, b = start + p // 2, p % 2
    c, d = q // 2, q % 2
    block = ref[a : a + rows, b, c : c + phases, d]
    return block.reshape(rows * phases * block.shape[2], block.shape[3])


def store_map(ref, value, rows, phases, start=0):
    shifted = later(value[:, phases - 1])
    value = {start + r: value[r] for r in range(rows)}
    shifted = {start + r: shifted[r] for r in range(rows)}
    for r in range(start, start + rows):
        ref[r // 2, r % 2, 0, 0] = shifted[r].astype(BF)
        for m in range(phases):
            s = m + 1
            ref[r // 2, r % 2, s // 2, s % 2] = value[r][m].astype(BF)


def map_grad(delta, weight_ref, rows, phases):
    out = {}

    def put(r, m, value):
        out[(r, m)] = value if (r, m) not in out else out[(r, m)] + value

    for p in range(3):
        for q in range(3):
            part = dot_nt(delta, weight_ref[3 * p + q])
            part = part.reshape(rows, phases, 16, part.shape[1])
            for m in range(phases):
                s = 2 * m + q - 1
                for o in range(rows):
                    value = part[o, m]
                    if s < 0:
                        put(2 * o + p, 2 * phases - 1, sooner(value))
                    else:
                        put(2 * o + p, s, value)
    return out


def every_second(ref, r, start):
    halves = [ref[r, h, pl.ds(start, 16, stride=2), :] for h in range(2)]
    return jnp.concatenate(halves, axis=1)


def lift_row(order, shifts, lift, source, row, keep, lifted, r):
    frames = []
    for t in range(5):
        line = source[t, row : row + 1, :]
        if keep is not None:
            line = line * keep
        bits = jnp.bitwise_and(jnp.right_shift(jnp.broadcast_to(line, (16, 128)), shifts), 1)
        frames.append(bits.astype(F32).astype(BF))
    turned = dot_nt(order, jnp.concatenate(frames, axis=0)).astype(BF)
    value = jnp.maximum(dot(turned, lift), 0.0).reshape(8, 16, 160)
    lifted[r // 2, r % 2, 0, 0] = later(value[7]).astype(BF)
    for m in range(8):
        s = m + 1
        lifted[r // 2, r % 2, s // 2, s % 2] = value[m].astype(BF)


def step_kernel(
    occ_ref,
    labels_ref,
    lift_ref,
    w1_hbm,
    w2_hbm,
    w3_hbm,
    w4_hbm,
    head_ref,
    total_ref,
    w1_ref,
    w2_ref,
    w3_ref,
    w4_ref,
    weight_sem,
    landed,
    halo_sem,
    grads_ref,
    lift_pad,
    lifted,
    first,
    first_slope,
    second,
    second_slope,
    third,
    third_slope,
    third_dx,
    first_delta,
    *reduce_scratch,
):
    loads = [
        pltpu.make_async_copy(source, target, weight_sem.at[i])
        for i, (source, target) in enumerate(
            ((w1_hbm, w1_ref), (w2_hbm, w2_ref), (w3_hbm, w3_ref), (w4_hbm, w4_ref))
        )
    ]
    for load in loads:
        load.start()
    here = position()
    space = lax.axis_index("space")
    below = lax.rem(space + 1, 8)
    above = lax.rem(space + 7, 8)
    dp = lax.axis_index("dp")
    greet(here, [(dp, below), (dp, above)])
    halo = pltpu.make_async_remote_copy(
        src_ref=occ_ref,
        dst_ref=landed,
        send_sem=halo_sem.at[0],
        recv_sem=halo_sem.at[1],
        device_id=(dp, below),
        device_id_type=MESH,
    )
    halo.start()
    reducing = Reduction(here, grads_ref, total_ref, reduce_scratch)

    to = lax.broadcasted_iota(jnp.int32, (128, 128), 0)
    come = lax.broadcasted_iota(jnp.int32, (128, 128), 1)
    order = jnp.where(come == lax.rem(to, 16) * 8 + to // 16, 1.0, 0.0).astype(BF)
    shifts = lax.broadcasted_iota(jnp.int32, (16, 128), 0)
    lift_pad[...] = jnp.zeros((16, 32), F32)
    lift_pad[0:13, :] = lift_ref[...].astype(F32)
    wide = jnp.concatenate([lift_pad[...]] * 5, axis=1)
    frame_of = lax.broadcasted_iota(jnp.int32, (16, 160), 1) // 32
    lift = jnp.concatenate([jnp.where(frame_of == t, wide, 0.0) for t in range(5)], axis=0)
    lift = lift.astype(BF)
    zero_row = jnp.zeros((5, 2, 16, 160), BF)
    lifted[15, 1] = zero_row
    lifted[16, 0] = zero_row
    lifted[16, 1] = zero_row
    for half in range(2):
        grads_ref[half * HALF + HALF_ENDS[half] : half * HALF + HALF] = jnp.zeros(
            (HALF - HALF_ENDS[half], 16, 128), BF
        )
    for row in range(16):
        lift_row(order, shifts, lift, occ_ref, row, None, lifted, row + 15)
    loads[0].wait()

    def first_rows(start, rows):
        pre = jnp.zeros((64 * rows, 64), F32)
        for p in range(3):
            for q in range(3):
                pre = pre + dot(tap_of(lifted, p, q, rows, 4, start), w1_ref[3 * p + q])
        value, slope = activate(pre)
        store_map(first, value.reshape(rows, 4, 16, 64), rows, 4, start)
        first_slope[start : start + rows] = slope.reshape(rows, 4, 16, 64)

    first_rows(8, 7)
    halo.wait_recv()
    keep = jnp.where(space == 0, 0, 1)
    for row in range(1, 16):
        lift_row(order, shifts, lift, landed, row, keep, lifted, row - 1)
    first_rows(0, 8)

    loads[1].wait()
    pre = jnp.zeros((224, 128), F32)
    for p in range(3):
        for q in range(3):
            pre = pre + dot(tap_of(first, p, q, 7, 2), w2_ref[3 * p + q])
    value, slope = activate(pre)
    store_map(second, value.reshape(7, 2, 16, 128), 7, 2)
    second_slope[...] = slope.reshape(7, 2, 16, 128)

    loads[2].wait()
    pre = jnp.zeros((48, 256), F32)
    for p in range(3):
        for q in range(3):
            pre = pre + dot(tap_of(second, p, q, 3, 1), w3_ref[3 * p + q])
    value, slope = activate(pre)
    third[...] = jnp.zeros((3, 2, 32, 128), F32)
    for r in range(3):
        for h in range(2):
            third[r, h, 0:16, :] = value[16 * r : 16 * r + 16, 128 * h : 128 * h + 128]
    third_slope[...] = slope.reshape(3, 16, 256)

    loads[3].wait()
    place = lax.broadcasted_iota(jnp.int32, (16, 256), 0)
    cells = []
    pre = jnp.zeros((16, 512), F32)
    for p in range(3):
        even = every_second(third, p, 0)
        odd = every_second(third, p, 1)
        left = jnp.where((place > 0) & (place < 8), pltpu.roll(odd, 1, 0), 0.0)
        for q, block in enumerate((left, even, odd)):
            block = block.astype(BF)
            cells.append(block)
            pre = pre + dot(block, w4_ref[3 * p + q])
    value, slope = activate(pre)
    fourth = value.astype(BF).astype(F32)
    head = head_ref[...].astype(F32).reshape(1, 512)
    logits = jnp.sum(fourth * head, axis=1, keepdims=True)
    cell = lax.broadcasted_iota(jnp.int32, (16, 8), 0)
    lane = lax.broadcasted_iota(jnp.int32, (16, 8), 1)
    labels = jnp.broadcast_to(labels_ref[...].astype(F32), (16, 8))
    labels = jnp.sum(jnp.where(cell == lane, labels, 0.0), axis=1, keepdims=True)
    logit_grad = (jax.nn.sigmoid(logits) - labels) / 32.0
    logit_grad = jnp.where(lax.broadcasted_iota(jnp.int32, (16, 1), 0) < 8, logit_grad, 0.0)
    delta = (logit_grad * head * slope).astype(BF)

    for t in range(9):
        grad = dot_tn(cells[t], delta).astype(BF)
        for lane in range(4):
            at = (lane // 2) * HALF + DEEPEST_AT + 32 * t + 16 * (lane % 2)
            grads_ref[at : at + 16] = grad[:, 128 * lane : 128 * lane + 128].reshape(16, 16, 128)
        if t == 1:
            reducing.begin(0)
        if t == 5:
            reducing.begin(1)
    head_grad = jnp.sum(fourth * logit_grad, axis=0, keepdims=True)
    row = lax.broadcasted_iota(jnp.int32, (16, 128), 0)
    head_tile = jnp.zeros((16, 128), F32)
    for lane in range(4):
        part = jnp.broadcast_to(head_grad[:, 128 * lane : 128 * lane + 128], (16, 128))
        head_tile = jnp.where(row == lane, part, head_tile)
    grads_ref[HALF + HEAD_AT] = head_tile.astype(BF)
    for p in range(3):
        parts = [dot_nt(delta, w4_ref[3 * p + q]) for q in range(3)]
        odd = parts[2] + pltpu.roll(parts[0], 15, 0)
        for h in range(2):
            lanes = slice(128 * h, 128 * h + 128)
            third_dx[p, h, pl.ds(0, 16, stride=2), :] = parts[1][:, lanes]
            third_dx[p, h, pl.ds(1, 16, stride=2), :] = odd[:, lanes]
    delta = jnp.concatenate(
        [
            jnp.concatenate([third_dx[r, h, 0:16, :] for h in range(2)], axis=1) * third_slope[r]
            for r in range(3)
        ],
        axis=0,
    ).astype(BF)

    reducing.advance(0)

    for t in range(9):
        grad = dot_tn(tap_of(second, t // 3, t % 3, 3, 1), delta).astype(BF)
        for half in range(2):
            at = half * HALF + DEEPER_AT + 8 * t
            grads_ref[at : at + 8] = grad[:, 128 * half : 128 * half + 128].reshape(8, 16, 128)
    reducing.begin(2)
    reducing.advance(1)
    dx = map_grad(delta, w3_ref, 3, 1)
    delta = jnp.concatenate(
        [dx[(r, m)] * second_slope[r, m] for r in range(7) for m in range(2)], axis=0
    ).astype(BF)

    for t in range(9):
        grad = dot_tn(tap_of(first, t // 3, t % 3, 7, 2), delta).astype(BF).reshape(4, 16, 128)
        for half in range(2):
            at = half * HALF + MIDDLE_AT + 2 * t
            grads_ref[at : at + 2] = grad[2 * half : 2 * half + 2]
    reducing.begin(3)
    reducing.advance(2)
    dx = map_grad(delta, w2_ref, 7, 2)
    for r in range(15):
        for m in range(4):
            at = 64 * r + 16 * m
            first_delta[at : at + 16, :] = dx[(r, m)] * first_slope[r, m]
    first_delta[960:1024, :] = jnp.zeros((64, 64), F32)

    turned = jnp.transpose(first_delta[...]).astype(BF)
    for t in range(9):
        grad = dot(turned, tap_of(lifted, t // 3, t % 3, 16, 4))
        grad = jnp.transpose(grad)
        grad = jnp.concatenate([grad[0:80], grad[80:160]], axis=1).astype(BF)
        at = TEMPORAL_AT + 5 * t if t < 5 else HALF + TEMPORAL_AT + 5 * (t - 5)
        grads_ref[at : at + 5] = grad.reshape(5, 16, 128)
        if t == 3:
            reducing.advance(3)
    reducing.begin(4)
    reducing.finish()
    halo.wait_send()


def step(occ, labels, lift, w1, w2, w3, w4, head):
    hbm = pl.BlockSpec(memory_space=pl.ANY)
    return pl.pallas_call(
        step_kernel,
        out_shape=jax.ShapeDtypeStruct((TILES, 16, 128), BF),
        in_specs=[vmem()] * 3 + [hbm] * 4 + [vmem()],
        out_specs=vmem(),
        scratch_shapes=[
            pltpu.VMEM(w1.shape, BF),
            pltpu.VMEM(w2.shape, BF),
            pltpu.VMEM(w3.shape, BF),
            pltpu.VMEM(w4.shape, BF),
            pltpu.SemaphoreType.DMA((4,)),
            pltpu.VMEM((5, 16, 128), jnp.int32),
            pltpu.SemaphoreType.DMA((2,)),
            pltpu.VMEM((TILES, 16, 128), BF),
            pltpu.VMEM((16, 32), F32),
            pltpu.VMEM((17, 2, 5, 2, 16, 160), BF),
            pltpu.VMEM((8, 2, 3, 2, 16, 64), BF),
            pltpu.VMEM((15, 4, 16, 64), F32),
            pltpu.VMEM((4, 2, 2, 2, 16, 128), BF),
            pltpu.VMEM((7, 2, 16, 128), F32),
            pltpu.VMEM((3, 2, 32, 128), F32),
            pltpu.VMEM((3, 16, 256), F32),
            pltpu.VMEM((3, 2, 32, 128), F32),
            pltpu.VMEM((1024, 64), F32),
        ]
        + reduce_scratch(),
        compiler_params=pltpu.CompilerParams(
            collective_id=0, has_side_effects=True, vmem_limit_bytes=67043328
        ),
    )(occ, labels, lift, w1, w2, w3, w4, head)


def position():
    dp = lax.axis_index("dp")
    space = lax.axis_index("space")
    return {
        "x": space // 2,
        "y": lax.rem(space, 2) * 2 + lax.rem(dp // 2, 2),
        "z": dp // 4,
        "core": lax.rem(dp, 2),
    }


def device_at(place):
    dp = place["z"] * 4 + lax.rem(place["y"], 2) * 2 + place["core"]
    space = place["x"] * 2 + place["y"] // 2
    return (dp, space)


def along(here, axis, distance):
    there = dict(here)
    size = SIZE[axis]
    there[axis] = lax.rem(here[axis] + distance + size, size)
    return there


class Wires:
    def __init__(self, send_sem, recv_sem):
        self.send_sem, self.recv_sem = send_sem, recv_sem
        self.used = 0
        self.sent = []

    def send(self, src, dst, place):
        copy = pltpu.make_async_remote_copy(
            src_ref=src,
            dst_ref=dst,
            send_sem=self.send_sem.at[self.used],
            recv_sem=self.recv_sem.at[self.used],
            device_id=device_at(place),
            device_id_type=MESH,
        )
        self.used += 1
        copy.start()
        self.sent.append(copy)
        return copy

    def finish(self):
        for copy in self.sent:
            copy.wait_send()


def greet(here, others):
    partner = dict(here)
    partner["core"] = 1 - here["core"]
    barrier = pltpu.get_barrier_semaphore()
    peers = [device_at(partner)] + others
    for axis, size in SIZE.items():
        peers += [device_at(along(here, axis, d)) for d in range(1, size)]
    for peer in peers:
        pl.semaphore_signal(barrier, inc=1, device_id=peer, device_id_type=MESH)
    pl.semaphore_wait(barrier, len(peers))


def f32(block):
    return block.astype(F32)


def direct_scatter(wires, here, axis, parts, landed):
    n = SIZE[axis]
    flights = []
    for d in range(1, n):
        there = along(here, axis, d)
        flights.append(wires.send(parts.at[there[axis]], landed.at[d - 1], there))
    yield
    for copy in flights:
        copy.wait_recv()
    total = f32(parts[here[axis]])
    for d in range(1, n):
        total = total + f32(landed[d - 1])
    return total


def direct_gather(wires, here, axis, total_ref, base, m):
    n = SIZE[axis]
    own = total_ref.at[pl.ds(base + here[axis] * m, m)]
    flights = [wires.send(own, own, along(here, axis, d)) for d in range(1, n)]
    yield
    for copy in flights:
        copy.wait_recv()


def direct_gather_swap(wires, here, axis, total_ref, base, m, partner):
    n = SIZE[axis]

    def chunk(distance):
        k = lax.rem(here[axis] + distance + n, n)
        return total_ref.at[pl.ds(base + k * m, m)]

    own = chunk(0)
    near_first = sorted(range(1, n), key=lambda d: min(d, n - d))
    flights = [(d, wires.send(own, own, along(here, axis, d))) for d in near_first]
    swapped = [wires.send(own, own, partner)]
    for d, copy in flights:
        yield
        copy.wait_recv()
        swapped.append(wires.send(chunk(-d), chunk(-d), partner))
    yield
    for copy in swapped:
        copy.wait_recv()


def direct_exchange(wires, here, axis, own, landed):
    n = SIZE[axis]
    me = here[axis]
    flights = []
    for d in range(1, n):
        flights.append(wires.send(own, landed.at[d - 1], along(here, axis, d)))
    yield
    for copy in flights:
        copy.wait_recv()
    total = jnp.zeros(own.shape, F32)
    for k in range(n):
        back = lax.rem(me - k + n, n)
        other = f32(landed[lax.rem(back + n - 1, n)])
        total = total + jnp.where(back == 0, f32(own[...]), other)
    return total


def part_scratch(order, split, kept):
    a, b, c = shares(order, split)
    m = b * c * kept
    return [
        pltpu.VMEM((a, m, 16, 128), BF),
        pltpu.VMEM((a - 1, m, 16, 128), BF),
        pltpu.VMEM((b, c * kept, 16, 128), BF),
        pltpu.VMEM((b - 1, c * kept, 16, 128), BF),
        pltpu.VMEM((c, kept, 16, 128), BF),
        pltpu.VMEM((SIZE[order[2]], kept, 16, 128), BF),
    ]


def reduce_part(wires, here, partner, grads_ref, total_ref, paired, scratch, start, part):
    shared, landed1, sum1, landed2, sum2, landed3 = scratch
    order, split, kept = part
    a, b, c = shares(order, split)
    m = b * c * kept
    core = here["core"]
    there = pl.ds((1 - core) * HALF + start, a * m)
    flight = wires.send(grads_ref.at[there], paired.at[pl.ds(start, a * m)], partner)
    yield
    flight.wait_recv()
    both = f32(grads_ref[pl.ds(core * HALF + start, a * m)]) + f32(paired[start : start + a * m])
    shared[...] = both.astype(BF).reshape(a, m, 16, 128)
    total = yield from direct_scatter(wires, here, order[0], shared, landed1)
    sum1[...] = total.astype(BF).reshape(b, c * kept, 16, 128)
    total = yield from direct_scatter(wires, here, order[1], sum1, landed2)
    sum2[...] = total.astype(BF).reshape(c, kept, 16, 128)
    if split:
        total = yield from direct_scatter(wires, here, order[2], sum2, landed3)
    else:
        total = yield from direct_exchange(wires, here, order[2], sum2.at[0], landed3)
    base0 = core * HALF + start
    base1 = base0 + here[order[0]] * m
    base2 = base1 + here[order[1]] * (c * kept)
    if split:
        total_ref[pl.ds(base2 + here[order[2]] * kept, kept)] = total.astype(BF)
        yield from direct_gather(wires, here, order[2], total_ref, base2, kept)
    else:
        total_ref[pl.ds(base2, kept)] = total.astype(BF)
    yield from direct_gather(wires, here, order[1], total_ref, base1, c * kept)
    yield from direct_gather_swap(wires, here, order[0], total_ref, base0, m, partner)


def interleave(programs):
    programs = list(programs)
    while programs:
        still = []
        for program in programs:
            try:
                next(program)
                still.append(program)
            except StopIteration:
                pass
        programs = still


class Reduction:
    def __init__(self, here, grads_ref, total_ref, scratch):
        paired, send_sem, recv_sem, *rest = scratch
        partner = dict(here)
        partner["core"] = 1 - here["core"]
        self.wires = Wires(send_sem, recv_sem)
        self.programs = []
        for i, part in enumerate(PARTS):
            own = rest[6 * i : 6 * i + 6]
            self.programs.append(
                reduce_part(
                    self.wires, here, partner, grads_ref, total_ref, paired, own, STARTS[i], part
                )
            )

    def begin(self, i):
        next(self.programs[i])

    advance = begin

    def finish(self):
        interleave([self.programs[i] for i in (4, 1, 0, 2, 3)])
        self.wires.finish()


def reduce_scratch():
    scratch = [
        pltpu.VMEM((HALF, 16, 128), BF),
        pltpu.SemaphoreType.DMA((192,)),
        pltpu.SemaphoreType.DMA((192,)),
    ]
    for order, split, kept in PARTS:
        scratch += part_scratch(order, split, kept)
    return scratch


def unpack_kernel(total_hbm, g1, g2, g3, g4, gh, total_ref, s1, s2, s3, s4, load_sem, sem):
    spans = [(32 * t, 32) for t in range(9)] + [(DEEPER_AT, HALF - DEEPER_AT)]
    loads = []
    for i, (at, size) in enumerate(spans):
        for half in range(2):
            where = pl.ds(half * HALF + at, size)
            load = pltpu.make_async_copy(
                total_hbm.at[where], total_ref.at[where], load_sem.at[2 * i + half]
            )
            load.start()
            loads.append(load)
    copies = []

    def out(source, target):
        copy = pltpu.make_async_copy(source, target, sem.at[len(copies)])
        copy.start()
        copies.append(copy)

    for t in range(9):
        loads[2 * t].wait()
        loads[2 * t + 1].wait()
        for lane in range(4):
            at = (lane // 2) * HALF + DEEPEST_AT + 32 * t + 16 * (lane % 2)
            s4[t, :, 128 * lane : 128 * lane + 128] = f32(
                total_ref[at : at + 16].reshape(256, 128)
            )
        out(s4.at[t], g4.at[t])
    loads[18].wait()
    loads[19].wait()
    for t in range(9):
        for half in range(2):
            at = half * HALF + DEEPER_AT + 8 * t
            s3[t, :, 128 * half : 128 * half + 128] = f32(
                total_ref[at : at + 8].reshape(128, 128)
            )
    out(s3, g3)
    for t in range(9):
        for half in range(2):
            at = half * HALF + MIDDLE_AT + 2 * t
            s2[t, 32 * half : 32 * half + 32, :] = f32(total_ref[at : at + 2].reshape(32, 128))
        at = TEMPORAL_AT + 5 * t if t < 5 else HALF + TEMPORAL_AT + 5 * (t - 5)
        block = f32(total_ref[at : at + 5].reshape(80, 128))
        s1[t, 0:80, :] = block[:, 0:64]
        s1[t, 80:160, :] = block[:, 64:128]
    out(s2, g2)
    out(s1, g1)
    tile = f32(total_ref[HALF + HEAD_AT])
    for lane in range(4):
        gh[pl.ds(128 * lane, 128)] = tile[lane]
    for copy in copies:
        copy.wait()


def unpack(total):
    shapes = ((9, 160, 64), (9, 64, 128), (9, 128, 256), (9, 256, 512))
    hbm = pl.BlockSpec(memory_space=pl.ANY)
    return pl.pallas_call(
        unpack_kernel,
        out_shape=[jax.ShapeDtypeStruct(shape, F32) for shape in shapes + ((512,),)],
        in_specs=[hbm],
        out_specs=[hbm] * 4 + [vmem()],
        scratch_shapes=[pltpu.VMEM((TILES, 16, 128), BF)]
        + [pltpu.VMEM(shape, F32) for shape in shapes]
        + [pltpu.SemaphoreType.DMA((20,)), pltpu.SemaphoreType.DMA((12,))],
        compiler_params=pltpu.CompilerParams(vmem_limit_bytes=67043328),
    )(total)


def local(
    occupancy,
    state_labels,
    lift_weight,
    temporal_weight,
    middle_weight,
    deeper_weight,
    deepest_weight,
    head_weight,
):
    total = step(
        occupancy[0],
        state_labels[0],
        lift_weight,
        temporal_weight.reshape(9, 160, 64),
        middle_weight.reshape(9, 64, 128),
        deeper_weight.reshape(9, 128, 256),
        deepest_weight.reshape(9, 256, 512),
        head_weight,
    )
    g1, g2, g3, g4, gh = unpack(total)
    return (
        g1.reshape(3, 3, 5, 32, 64),
        g2.reshape(3, 3, 64, 128),
        g3.reshape(3, 3, 128, 256),
        g4.reshape(3, 3, 256, 512),
        gh,
    )


def solution(mesh):
    return jax.shard_map(
        local,
        mesh=mesh,
        in_specs=(
            P("dp", None, "space", None),
            P("dp", "space", None),
            P(),
            P(),
            P(),
            P(),
            P(),
            P(),
        ),
        out_specs=(P(), P(), P(), P(), P()),
        check_vma=False,
    )
```

```python
import math

import jax
import jax.numpy as jnp
from jax import lax
from jax.experimental import pallas as pl
from jax.experimental.pallas import tpu as pltpu
from jax.sharding import PartitionSpec as P

BF = jnp.bfloat16
F32 = jnp.float32
MESH = pl.DeviceIdType.MESH

NX, NY, NZ = 4, 4, 8
SIZE = {"x": NX, "y": NY, "z": NZ}
DEEPEST_AT, DEEPER_AT, MIDDLE_AT, TEMPORAL_AT = 0, 288, 360, 378
HEAD_AT, HALF_ENDS = 398, (403, 399)
PARTS = (
    (("z", "x", "y"), False, 2),
    (("x", "y", "z"), True, 1),
    (("y", "x", "z"), True, 1),
    (("x", "y", "z"), False, 3),
    (("y", "x", "z"), False, 3),
)


def shares(order, split):
    return SIZE[order[0]], SIZE[order[1]], SIZE[order[2]] if split else 1


LENGTHS = tuple(math.prod(shares(order, split)) * kept for order, split, kept in PARTS)
STARTS = tuple(sum(LENGTHS[:i]) for i in range(len(PARTS)))
HALF = sum(LENGTHS)
TILES = 2 * HALF


def vmem():
    return pl.BlockSpec(memory_space=pltpu.VMEM)


def dot(a, b):
    return lax.dot_general(a, b, (((1,), (0,)), ((), ())), preferred_element_type=F32)


def dot_nt(a, b):
    return lax.dot_general(a, b, (((1,), (1,)), ((), ())), preferred_element_type=F32)


def dot_tn(a, b):
    return lax.dot_general(a, b, (((0,), (0,)), ((), ())), preferred_element_type=F32)


def activate(pre):
    gate = jax.nn.sigmoid(pre)
    slope = gate * (1.0 + pre * (1.0 - gate))
    return pre * gate, slope


def later(block):
    rolled = pltpu.roll(block, 1, block.ndim - 2)
    index = lax.broadcasted_iota(jnp.int32, block.shape, block.ndim - 2)
    return jnp.where(index == 0, 0.0, rolled)


def sooner(block):
    size = block.shape[-2]
    rolled = pltpu.roll(block, size - 1, block.ndim - 2)
    index = lax.broadcasted_iota(jnp.int32, block.shape, block.ndim - 2)
    return jnp.where(index == size - 1, 0.0, rolled)


def tap_of(ref, p, q, rows, phases, start=0):
    a, b = start + p // 2, p % 2
    c, d = q // 2, q % 2
    block = ref[a : a + rows, b, c : c + phases, d]
    return block.reshape(rows * phases * block.shape[2], block.shape[3])


def store_map(ref, value, rows, phases, start=0):
    shifted = later(value[:, phases - 1])
    value = {start + r: value[r] for r in range(rows)}
    shifted = {start + r: shifted[r] for r in range(rows)}
    for r in range(start, start + rows):
        ref[r // 2, r % 2, 0, 0] = shifted[r].astype(BF)
        for m in range(phases):
            s = m + 1
            ref[r // 2, r % 2, s // 2, s % 2] = value[r][m].astype(BF)


def map_grad(delta, weight_ref, rows, phases):
    out = {}

    def put(r, m, value):
        out[(r, m)] = value if (r, m) not in out else out[(r, m)] + value

    for p in range(3):
        for q in range(3):
            part = dot_nt(delta, weight_ref[3 * p + q])
            part = part.reshape(rows, phases, 16, part.shape[1])
            for m in range(phases):
                s = 2 * m + q - 1
                for o in range(rows):
                    value = part[o, m]
                    if s < 0:
                        put(2 * o + p, 2 * phases - 1, sooner(value))
                    else:
                        put(2 * o + p, s, value)
    return out


def every_second(ref, r, start):
    halves = [ref[r, h, pl.ds(start, 16, stride=2), :] for h in range(2)]
    return jnp.concatenate(halves, axis=1)


def lift_row(order, shifts, lift, source, row, keep, lifted, r):
    frames = []
    for t in range(5):
        line = source[t, row : row + 1, :]
        if keep is not None:
            line = line * keep
        bits = jnp.bitwise_and(jnp.right_shift(jnp.broadcast_to(line, (16, 128)), shifts), 1)
        frames.append(bits.astype(F32).astype(BF))
    turned = dot_nt(order, jnp.concatenate(frames, axis=0)).astype(BF)
    value = jnp.maximum(dot(turned, lift), 0.0).reshape(8, 16, 160)
    lifted[r // 2, r % 2, 0, 0] = later(value[7]).astype(BF)
    for m in range(8):
        s = m + 1
        lifted[r // 2, r % 2, s // 2, s % 2] = value[m].astype(BF)


def step_kernel(
    occ_ref,
    labels_ref,
    lift_ref,
    w1_hbm,
    w2_hbm,
    w3_hbm,
    w4_hbm,
    head_ref,
    total_ref,
    w1_ref,
    w2_ref,
    w3_ref,
    w4_ref,
    weight_sem,
    landed,
    halo_sem,
    grads_ref,
    lift_pad,
    lifted,
    first,
    first_slope,
    second,
    second_slope,
    third,
    third_slope,
    third_dx,
    first_delta,
    *reduce_scratch,
):
    loads = [
        pltpu.make_async_copy(source, target, weight_sem.at[i])
        for i, (source, target) in enumerate(
            ((w1_hbm, w1_ref), (w2_hbm, w2_ref), (w3_hbm, w3_ref), (w4_hbm, w4_ref))
        )
    ]
    for load in loads:
        load.start()
    here = position()
    space = lax.axis_index("space")
    below = lax.rem(space + 1, 8)
    above = lax.rem(space + 7, 8)
    dp = lax.axis_index("dp")
    greet(here, [(dp, below), (dp, above)])
    halo = pltpu.make_async_remote_copy(
        src_ref=occ_ref,
        dst_ref=landed,
        send_sem=halo_sem.at[0],
        recv_sem=halo_sem.at[1],
        device_id=(dp, below),
        device_id_type=MESH,
    )
    halo.start()
    reducing = Reduction(here, grads_ref, total_ref, reduce_scratch)

    to = lax.broadcasted_iota(jnp.int32, (128, 128), 0)
    come = lax.broadcasted_iota(jnp.int32, (128, 128), 1)
    order = jnp.where(come == lax.rem(to, 16) * 8 + to // 16, 1.0, 0.0).astype(BF)
    shifts = lax.broadcasted_iota(jnp.int32, (16, 128), 0)
    lift_pad[...] = jnp.zeros((16, 32), F32)
    lift_pad[0:13, :] = lift_ref[...].astype(F32)
    wide = jnp.concatenate([lift_pad[...]] * 5, axis=1)
    frame_of = lax.broadcasted_iota(jnp.int32, (16, 160), 1) // 32
    lift = jnp.concatenate([jnp.where(frame_of == t, wide, 0.0) for t in range(5)], axis=0)
    lift = lift.astype(BF)
    zero_row = jnp.zeros((5, 2, 16, 160), BF)
    lifted[15, 1] = zero_row
    lifted[16, 0] = zero_row
    lifted[16, 1] = zero_row
    for half in range(2):
        grads_ref[half * HALF + HALF_ENDS[half] : half * HALF + HALF] = jnp.zeros(
            (HALF - HALF_ENDS[half], 16, 128), BF
        )
    for row in range(16):
        lift_row(order, shifts, lift, occ_ref, row, None, lifted, row + 15)
    loads[0].wait()

    def first_rows(start, rows):
        pre = jnp.zeros((64 * rows, 64), F32)
        for p in range(3):
            for q in range(3):
                pre = pre + dot(tap_of(lifted, p, q, rows, 4, start), w1_ref[3 * p + q])
        value, slope = activate(pre)
        store_map(first, value.reshape(rows, 4, 16, 64), rows, 4, start)
        first_slope[start : start + rows] = slope.reshape(rows, 4, 16, 64)

    first_rows(8, 7)
    halo.wait_recv()
    keep = jnp.where(space == 0, 0, 1)
    for row in range(1, 16):
        lift_row(order, shifts, lift, landed, row, keep, lifted, row - 1)
    first_rows(0, 8)

    loads[1].wait()
    pre = jnp.zeros((224, 128), F32)
    for p in range(3):
        for q in range(3):
            pre = pre + dot(tap_of(first, p, q, 7, 2), w2_ref[3 * p + q])
    value, slope = activate(pre)
    store_map(second, value.reshape(7, 2, 16, 128), 7, 2)
    second_slope[...] = slope.reshape(7, 2, 16, 128)

    loads[2].wait()
    pre = jnp.zeros((48, 256), F32)
    for p in range(3):
        for q in range(3):
            pre = pre + dot(tap_of(second, p, q, 3, 1), w3_ref[3 * p + q])
    value, slope = activate(pre)
    third[...] = jnp.zeros((3, 2, 32, 128), F32)
    for r in range(3):
        for h in range(2):
            third[r, h, 0:16, :] = value[16 * r : 16 * r + 16, 128 * h : 128 * h + 128]
    third_slope[...] = slope.reshape(3, 16, 256)

    loads[3].wait()
    place = lax.broadcasted_iota(jnp.int32, (16, 256), 0)
    cells = []
    pre = jnp.zeros((16, 512), F32)
    for p in range(3):
        even = every_second(third, p, 0)
        odd = every_second(third, p, 1)
        left = jnp.where((place > 0) & (place < 8), pltpu.roll(odd, 1, 0), 0.0)
        for q, block in enumerate((left, even, odd)):
            block = block.astype(BF)
            cells.append(block)
            pre = pre + dot(block, w4_ref[3 * p + q])
    value, slope = activate(pre)
    fourth = value.astype(BF).astype(F32)
    head = head_ref[...].astype(F32).reshape(1, 512)
    logits = jnp.sum(fourth * head, axis=1, keepdims=True)
    cell = lax.broadcasted_iota(jnp.int32, (16, 8), 0)
    lane = lax.broadcasted_iota(jnp.int32, (16, 8), 1)
    labels = jnp.broadcast_to(labels_ref[...].astype(F32), (16, 8))
    labels = jnp.sum(jnp.where(cell == lane, labels, 0.0), axis=1, keepdims=True)
    logit_grad = (jax.nn.sigmoid(logits) - labels) / 32.0
    logit_grad = jnp.where(lax.broadcasted_iota(jnp.int32, (16, 1), 0) < 8, logit_grad, 0.0)
    delta = (logit_grad * head * slope).astype(BF)

    for t in range(9):
        grad = dot_tn(cells[t], delta).astype(BF)
        for lane in range(4):
            at = (lane // 2) * HALF + DEEPEST_AT + 32 * t + 16 * (lane % 2)
            grads_ref[at : at + 16] = grad[:, 128 * lane : 128 * lane + 128].reshape(16, 16, 128)
        if t == 1:
            reducing.begin(0)
        if t == 5:
            reducing.begin(1)
    head_grad = jnp.sum(fourth * logit_grad, axis=0, keepdims=True)
    row = lax.broadcasted_iota(jnp.int32, (16, 128), 0)
    head_tile = jnp.zeros((16, 128), F32)
    for lane in range(4):
        part = jnp.broadcast_to(head_grad[:, 128 * lane : 128 * lane + 128], (16, 128))
        head_tile = jnp.where(row == lane, part, head_tile)
    grads_ref[HALF + HEAD_AT] = head_tile.astype(BF)
    for p in range(3):
        parts = [dot_nt(delta, w4_ref[3 * p + q]) for q in range(3)]
        odd = parts[2] + pltpu.roll(parts[0], 15, 0)
        for h in range(2):
            lanes = slice(128 * h, 128 * h + 128)
            third_dx[p, h, pl.ds(0, 16, stride=2), :] = parts[1][:, lanes]
            third_dx[p, h, pl.ds(1, 16, stride=2), :] = odd[:, lanes]
    delta = jnp.concatenate(
        [
            jnp.concatenate([third_dx[r, h, 0:16, :] for h in range(2)], axis=1) * third_slope[r]
            for r in range(3)
        ],
        axis=0,
    ).astype(BF)

    reducing.advance(0)

    for t in range(9):
        grad = dot_tn(tap_of(second, t // 3, t % 3, 3, 1), delta).astype(BF)
        for half in range(2):
            at = half * HALF + DEEPER_AT + 8 * t
            grads_ref[at : at + 8] = grad[:, 128 * half : 128 * half + 128].reshape(8, 16, 128)
    reducing.begin(2)
    reducing.advance(1)
    dx = map_grad(delta, w3_ref, 3, 1)
    delta = jnp.concatenate(
        [dx[(r, m)] * second_slope[r, m] for r in range(7) for m in range(2)], axis=0
    ).astype(BF)

    for t in range(9):
        grad = dot_tn(tap_of(first, t // 3, t % 3, 7, 2), delta).astype(BF).reshape(4, 16, 128)
        for half in range(2):
            at = half * HALF + MIDDLE_AT + 2 * t
            grads_ref[at : at + 2] = grad[2 * half : 2 * half + 2]
    reducing.begin(3)
    reducing.advance(2)
    dx = map_grad(delta, w2_ref, 7, 2)
    for r in range(15):
        for m in range(4):
            at = 64 * r + 16 * m
            first_delta[at : at + 16, :] = dx[(r, m)] * first_slope[r, m]
    first_delta[960:1024, :] = jnp.zeros((64, 64), F32)

    turned = jnp.transpose(first_delta[...]).astype(BF)
    for t in range(9):
        grad = dot(turned, tap_of(lifted, t // 3, t % 3, 16, 4))
        grad = jnp.transpose(grad)
        grad = jnp.concatenate([grad[0:80], grad[80:160]], axis=1).astype(BF)
        at = TEMPORAL_AT + 5 * t if t < 5 else HALF + TEMPORAL_AT + 5 * (t - 5)
        grads_ref[at : at + 5] = grad.reshape(5, 16, 128)
        if t == 3:
            reducing.advance(3)
    reducing.begin(4)
    reducing.finish()
    halo.wait_send()


def step(occ, labels, lift, w1, w2, w3, w4, head):
    hbm = pl.BlockSpec(memory_space=pl.ANY)
    return pl.pallas_call(
        step_kernel,
        out_shape=jax.ShapeDtypeStruct((TILES, 16, 128), BF),
        in_specs=[vmem()] * 3 + [hbm] * 4 + [vmem()],
        out_specs=vmem(),
        scratch_shapes=[
            pltpu.VMEM(w1.shape, BF),
            pltpu.VMEM(w2.shape, BF),
            pltpu.VMEM(w3.shape, BF),
            pltpu.VMEM(w4.shape, BF),
            pltpu.SemaphoreType.DMA((4,)),
            pltpu.VMEM((5, 16, 128), jnp.int32),
            pltpu.SemaphoreType.DMA((2,)),
            pltpu.VMEM((TILES, 16, 128), BF),
            pltpu.VMEM((16, 32), F32),
            pltpu.VMEM((17, 2, 5, 2, 16, 160), BF),
            pltpu.VMEM((8, 2, 3, 2, 16, 64), BF),
            pltpu.VMEM((15, 4, 16, 64), F32),
            pltpu.VMEM((4, 2, 2, 2, 16, 128), BF),
            pltpu.VMEM((7, 2, 16, 128), F32),
            pltpu.VMEM((3, 2, 32, 128), F32),
            pltpu.VMEM((3, 16, 256), F32),
            pltpu.VMEM((3, 2, 32, 128), F32),
            pltpu.VMEM((1024, 64), F32),
        ]
        + reduce_scratch(),
        compiler_params=pltpu.CompilerParams(
            collective_id=0, has_side_effects=True, vmem_limit_bytes=67043328
        ),
    )(occ, labels, lift, w1, w2, w3, w4, head)


def position():
    dp = lax.axis_index("dp")
    space = lax.axis_index("space")
    return {
        "x": space // 2,
        "y": lax.rem(space, 2) * 2 + lax.rem(dp // 2, 2),
        "z": dp // 4,
        "core": lax.rem(dp, 2),
    }


def device_at(place):
    dp = place["z"] * 4 + lax.rem(place["y"], 2) * 2 + place["core"]
    space = place["x"] * 2 + place["y"] // 2
    return (dp, space)


def along(here, axis, distance):
    there = dict(here)
    size = SIZE[axis]
    there[axis] = lax.rem(here[axis] + distance + size, size)
    return there


class Wires:
    def __init__(self, send_sem, recv_sem):
        self.send_sem, self.recv_sem = send_sem, recv_sem
        self.used = 0
        self.sent = []

    def send(self, src, dst, place):
        copy = pltpu.make_async_remote_copy(
            src_ref=src,
            dst_ref=dst,
            send_sem=self.send_sem.at[self.used],
            recv_sem=self.recv_sem.at[self.used],
            device_id=device_at(place),
            device_id_type=MESH,
        )
        self.used += 1
        copy.start()
        self.sent.append(copy)
        return copy

    def finish(self):
        for copy in self.sent:
            copy.wait_send()


def greet(here, others):
    partner = dict(here)
    partner["core"] = 1 - here["core"]
    barrier = pltpu.get_barrier_semaphore()
    peers = [device_at(partner)] + others
    for axis, size in SIZE.items():
        peers += [device_at(along(here, axis, d)) for d in range(1, size)]
    for peer in peers:
        pl.semaphore_signal(barrier, inc=1, device_id=peer, device_id_type=MESH)
    pl.semaphore_wait(barrier, len(peers))


def f32(block):
    return block.astype(F32)


def direct_scatter(wires, here, axis, parts, landed):
    n = SIZE[axis]
    flights = []
    for d in range(1, n):
        there = along(here, axis, d)
        flights.append(wires.send(parts.at[there[axis]], landed.at[d - 1], there))
    yield
    for copy in flights:
        copy.wait_recv()
    total = f32(parts[here[axis]])
    for d in range(1, n):
        total = total + f32(landed[d - 1])
    return total


def direct_gather(wires, here, axis, total_ref, base, m):
    n = SIZE[axis]
    own = total_ref.at[pl.ds(base + here[axis] * m, m)]
    flights = [wires.send(own, own, along(here, axis, d)) for d in range(1, n)]
    yield
    for copy in flights:
        copy.wait_recv()


def direct_gather_swap(wires, here, axis, total_ref, base, m, partner):
    n = SIZE[axis]

    def chunk(distance):
        k = lax.rem(here[axis] + distance + n, n)
        return total_ref.at[pl.ds(base + k * m, m)]

    own = chunk(0)
    near_first = sorted(range(1, n), key=lambda d: min(d, n - d))
    flights = [(d, wires.send(own, own, along(here, axis, d))) for d in near_first]
    swapped = [wires.send(own, own, partner)]
    for d, copy in flights:
        yield
        copy.wait_recv()
        swapped.append(wires.send(chunk(-d), chunk(-d), partner))
    yield
    for copy in swapped:
        copy.wait_recv()


def relayed_gather_swap(wires, here, axis, total_ref, base, m, partner):
    n = SIZE[axis]
    h = m // 2
    right, left = along(here, axis, 1), along(here, axis, -1)

    def piece(distance, at, size):
        k = lax.rem(here[axis] + distance + n, n)
        return total_ref.at[pl.ds(base + k * m + at, size)]

    own, behind, ahead = (piece(distance, 0, m) for distance in (0, -1, 1))
    from_left = wires.send(own, own, right)
    from_right = wires.send(own, own, left)
    swapped = [wires.send(own, own, partner)]
    yield
    low, high = piece(-1, 0, h), piece(1, h, m - h)
    from_left.wait_recv()
    far_left = wires.send(low, low, right)
    from_right.wait_recv()
    far_right = wires.send(high, high, left)
    swapped += [wires.send(behind, behind, partner), wires.send(ahead, ahead, partner)]
    yield
    far_left.wait_recv()
    low = piece(2, 0, h)
    swapped.append(wires.send(low, low, partner))
    far_right.wait_recv()
    high = piece(2, h, m - h)
    swapped.append(wires.send(high, high, partner))
    yield
    for copy in swapped:
        copy.wait_recv()


def direct_exchange(wires, here, axis, own, landed):
    n = SIZE[axis]
    me = here[axis]
    flights = []
    for d in range(1, n):
        flights.append(wires.send(own, landed.at[d - 1], along(here, axis, d)))
    yield
    for copy in flights:
        copy.wait_recv()
    total = jnp.zeros(own.shape, F32)
    for k in range(n):
        back = lax.rem(me - k + n, n)
        other = f32(landed[lax.rem(back + n - 1, n)])
        total = total + jnp.where(back == 0, f32(own[...]), other)
    return total


def part_scratch(order, split, kept):
    a, b, c = shares(order, split)
    m = b * c * kept
    return [
        pltpu.VMEM((a, m, 16, 128), BF),
        pltpu.VMEM((a - 1, m, 16, 128), BF),
        pltpu.VMEM((b, c * kept, 16, 128), BF),
        pltpu.VMEM((b - 1, c * kept, 16, 128), BF),
        pltpu.VMEM((c, kept, 16, 128), BF),
        pltpu.VMEM((SIZE[order[2]], kept, 16, 128), BF),
    ]


def reduce_part(wires, here, partner, grads_ref, total_ref, paired, scratch, start, part):
    shared, landed1, sum1, landed2, sum2, landed3 = scratch
    order, split, kept = part
    a, b, c = shares(order, split)
    m = b * c * kept
    core = here["core"]
    there = pl.ds((1 - core) * HALF + start, a * m)
    flight = wires.send(grads_ref.at[there], paired.at[pl.ds(start, a * m)], partner)
    yield
    flight.wait_recv()
    both = f32(grads_ref[pl.ds(core * HALF + start, a * m)]) + f32(paired[start : start + a * m])
    shared[...] = both.astype(BF).reshape(a, m, 16, 128)
    total = yield from direct_scatter(wires, here, order[0], shared, landed1)
    sum1[...] = total.astype(BF).reshape(b, c * kept, 16, 128)
    total = yield from direct_scatter(wires, here, order[1], sum1, landed2)
    sum2[...] = total.astype(BF).reshape(c, kept, 16, 128)
    if split:
        total = yield from direct_scatter(wires, here, order[2], sum2, landed3)
    else:
        total = yield from direct_exchange(wires, here, order[2], sum2.at[0], landed3)
    base0 = core * HALF + start
    base1 = base0 + here[order[0]] * m
    base2 = base1 + here[order[1]] * (c * kept)
    if split:
        total_ref[pl.ds(base2 + here[order[2]] * kept, kept)] = total.astype(BF)
        yield from direct_gather(wires, here, order[2], total_ref, base2, kept)
    else:
        total_ref[pl.ds(base2, kept)] = total.astype(BF)
    yield from direct_gather(wires, here, order[1], total_ref, base1, c * kept)
    last = relayed_gather_swap if a == 4 else direct_gather_swap
    yield from last(wires, here, order[0], total_ref, base0, m, partner)


def interleave(programs):
    programs = list(programs)
    while programs:
        still = []
        for program in programs:
            try:
                next(program)
                still.append(program)
            except StopIteration:
                pass
        programs = still


class Reduction:
    def __init__(self, here, grads_ref, total_ref, scratch):
        paired, send_sem, recv_sem, *rest = scratch
        partner = dict(here)
        partner["core"] = 1 - here["core"]
        self.wires = Wires(send_sem, recv_sem)
        self.programs = []
        for i, part in enumerate(PARTS):
            own = rest[6 * i : 6 * i + 6]
            self.programs.append(
                reduce_part(
                    self.wires, here, partner, grads_ref, total_ref, paired, own, STARTS[i], part
                )
            )

    def begin(self, i):
        next(self.programs[i])

    advance = begin

    def finish(self):
        interleave([self.programs[i] for i in (4, 1, 0, 2, 3)])
        self.wires.finish()


def reduce_scratch():
    scratch = [
        pltpu.VMEM((HALF, 16, 128), BF),
        pltpu.SemaphoreType.DMA((192,)),
        pltpu.SemaphoreType.DMA((192,)),
    ]
    for order, split, kept in PARTS:
        scratch += part_scratch(order, split, kept)
    return scratch


def unpack_kernel(total_hbm, g1, g2, g3, g4, gh, total_ref, s1, s2, s3, s4, load_sem, sem):
    spans = [(32 * t, 32) for t in range(9)] + [(DEEPER_AT, HALF - DEEPER_AT)]
    loads = []
    for i, (at, size) in enumerate(spans):
        for half in range(2):
            where = pl.ds(half * HALF + at, size)
            load = pltpu.make_async_copy(
                total_hbm.at[where], total_ref.at[where], load_sem.at[2 * i + half]
            )
            load.start()
            loads.append(load)
    copies = []

    def out(source, target):
        copy = pltpu.make_async_copy(source, target, sem.at[len(copies)])
        copy.start()
        copies.append(copy)

    for t in range(9):
        loads[2 * t].wait()
        loads[2 * t + 1].wait()
        for lane in range(4):
            at = (lane // 2) * HALF + DEEPEST_AT + 32 * t + 16 * (lane % 2)
            s4[t, :, 128 * lane : 128 * lane + 128] = f32(
                total_ref[at : at + 16].reshape(256, 128)
            )
        out(s4.at[t], g4.at[t])
    loads[18].wait()
    loads[19].wait()
    for t in range(9):
        for half in range(2):
            at = half * HALF + DEEPER_AT + 8 * t
            s3[t, :, 128 * half : 128 * half + 128] = f32(
                total_ref[at : at + 8].reshape(128, 128)
            )
    out(s3, g3)
    for t in range(9):
        for half in range(2):
            at = half * HALF + MIDDLE_AT + 2 * t
            s2[t, 32 * half : 32 * half + 32, :] = f32(total_ref[at : at + 2].reshape(32, 128))
        at = TEMPORAL_AT + 5 * t if t < 5 else HALF + TEMPORAL_AT + 5 * (t - 5)
        block = f32(total_ref[at : at + 5].reshape(80, 128))
        s1[t, 0:80, :] = block[:, 0:64]
        s1[t, 80:160, :] = block[:, 64:128]
    out(s2, g2)
    out(s1, g1)
    tile = f32(total_ref[HALF + HEAD_AT])
    for lane in range(4):
        gh[pl.ds(128 * lane, 128)] = tile[lane]
    for copy in copies:
        copy.wait()


def unpack(total):
    shapes = ((9, 160, 64), (9, 64, 128), (9, 128, 256), (9, 256, 512))
    hbm = pl.BlockSpec(memory_space=pl.ANY)
    return pl.pallas_call(
        unpack_kernel,
        out_shape=[jax.ShapeDtypeStruct(shape, F32) for shape in shapes + ((512,),)],
        in_specs=[hbm],
        out_specs=[hbm] * 4 + [vmem()],
        scratch_shapes=[pltpu.VMEM((TILES, 16, 128), BF)]
        + [pltpu.VMEM(shape, F32) for shape in shapes]
        + [pltpu.SemaphoreType.DMA((20,)), pltpu.SemaphoreType.DMA((12,))],
        compiler_params=pltpu.CompilerParams(vmem_limit_bytes=67043328),
    )(total)


def local(
    occupancy,
    state_labels,
    lift_weight,
    temporal_weight,
    middle_weight,
    deeper_weight,
    deepest_weight,
    head_weight,
):
    total = step(
        occupancy[0],
        state_labels[0],
        lift_weight,
        temporal_weight.reshape(9, 160, 64),
        middle_weight.reshape(9, 64, 128),
        deeper_weight.reshape(9, 128, 256),
        deepest_weight.reshape(9, 256, 512),
        head_weight,
    )
    g1, g2, g3, g4, gh = unpack(total)
    return (
        g1.reshape(3, 3, 5, 32, 64),
        g2.reshape(3, 3, 64, 128),
        g3.reshape(3, 3, 128, 256),
        g4.reshape(3, 3, 256, 512),
        gh,
    )


def solution(mesh):
    return jax.shard_map(
        local,
        mesh=mesh,
        in_specs=(
            P("dp", None, "space", None),
            P("dp", "space", None),
            P(),
            P(),
            P(),
            P(),
            P(),
            P(),
        ),
        out_specs=(P(), P(), P(), P(), P()),
        check_vma=False,
    )
```

```python
import math

import jax
import jax.numpy as jnp
from jax import lax
from jax.experimental import pallas as pl
from jax.experimental.pallas import tpu as pltpu
from jax.sharding import PartitionSpec as P

BF = jnp.bfloat16
F32 = jnp.float32
MESH = pl.DeviceIdType.MESH

NX, NY, NZ = 4, 4, 8
SIZE = {"x": NX, "y": NY, "z": NZ}
DEEPEST_AT, DEEPER_AT, MIDDLE_AT, TEMPORAL_AT = 0, 288, 360, 378
HEAD_AT, HALF_ENDS = 398, (403, 399)
PARTS = (
    (("z", "x", "y"), False, 2),
    (("x", "y", "z"), True, 1),
    (("y", "x", "z"), True, 1),
    (("x", "y", "z"), False, 3),
    (("y", "x", "z"), False, 3),
)


def shares(order, split):
    return SIZE[order[0]], SIZE[order[1]], SIZE[order[2]] if split else 1


LENGTHS = tuple(math.prod(shares(order, split)) * kept for order, split, kept in PARTS)
STARTS = tuple(sum(LENGTHS[:i]) for i in range(len(PARTS)))
HALF = sum(LENGTHS)
TILES = 2 * HALF


def vmem():
    return pl.BlockSpec(memory_space=pltpu.VMEM)


def dot(a, b):
    return lax.dot_general(a, b, (((1,), (0,)), ((), ())), preferred_element_type=F32)


def dot_nt(a, b):
    return lax.dot_general(a, b, (((1,), (1,)), ((), ())), preferred_element_type=F32)


def dot_tn(a, b):
    return lax.dot_general(a, b, (((0,), (0,)), ((), ())), preferred_element_type=F32)


def activate(pre):
    gate = jax.nn.sigmoid(pre)
    slope = gate * (1.0 + pre * (1.0 - gate))
    return pre * gate, slope


def later(block):
    rolled = pltpu.roll(block, 1, block.ndim - 2)
    index = lax.broadcasted_iota(jnp.int32, block.shape, block.ndim - 2)
    return jnp.where(index == 0, 0.0, rolled)


def sooner(block):
    size = block.shape[-2]
    rolled = pltpu.roll(block, size - 1, block.ndim - 2)
    index = lax.broadcasted_iota(jnp.int32, block.shape, block.ndim - 2)
    return jnp.where(index == size - 1, 0.0, rolled)


def tap_of(ref, p, q, rows, phases, start=0):
    a, b = start + p // 2, p % 2
    c, d = q // 2, q % 2
    block = ref[a : a + rows, b, c : c + phases, d]
    return block.reshape(rows * phases * block.shape[2], block.shape[3])


def store_map(ref, value, rows, phases, start=0):
    shifted = later(value[:, phases - 1])
    value = {start + r: value[r] for r in range(rows)}
    shifted = {start + r: shifted[r] for r in range(rows)}
    for r in range(start, start + rows):
        ref[r // 2, r % 2, 0, 0] = shifted[r].astype(BF)
        for m in range(phases):
            s = m + 1
            ref[r // 2, r % 2, s // 2, s % 2] = value[r][m].astype(BF)


def map_grad(delta, weight_ref, rows, phases):
    out = {}

    def put(r, m, value):
        out[(r, m)] = value if (r, m) not in out else out[(r, m)] + value

    for p in range(3):
        for q in range(3):
            part = dot_nt(delta, weight_ref[3 * p + q])
            part = part.reshape(rows, phases, 16, part.shape[1])
            for m in range(phases):
                s = 2 * m + q - 1
                for o in range(rows):
                    value = part[o, m]
                    if s < 0:
                        put(2 * o + p, 2 * phases - 1, sooner(value))
                    else:
                        put(2 * o + p, s, value)
    return out


def every_second(ref, r, start):
    halves = [ref[r, h, pl.ds(start, 16, stride=2), :] for h in range(2)]
    return jnp.concatenate(halves, axis=1)


def lift_row(order, shifts, lift, source, row, keep, lifted, r):
    frames = []
    for t in range(5):
        line = source[t, row : row + 1, :]
        if keep is not None:
            line = line * keep
        bits = jnp.bitwise_and(jnp.right_shift(jnp.broadcast_to(line, (16, 128)), shifts), 1)
        frames.append(bits.astype(F32).astype(BF))
    turned = dot_nt(order, jnp.concatenate(frames, axis=0)).astype(BF)
    value = jnp.maximum(dot(turned, lift), 0.0).reshape(8, 16, 160)
    lifted[r // 2, r % 2, 0, 0] = later(value[7]).astype(BF)
    for m in range(8):
        s = m + 1
        lifted[r // 2, r % 2, s // 2, s % 2] = value[m].astype(BF)


def step_kernel(
    occ_ref,
    labels_ref,
    lift_ref,
    w1_hbm,
    w2_hbm,
    w3_hbm,
    w4_hbm,
    head_ref,
    total_ref,
    w1_ref,
    w2_ref,
    w3_ref,
    w4_ref,
    weight_sem,
    landed,
    halo_sem,
    grads_ref,
    lift_pad,
    lifted,
    first,
    first_slope,
    second,
    second_slope,
    third,
    third_slope,
    third_dx,
    first_delta,
    *reduce_scratch,
):
    loads = [
        pltpu.make_async_copy(source, target, weight_sem.at[i])
        for i, (source, target) in enumerate(
            ((w1_hbm, w1_ref), (w2_hbm, w2_ref), (w3_hbm, w3_ref), (w4_hbm, w4_ref))
        )
    ]
    for load in loads:
        load.start()
    here = position()
    space = lax.axis_index("space")
    below = lax.rem(space + 1, 8)
    above = lax.rem(space + 7, 8)
    dp = lax.axis_index("dp")
    greet(here, [(dp, below), (dp, above)])
    halo = pltpu.make_async_remote_copy(
        src_ref=occ_ref,
        dst_ref=landed,
        send_sem=halo_sem.at[0],
        recv_sem=halo_sem.at[1],
        device_id=(dp, below),
        device_id_type=MESH,
    )
    halo.start()
    reducing = Reduction(here, grads_ref, total_ref, reduce_scratch)

    to = lax.broadcasted_iota(jnp.int32, (128, 128), 0)
    come = lax.broadcasted_iota(jnp.int32, (128, 128), 1)
    order = jnp.where(come == lax.rem(to, 16) * 8 + to // 16, 1.0, 0.0).astype(BF)
    shifts = lax.broadcasted_iota(jnp.int32, (16, 128), 0)
    lift_pad[...] = jnp.zeros((16, 32), F32)
    lift_pad[0:13, :] = lift_ref[...].astype(F32)
    wide = jnp.concatenate([lift_pad[...]] * 5, axis=1)
    frame_of = lax.broadcasted_iota(jnp.int32, (16, 160), 1) // 32
    lift = jnp.concatenate([jnp.where(frame_of == t, wide, 0.0) for t in range(5)], axis=0)
    lift = lift.astype(BF)
    zero_row = jnp.zeros((5, 2, 16, 160), BF)
    lifted[15, 1] = zero_row
    lifted[16, 0] = zero_row
    lifted[16, 1] = zero_row
    for half in range(2):
        grads_ref[half * HALF + HALF_ENDS[half] : half * HALF + HALF] = jnp.zeros(
            (HALF - HALF_ENDS[half], 16, 128), BF
        )
    for row in range(16):
        lift_row(order, shifts, lift, occ_ref, row, None, lifted, row + 15)
    loads[0].wait()

    def first_rows(start, rows):
        pre = jnp.zeros((64 * rows, 64), F32)
        for p in range(3):
            for q in range(3):
                pre = pre + dot(tap_of(lifted, p, q, rows, 4, start), w1_ref[3 * p + q])
        value, slope = activate(pre)
        store_map(first, value.reshape(rows, 4, 16, 64), rows, 4, start)
        first_slope[start : start + rows] = slope.reshape(rows, 4, 16, 64)

    first_rows(8, 7)
    halo.wait_recv()
    keep = jnp.where(space == 0, 0, 1)
    for row in range(1, 16):
        lift_row(order, shifts, lift, landed, row, keep, lifted, row - 1)
    first_rows(0, 8)

    loads[1].wait()
    pre = jnp.zeros((224, 128), F32)
    for p in range(3):
        for q in range(3):
            pre = pre + dot(tap_of(first, p, q, 7, 2), w2_ref[3 * p + q])
    value, slope = activate(pre)
    store_map(second, value.reshape(7, 2, 16, 128), 7, 2)
    second_slope[...] = slope.reshape(7, 2, 16, 128)

    loads[2].wait()
    pre = jnp.zeros((48, 256), F32)
    for p in range(3):
        for q in range(3):
            pre = pre + dot(tap_of(second, p, q, 3, 1), w3_ref[3 * p + q])
    value, slope = activate(pre)
    third[...] = jnp.zeros((3, 2, 32, 128), F32)
    for r in range(3):
        for h in range(2):
            third[r, h, 0:16, :] = value[16 * r : 16 * r + 16, 128 * h : 128 * h + 128]
    third_slope[...] = slope.reshape(3, 16, 256)

    loads[3].wait()
    place = lax.broadcasted_iota(jnp.int32, (16, 256), 0)
    cells = []
    pre = jnp.zeros((16, 512), F32)
    for p in range(3):
        even = every_second(third, p, 0)
        odd = every_second(third, p, 1)
        left = jnp.where((place > 0) & (place < 8), pltpu.roll(odd, 1, 0), 0.0)
        for q, block in enumerate((left, even, odd)):
            block = block.astype(BF)
            cells.append(block)
            pre = pre + dot(block, w4_ref[3 * p + q])
    value, slope = activate(pre)
    fourth = value.astype(BF).astype(F32)
    head = head_ref[...].astype(F32).reshape(1, 512)
    logits = jnp.sum(fourth * head, axis=1, keepdims=True)
    cell = lax.broadcasted_iota(jnp.int32, (16, 8), 0)
    lane = lax.broadcasted_iota(jnp.int32, (16, 8), 1)
    labels = jnp.broadcast_to(labels_ref[...].astype(F32), (16, 8))
    labels = jnp.sum(jnp.where(cell == lane, labels, 0.0), axis=1, keepdims=True)
    logit_grad = (jax.nn.sigmoid(logits) - labels) / 32.0
    logit_grad = jnp.where(lax.broadcasted_iota(jnp.int32, (16, 1), 0) < 8, logit_grad, 0.0)
    delta = (logit_grad * head * slope).astype(BF)

    for t in range(9):
        grad = dot_tn(cells[t], delta).astype(BF)
        for lane in range(4):
            at = (lane // 2) * HALF + DEEPEST_AT + 32 * t + 16 * (lane % 2)
            grads_ref[at : at + 16] = grad[:, 128 * lane : 128 * lane + 128].reshape(16, 16, 128)
        if t == 1:
            reducing.begin(0)
        if t == 5:
            reducing.begin(1)
    head_grad = jnp.sum(fourth * logit_grad, axis=0, keepdims=True)
    row = lax.broadcasted_iota(jnp.int32, (16, 128), 0)
    head_tile = jnp.zeros((16, 128), F32)
    for lane in range(4):
        part = jnp.broadcast_to(head_grad[:, 128 * lane : 128 * lane + 128], (16, 128))
        head_tile = jnp.where(row == lane, part, head_tile)
    grads_ref[HALF + HEAD_AT] = head_tile.astype(BF)
    for p in range(3):
        parts = [dot_nt(delta, w4_ref[3 * p + q]) for q in range(3)]
        odd = parts[2] + pltpu.roll(parts[0], 15, 0)
        for h in range(2):
            lanes = slice(128 * h, 128 * h + 128)
            third_dx[p, h, pl.ds(0, 16, stride=2), :] = parts[1][:, lanes]
            third_dx[p, h, pl.ds(1, 16, stride=2), :] = odd[:, lanes]
    delta = jnp.concatenate(
        [
            jnp.concatenate([third_dx[r, h, 0:16, :] for h in range(2)], axis=1) * third_slope[r]
            for r in range(3)
        ],
        axis=0,
    ).astype(BF)

    reducing.advance(0)

    for t in range(9):
        grad = dot_tn(tap_of(second, t // 3, t % 3, 3, 1), delta).astype(BF)
        for half in range(2):
            at = half * HALF + DEEPER_AT + 8 * t
            grads_ref[at : at + 8] = grad[:, 128 * half : 128 * half + 128].reshape(8, 16, 128)
    reducing.begin(2)
    reducing.advance(1)
    dx = map_grad(delta, w3_ref, 3, 1)
    delta = jnp.concatenate(
        [dx[(r, m)] * second_slope[r, m] for r in range(7) for m in range(2)], axis=0
    ).astype(BF)

    for t in range(9):
        grad = dot_tn(tap_of(first, t // 3, t % 3, 7, 2), delta).astype(BF).reshape(4, 16, 128)
        for half in range(2):
            at = half * HALF + MIDDLE_AT + 2 * t
            grads_ref[at : at + 2] = grad[2 * half : 2 * half + 2]
    reducing.begin(3)
    reducing.advance(2)
    dx = map_grad(delta, w2_ref, 7, 2)
    for r in range(15):
        for m in range(4):
            at = 64 * r + 16 * m
            first_delta[at : at + 16, :] = dx[(r, m)] * first_slope[r, m]
    first_delta[960:1024, :] = jnp.zeros((64, 64), F32)

    turned = jnp.transpose(first_delta[...]).astype(BF)
    for t in range(9):
        grad = dot(turned, tap_of(lifted, t // 3, t % 3, 16, 4))
        grad = jnp.transpose(grad)
        grad = jnp.concatenate([grad[0:80], grad[80:160]], axis=1).astype(BF)
        at = TEMPORAL_AT + 5 * t if t < 5 else HALF + TEMPORAL_AT + 5 * (t - 5)
        grads_ref[at : at + 5] = grad.reshape(5, 16, 128)
        if t == 3:
            reducing.advance(3)
    reducing.begin(4)
    reducing.finish()
    halo.wait_send()


def step(occ, labels, lift, w1, w2, w3, w4, head):
    hbm = pl.BlockSpec(memory_space=pl.ANY)
    return pl.pallas_call(
        step_kernel,
        out_shape=pltpu.VMEM((TILES, 16, 128), BF),
        in_specs=[vmem()] * 3 + [hbm] * 4 + [vmem()],
        out_specs=vmem(),
        scratch_shapes=[
            pltpu.VMEM(w1.shape, BF),
            pltpu.VMEM(w2.shape, BF),
            pltpu.VMEM(w3.shape, BF),
            pltpu.VMEM(w4.shape, BF),
            pltpu.SemaphoreType.DMA((4,)),
            pltpu.VMEM((5, 16, 128), jnp.int32),
            pltpu.SemaphoreType.DMA((2,)),
            pltpu.VMEM((TILES, 16, 128), BF),
            pltpu.VMEM((16, 32), F32),
            pltpu.VMEM((17, 2, 5, 2, 16, 160), BF),
            pltpu.VMEM((8, 2, 3, 2, 16, 64), BF),
            pltpu.VMEM((15, 4, 16, 64), F32),
            pltpu.VMEM((4, 2, 2, 2, 16, 128), BF),
            pltpu.VMEM((7, 2, 16, 128), F32),
            pltpu.VMEM((3, 2, 32, 128), F32),
            pltpu.VMEM((3, 16, 256), F32),
            pltpu.VMEM((3, 2, 32, 128), F32),
            pltpu.VMEM((1024, 64), F32),
        ]
        + reduce_scratch(),
        compiler_params=pltpu.CompilerParams(
            collective_id=0, has_side_effects=True, vmem_limit_bytes=61500000
        ),
    )(occ, labels, lift, w1, w2, w3, w4, head)


def position():
    dp = lax.axis_index("dp")
    space = lax.axis_index("space")
    return {
        "x": space // 2,
        "y": lax.rem(space, 2) * 2 + lax.rem(dp // 2, 2),
        "z": dp // 4,
        "core": lax.rem(dp, 2),
    }


def device_at(place):
    dp = place["z"] * 4 + lax.rem(place["y"], 2) * 2 + place["core"]
    space = place["x"] * 2 + place["y"] // 2
    return (dp, space)


def along(here, axis, distance):
    there = dict(here)
    size = SIZE[axis]
    there[axis] = lax.rem(here[axis] + distance + size, size)
    return there


class Wires:
    def __init__(self, send_sem, recv_sem):
        self.send_sem, self.recv_sem = send_sem, recv_sem
        self.used = 0
        self.sent = []

    def send(self, src, dst, place):
        copy = pltpu.make_async_remote_copy(
            src_ref=src,
            dst_ref=dst,
            send_sem=self.send_sem.at[self.used],
            recv_sem=self.recv_sem.at[self.used],
            device_id=device_at(place),
            device_id_type=MESH,
        )
        self.used += 1
        copy.start()
        self.sent.append(copy)
        return copy

    def finish(self):
        for copy in self.sent:
            copy.wait_send()


def greet(here, others):
    partner = dict(here)
    partner["core"] = 1 - here["core"]
    barrier = pltpu.get_barrier_semaphore()
    peers = [device_at(partner)] + others
    for axis, size in SIZE.items():
        peers += [device_at(along(here, axis, d)) for d in range(1, size)]
    for peer in peers:
        pl.semaphore_signal(barrier, inc=1, device_id=peer, device_id_type=MESH)
    pl.semaphore_wait(barrier, len(peers))


def f32(block):
    return block.astype(F32)


def direct_scatter(wires, here, axis, parts, landed):
    n = SIZE[axis]
    flights = []
    for d in range(1, n):
        there = along(here, axis, d)
        flights.append(wires.send(parts.at[there[axis]], landed.at[d - 1], there))
    yield
    for copy in flights:
        copy.wait_recv()
    total = f32(parts[here[axis]])
    for d in range(1, n):
        total = total + f32(landed[d - 1])
    return total


def direct_gather(wires, here, axis, total_ref, base, m):
    n = SIZE[axis]
    own = total_ref.at[pl.ds(base + here[axis] * m, m)]
    flights = [wires.send(own, own, along(here, axis, d)) for d in range(1, n)]
    yield
    for copy in flights:
        copy.wait_recv()


def direct_gather_swap(wires, here, axis, total_ref, base, m, partner):
    n = SIZE[axis]

    def chunk(distance):
        k = lax.rem(here[axis] + distance + n, n)
        return total_ref.at[pl.ds(base + k * m, m)]

    own = chunk(0)
    near_first = sorted(range(1, n), key=lambda d: min(d, n - d))
    flights = [(d, wires.send(own, own, along(here, axis, d))) for d in near_first]
    swapped = [wires.send(own, own, partner)]
    for d, copy in flights:
        yield
        copy.wait_recv()
        swapped.append(wires.send(chunk(-d), chunk(-d), partner))
    yield
    for copy in swapped:
        copy.wait_recv()


def direct_exchange(wires, here, axis, own, landed):
    n = SIZE[axis]
    me = here[axis]
    flights = []
    for d in range(1, n):
        flights.append(wires.send(own, landed.at[d - 1], along(here, axis, d)))
    yield
    for copy in flights:
        copy.wait_recv()
    total = jnp.zeros(own.shape, F32)
    for k in range(n):
        back = lax.rem(me - k + n, n)
        other = f32(landed[lax.rem(back + n - 1, n)])
        total = total + jnp.where(back == 0, f32(own[...]), other)
    return total


def part_scratch(order, split, kept):
    a, b, c = shares(order, split)
    m = b * c * kept
    return [
        pltpu.VMEM((a, m, 16, 128), BF),
        pltpu.VMEM((a - 1, m, 16, 128), BF),
        pltpu.VMEM((b, c * kept, 16, 128), BF),
        pltpu.VMEM((b - 1, c * kept, 16, 128), BF),
        pltpu.VMEM((c, kept, 16, 128), BF),
        pltpu.VMEM((SIZE[order[2]], kept, 16, 128), BF),
    ]


def reduce_part(wires, here, partner, grads_ref, total_ref, paired, scratch, start, part):
    shared, landed1, sum1, landed2, sum2, landed3 = scratch
    order, split, kept = part
    a, b, c = shares(order, split)
    m = b * c * kept
    core = here["core"]
    there = pl.ds((1 - core) * HALF + start, a * m)
    flight = wires.send(grads_ref.at[there], paired.at[pl.ds(start, a * m)], partner)
    yield
    flight.wait_recv()
    both = f32(grads_ref[pl.ds(core * HALF + start, a * m)]) + f32(paired[start : start + a * m])
    shared[...] = both.astype(BF).reshape(a, m, 16, 128)
    total = yield from direct_scatter(wires, here, order[0], shared, landed1)
    sum1[...] = total.astype(BF).reshape(b, c * kept, 16, 128)
    total = yield from direct_scatter(wires, here, order[1], sum1, landed2)
    sum2[...] = total.astype(BF).reshape(c, kept, 16, 128)
    if split:
        total = yield from direct_scatter(wires, here, order[2], sum2, landed3)
    else:
        total = yield from direct_exchange(wires, here, order[2], sum2.at[0], landed3)
    base0 = core * HALF + start
    base1 = base0 + here[order[0]] * m
    base2 = base1 + here[order[1]] * (c * kept)
    if split:
        total_ref[pl.ds(base2 + here[order[2]] * kept, kept)] = total.astype(BF)
        yield from direct_gather(wires, here, order[2], total_ref, base2, kept)
    else:
        total_ref[pl.ds(base2, kept)] = total.astype(BF)
    yield from direct_gather(wires, here, order[1], total_ref, base1, c * kept)
    yield from direct_gather_swap(wires, here, order[0], total_ref, base0, m, partner)


def interleave(programs):
    programs = list(programs)
    while programs:
        still = []
        for program in programs:
            try:
                next(program)
                still.append(program)
            except StopIteration:
                pass
        programs = still


class Reduction:
    def __init__(self, here, grads_ref, total_ref, scratch):
        paired, send_sem, recv_sem, *rest = scratch
        partner = dict(here)
        partner["core"] = 1 - here["core"]
        self.wires = Wires(send_sem, recv_sem)
        self.programs = []
        for i, part in enumerate(PARTS):
            own = rest[6 * i : 6 * i + 6]
            self.programs.append(
                reduce_part(
                    self.wires, here, partner, grads_ref, total_ref, paired, own, STARTS[i], part
                )
            )

    def begin(self, i):
        next(self.programs[i])

    advance = begin

    def finish(self):
        interleave([self.programs[i] for i in (4, 1, 0, 2, 3)])
        self.wires.finish()


def reduce_scratch():
    scratch = [
        pltpu.VMEM((HALF, 16, 128), BF),
        pltpu.SemaphoreType.DMA((192,)),
        pltpu.SemaphoreType.DMA((192,)),
    ]
    for order, split, kept in PARTS:
        scratch += part_scratch(order, split, kept)
    return scratch


def unpack_kernel(total_ref, g1, g2, g3, g4, gh, s1, s2, s3, s4, sem):
    copies = []

    def out(source, target):
        copy = pltpu.make_async_copy(source, target, sem.at[len(copies)])
        copy.start()
        copies.append(copy)

    for t in range(9):
        for lane in range(4):
            at = (lane // 2) * HALF + DEEPEST_AT + 32 * t + 16 * (lane % 2)
            s4[t, :, 128 * lane : 128 * lane + 128] = f32(
                total_ref[at : at + 16].reshape(256, 128)
            )
        out(s4.at[t], g4.at[t])
    for t in range(9):
        for half in range(2):
            at = half * HALF + DEEPER_AT + 8 * t
            s3[t, :, 128 * half : 128 * half + 128] = f32(
                total_ref[at : at + 8].reshape(128, 128)
            )
    out(s3, g3)
    for t in range(9):
        for half in range(2):
            at = half * HALF + MIDDLE_AT + 2 * t
            s2[t, 32 * half : 32 * half + 32, :] = f32(total_ref[at : at + 2].reshape(32, 128))
        at = TEMPORAL_AT + 5 * t if t < 5 else HALF + TEMPORAL_AT + 5 * (t - 5)
        block = f32(total_ref[at : at + 5].reshape(80, 128))
        s1[t, 0:80, :] = block[:, 0:64]
        s1[t, 80:160, :] = block[:, 64:128]
    out(s2, g2)
    out(s1, g1)
    tile = f32(total_ref[HALF + HEAD_AT])
    for lane in range(4):
        gh[pl.ds(128 * lane, 128)] = tile[lane]
    for copy in copies:
        copy.wait()


def unpack(total):
    shapes = ((9, 160, 64), (9, 64, 128), (9, 128, 256), (9, 256, 512))
    hbm = pl.BlockSpec(memory_space=pl.ANY)
    return pl.pallas_call(
        unpack_kernel,
        out_shape=[jax.ShapeDtypeStruct(shape, F32) for shape in shapes + ((512,),)],
        in_specs=[vmem()],
        out_specs=[hbm] * 4 + [vmem()],
        scratch_shapes=[pltpu.VMEM(shape, F32) for shape in shapes]
        + [pltpu.SemaphoreType.DMA((12,))],
        compiler_params=pltpu.CompilerParams(vmem_limit_bytes=48000000),
    )(total)


def local(
    occupancy,
    state_labels,
    lift_weight,
    temporal_weight,
    middle_weight,
    deeper_weight,
    deepest_weight,
    head_weight,
):
    total = step(
        occupancy[0],
        state_labels[0],
        lift_weight,
        temporal_weight.reshape(9, 160, 64),
        middle_weight.reshape(9, 64, 128),
        deeper_weight.reshape(9, 128, 256),
        deepest_weight.reshape(9, 256, 512),
        head_weight,
    )
    g1, g2, g3, g4, gh = unpack(total)
    return (
        g1.reshape(3, 3, 5, 32, 64),
        g2.reshape(3, 3, 64, 128),
        g3.reshape(3, 3, 128, 256),
        g4.reshape(3, 3, 256, 512),
        gh,
    )


def solution(mesh):
    return jax.shard_map(
        local,
        mesh=mesh,
        in_specs=(
            P("dp", None, "space", None),
            P("dp", "space", None),
            P(),
            P(),
            P(),
            P(),
            P(),
            P(),
        ),
        out_specs=(P(), P(), P(), P(), P()),
        check_vma=False,
    )
```
